32 devices in a mesh: dp: 16 (over z, x, core), head: 2 (over y).
Axes of the slice: x: 2, y: 2, z: 4, core: 2. Of those that a mesh axis runs over, the one named last changes fastest.
Arguments:
- x_input: bfloat16 [2048, 8192], P('dp'), may hold values from -8 to 8
- wq_old: bfloat16 [8192, 1024], P('dp', 'head'), may hold values from -0.0625 to 0.0625
- wq_fresh: bfloat16 [8192, 256], P('dp', 'head'), may hold values from -0.0625 to 0.0625
- key_projection_weight: bfloat16 [8192, 256], P('dp', 'head'), may hold values from -0.0625 to 0.0625
- value_projection_weight: bfloat16 [8192, 256], P('dp', 'head'), may hold values from -0.0625 to 0.0625
- attention_output_gradient: bfloat16 [2048, 1280], P('dp', 'head'), may hold values from -6 to 6
- head_source: int32 [10], replicated, may hold values from 0 to 9, as said below
- doc_ids: int32 [2048], P('dp'), may hold values from 0 to 63, never falling along the last dimension, each value on 1 to 128 neighbouring positions
Outputs:
- attn_out: bfloat16 [2048, 1280], P('dp', 'head')
- x_grad: bfloat16 [2048, 8192], P('dp', 'head')
The draws below stay inside these ranges and needn't reach their ends.
Inputs may be any that keep to these rules, and one draw needn't show every extreme that they name: head_source is a permutation. There are shifts s_k and a permutation t of the 5 local indices, the same for every owner d, such that new head d * 5 + k takes candidate ((d - s_k) mod 2) * 5 + t_k; one owner takes at most 3 new head from any one former owner, and some pair reaches 3.
All inputs are finite; a program needn't handle non-finite values.
Results may differ from the reference program's by a relative error of at most 0.014.
The reference program's roundings to bfloat16 on the way count: a program that leaves them out, or rounds other values in their place, can miss the bound.
Values may be sent and summed in bfloat16 or wider, within the bound.
A program may use at most 64 MiB of HBM per device.

```python
import math
import jax
import jax.numpy as jnp
import numpy as np
from jax import lax

MODEL_DIMENSION = 8192
HEAD_SIZE = 128
GROUP = 5
OLD_DEV = 4
FRESH_DEV = 1
TOK_DEV = 128
TOKENS = 2048
KEY_VALUE_HEADS = 2
HQ = 10
HQ_OLD = 8
FRESH = 2
N_DP = 16
N_HEAD = 2


def draw_head_source(key, part):
    key_order, key_offset, key_taken = jax.random.split(jax.random.fold_in(key, 17), 3)
    order = jax.random.permutation(key_order, GROUP)
    offset = jax.random.randint(key_offset, (), 0, N_HEAD)
    shifts = (order + offset) % N_HEAD
    taken_index = jax.random.permutation(key_taken, GROUP)
    device = jnp.arange(N_HEAD)[:, None]
    source = (device - shifts[None, :]) % N_HEAD * GROUP + taken_index[None, :]
    return source.reshape(HQ).astype(jnp.int32)


def draw_x_input(key, part):
    key_values = jax.random.fold_in(jax.random.fold_in(key, 29), 0)
    entries = jax.random.truncated_normal(key_values, -6.0, 6.0, (TOKENS, MODEL_DIMENSION), jnp.float32)
    return entries.astype(jnp.bfloat16)


def block_scale(stream_key, dims, shards, smallest, high):
    def one(axis_at, blocks):
        draws = jax.random.uniform(jax.random.fold_in(jax.random.fold_in(stream_key, 6), axis_at), (blocks,), jnp.float32, smallest / len(shards), high / len(shards))
        return jnp.repeat(jnp.exp(draws), dims[axis_at] // blocks).reshape((-1,) + (1,) * (len(dims) - axis_at - 1))

    level = one(*shards[0])
    for cut in shards[1:]:
        level = level * one(*cut)
    return level


def profile(amount, total, limit, skew):
    weights = [(1 << 20) // math.isqrt(grade ** skew) + 1 for grade in range(2, amount + 1)]
    spare, counts = total - limit - (amount - 1), [1] * (amount - 1)
    while spare > 0:
        free = [i for i in range(amount - 1) if counts[i] < limit]
        whole, budget = sum([weights[i] for i in free]), spare
        for i in free:
            addition = min(limit - counts[i], max(1, budget * weights[i] // whole), spare)
            counts[i] = counts[i] + addition
            spare = spare - addition
    return np.array([limit] + counts)


def ragged_sizes(rng, amount, total, bound, lean):
    if amount == 2:
        one = jax.random.randint(rng, (), max(1, total - bound), min(bound, total - 1) + 1)
        return jnp.stack([one, total - one])
    lengths = jnp.asarray(profile(amount, total, bound, lean), jnp.int32)
    couples = (amount - 1) // 2
    source_of, sink = lengths[1:1 + 2 * couples:2], lengths[2:2 + 2 * couples:2]
    room = jnp.minimum(source_of - 1, bound - sink)
    passed = jax.random.randint(jax.random.fold_in(rng, 1), (couples,), 0, 1 << 20) % (room + 1)
    lengths = lengths.at[1:1 + 2 * couples:2].set(source_of - passed).at[2:2 + 2 * couples:2].set(sink + passed)
    return lengths[jax.random.permutation(jax.random.fold_in(rng, 2), amount)]


def scatter_about(stream_key, dims, deviation, most, shards=(), held_as=jnp.bfloat16):
    level = block_scale(stream_key, dims, shards, -0.22, 0.18) if shards else 1.0
    result = jax.random.normal(stream_key, dims, jnp.float32) * deviation * level
    return jnp.minimum(jnp.maximum(result, -most), most).astype(held_as)


def setup_inputs(seed: int = 0) -> dict:
    streams_of = jax.random.split(jax.random.key(seed), 9)
    return {
        "x_input": draw_x_input(jax.random.fold_in(streams_of[8], 71), 0),
        "wq_old": scatter_about(streams_of[1], (MODEL_DIMENSION, HQ_OLD * HEAD_SIZE), MODEL_DIMENSION ** -0.5, 0.0625, ((0, 16), (1, 2))),
        "wq_fresh": scatter_about(streams_of[2], (MODEL_DIMENSION, FRESH * HEAD_SIZE), MODEL_DIMENSION ** -0.5, 0.0625, ((0, 16), (1, 2))),
        "key_projection_weight": scatter_about(streams_of[3], (MODEL_DIMENSION, KEY_VALUE_HEADS * HEAD_SIZE), MODEL_DIMENSION ** -0.5, 0.0625, ((0, 16), (1, 2))),
        "value_projection_weight": scatter_about(streams_of[4], (MODEL_DIMENSION, KEY_VALUE_HEADS * HEAD_SIZE), MODEL_DIMENSION ** -0.5, 0.0625, ((0, 16), (1, 2))),
        "attention_output_gradient": scatter_about(streams_of[5], (TOKENS, HQ * HEAD_SIZE), 1.0, 6.0, ((0, 16), (1, 2))),
        "head_source": draw_head_source(jax.random.fold_in(streams_of[8], 71), 0),
        "doc_ids": jnp.searchsorted(jnp.cumsum(ragged_sizes(streams_of[7], 4 * N_DP, TOKENS, TOK_DEV, 1)), jnp.arange(TOKENS), side="right").astype(jnp.int32),
    }


theta_base = 500000.0
neg_large = -1e+30

def rotary_tables(length, head_width):
    half_dim = head_width // 2
    frequency = theta_base ** (-2.0 * jnp.arange(half_dim, dtype=jnp.float32) / head_width)
    angles = jnp.arange(length, dtype=jnp.float32)[:, None] * frequency[None, :]
    return (jnp.cos(angles), jnp.sin(angles))

def rotate(field, cosine, sine_table):
    half_dim = field.shape[-1] // 2
    lower_half = field[..., :half_dim]
    upper_half = field[..., half_dim:]
    cosine = cosine[:, None, :]
    sine_table = sine_table[:, None, :]
    return jnp.concatenate([lower_half * cosine - upper_half * sine_table, upper_half * cosine + lower_half * sine_table], axis=-1)

def rotate_back(field, cosine, sine_table):
    half_dim = field.shape[-1] // 2
    lower_half = field[..., :half_dim]
    upper_half = field[..., half_dim:]
    cosine = cosine[:, None, :]
    sine_table = sine_table[:, None, :]
    return jnp.concatenate([lower_half * cosine + upper_half * sine_table, upper_half * cosine - lower_half * sine_table], axis=-1)

def attention_pair(queries, key_rot, values, cotangent, doc_rows):
    length = queries.shape[0]
    scale_factor = 1.0 / math.sqrt(queries.shape[-1])
    query_f = queries.astype(jnp.float32)
    key_f = key_rot.astype(jnp.float32)
    value_f = values.astype(jnp.float32)
    cotan_f = cotangent.astype(jnp.float32)
    scores = jnp.einsum('qhd,kd->hqk', query_f, key_f) * scale_factor
    positions = jnp.arange(length)
    allowed = (positions[None, :] <= positions[:, None]) & (doc_rows[None, :] == doc_rows[:, None])
    scores = jnp.where(allowed[None], scores, neg_large)
    row_maximum = lax.optimization_barrier(jnp.max(scores, axis=-1, keepdims=True))
    weights = jnp.exp(scores - row_maximum)
    probability = weights / lax.optimization_barrier(jnp.sum(weights, axis=-1, keepdims=True))
    prob_b = probability.astype(jnp.bfloat16)
    prob_bf = prob_b.astype(jnp.float32)
    output = jnp.einsum('hqk,kd->qhd', prob_bf, value_f).astype(jnp.bfloat16)
    prob_grad = jnp.einsum('qhd,kd->hqk', cotan_f, value_f)
    centre = lax.optimization_barrier(jnp.sum(probability * prob_grad, axis=-1, keepdims=True))
    dscore = (probability * (prob_grad - centre) * scale_factor).astype(jnp.bfloat16).astype(jnp.float32)
    dquery = jnp.einsum('hqk,kd->qhd', dscore, key_f)
    key_grad = jnp.einsum('hqk,qhd->kd', dscore, query_f)
    dvalue = jnp.einsum('hqk,qhd->kd', prob_bf, cotan_f)
    return (output, dquery, key_grad, dvalue)

def reference(x_input, wq_old, wq_fresh, key_projection_weight, value_projection_weight, attention_output_gradient, head_source, doc_ids):
    model_width = x_input.shape[1]
    token_stream = x_input.shape[0]
    source = jnp.concatenate([wq_old.reshape(model_width, N_HEAD, OLD_DEV, HEAD_SIZE), wq_fresh.reshape(model_width, N_HEAD, FRESH_DEV, HEAD_SIZE)], axis=2).reshape(model_width, HQ, HEAD_SIZE)
    wq_new = jnp.take(source, head_source, axis=1).reshape(model_width, HQ * HEAD_SIZE)
    cosine, sine_table = rotary_tables(TOK_DEV, HEAD_SIZE)
    projected = jnp.dot(x_input, wq_new, preferred_element_type=jnp.float32).reshape(N_DP, TOK_DEV, HQ, HEAD_SIZE)
    queries = rotate(projected, cosine, sine_table).astype(jnp.bfloat16).reshape(N_DP, TOK_DEV, N_HEAD, GROUP, HEAD_SIZE)
    key_proj = jnp.dot(x_input, key_projection_weight, preferred_element_type=jnp.float32).reshape(N_DP, TOK_DEV, N_HEAD, HEAD_SIZE)
    key_rot = rotate(key_proj, cosine, sine_table).astype(jnp.bfloat16)
    values = jnp.dot(x_input, value_projection_weight, preferred_element_type=jnp.float32).astype(jnp.bfloat16).reshape(N_DP, TOK_DEV, N_HEAD, HEAD_SIZE)
    cotangent = attention_output_gradient.reshape(N_DP, TOK_DEV, N_HEAD, GROUP, HEAD_SIZE)
    doc_rows = doc_ids.reshape(N_DP, TOK_DEV)
    per_group = jax.vmap(attention_pair, in_axes=(1, 1, 1, 1, None), out_axes=(1, 1, 1, 1))
    per_sequence = jax.vmap(per_group, in_axes=(0, 0, 0, 0, 0), out_axes=(0, 0, 0, 0))
    output, dquery, key_grad, dvalue = per_sequence(queries, key_rot, values, cotangent, doc_rows)
    attn_out = output.reshape(token_stream, HQ * HEAD_SIZE)
    dquery = rotate_back(dquery.reshape(N_DP, TOK_DEV, HQ, HEAD_SIZE), cosine, sine_table).astype(jnp.bfloat16).reshape(token_stream, HQ * HEAD_SIZE)
    key_grad = rotate_back(key_grad, cosine, sine_table).astype(jnp.bfloat16).reshape(token_stream, N_HEAD * HEAD_SIZE)
    dvalue = dvalue.astype(jnp.bfloat16).reshape(token_stream, N_HEAD * HEAD_SIZE)
    summed = jnp.zeros((token_stream, model_width), jnp.float32)
    query_cols = GROUP * HEAD_SIZE
    for member in range(N_HEAD):
        q_lo = member * query_cols
        k_lo = member * HEAD_SIZE
        portion = jnp.dot(dquery[:, q_lo:q_lo + query_cols], wq_new[:, q_lo:q_lo + query_cols].T, preferred_element_type=jnp.float32)
        portion = portion + jnp.dot(key_grad[:, k_lo:k_lo + HEAD_SIZE], key_projection_weight[:, k_lo:k_lo + HEAD_SIZE].T, preferred_element_type=jnp.float32)
        portion = portion + jnp.dot(dvalue[:, k_lo:k_lo + HEAD_SIZE], value_projection_weight[:, k_lo:k_lo + HEAD_SIZE].T, preferred_element_type=jnp.float32)
        rounded = lax.optimization_barrier(portion.astype(jnp.bfloat16))
        summed = summed + rounded.astype(jnp.float32)
    return (attn_out, summed.astype(jnp.bfloat16))
```

```python
import functools
import math

import jax
import jax.numpy as jnp
import numpy as np
from jax import lax
from jax.experimental import pallas as pl
from jax.experimental.pallas import tpu as pltpu
from jax.sharding import PartitionSpec as P

theta_base = 500000.0
neg_large = -1e30
MESH = pl.DeviceIdType.MESH


def rotary_tables(length, width):
    half = width // 2
    frequency = theta_base ** (-2.0 * np.arange(half, dtype=np.float64) / width)
    angles = np.arange(length, dtype=np.float64)[:, None] * frequency[None, :]
    cosine, sine = np.cos(angles), np.sin(angles)
    return (
        np.concatenate([cosine, cosine], axis=1).astype(np.float32),
        np.concatenate([-sine, sine], axis=1).astype(np.float32),
    )


def dot(a, b, ca, cb):
    return lax.dot_general(
        a, b, (((ca,), (cb,)), ((), ())), preferred_element_type=jnp.float32
    )


def kernel(
    n_dp, n_head, group, ways,
    src_ref, doc_hbm, cos_hbm, sin_hbm, x_hbm, old_hbm, fresh_hbm, k_hbm, v_hbm, g_hbm,
    out_ref, grad_ref,
    doc_ref, cos_ref, sin_ref, x_ref, own_ref, g_ref, wq, wkv, parcel, arrived, accq, acckv, dq_ref, dkv_ref,
    psend, precv,
    in_sem, rs, rr, cs, cr, hs, hr, ps, pr,
):
    me, head = lax.axis_index("dp"), lax.axis_index("head")
    rows, hd = k_hbm.shape
    length = x_ref.shape[0]
    lanes = 2
    m = n_dp // lanes
    core, chip = me % lanes, me // lanes
    side, level = chip % 2, chip // 2
    pos = (1 - side) * level + side * (m - 1 - level)
    piece = rows // ways
    sub = piece // 2
    lead = min(2, m - 2)
    parts = 3
    capacity = parcel.shape[2]
    signs = (1, -1)[:ways]
    bufs = (wkv, wq)
    spans = ((0, piece), (0, sub), (sub, sub))

    def index_of(p, lane):
        p = (p + 2 * m) % m
        far = p // (m // 2)
        return ((1 - far) * 2 * p + far * (2 * (m - 1 - p) + 1)) * lanes + lane

    right, left = index_of(pos + 1, core), index_of(pos - 1, core)
    targets = (right, left)[:ways]
    partner = index_of(pos, 1 - core)

    loads = [
        pltpu.make_async_copy(k_hbm, wkv.at[me, :, pl.ds(0, hd)], in_sem.at[0]),
        pltpu.make_async_copy(v_hbm, wkv.at[me, :, pl.ds(hd, hd)], in_sem.at[1]),
        pltpu.make_async_copy(old_hbm, own_ref.at[:, pl.ds(0, (group - 1) * hd)], in_sem.at[2]),
        pltpu.make_async_copy(fresh_hbm, own_ref.at[:, pl.ds((group - 1) * hd, hd)], in_sem.at[3]),
        pltpu.make_async_copy(x_hbm, x_ref, in_sem.at[4]),
        pltpu.make_async_copy(g_hbm, g_ref, in_sem.at[5]),
        pltpu.make_async_copy(doc_hbm, doc_ref, in_sem.at[6]),
        pltpu.make_async_copy(cos_hbm, cos_ref, in_sem.at[7]),
        pltpu.make_async_copy(sin_hbm, sin_ref, in_sem.at[8]),
    ]
    for load in loads:
        load.start()

    barrier = pltpu.get_barrier_semaphore()
    peers = [(right, head), (left, head), (partner, head)]
    peers += [(me, (head + j) % n_head) for j in range(1, n_head)]
    for peer in peers:
        pl.semaphore_signal(barrier, inc=1, device_id=peer, device_id_type=MESH)

    def part_of(p, w, owner):
        first, count = spans[p]
        return bufs[min(p, 1)].at[owner, pl.ds(w * piece + first, count)]

    def ring(p, w, s):
        ref = part_of(p, w, index_of(pos - signs[w] * s, core))
        return pltpu.make_async_remote_copy(
            ref, ref, rs.at[w * parts + p, s], rr.at[w * parts + p, s],
            device_id=(targets[w], head), device_id_type=MESH)

    def ring_in(p, w, s):
        ref = part_of(p, w, index_of(pos - signs[w] * (s + 1), core))
        return pltpu.make_async_remote_copy(
            ref, ref, rs.at[w * parts + p, s], rr.at[w * parts + p, s],
            device_id=(targets[w], head), device_id_type=MESH)

    def across(p, w, s, lane):
        ref = part_of(p, w, index_of(pos - signs[w] * s, lane))
        return pltpu.make_async_remote_copy(
            ref, ref, cs.at[w * parts + p, s], cr.at[w * parts + p, s],
            device_id=(partner, head), device_id_type=MESH)

    def relay(u, j):
        return pltpu.make_async_remote_copy(
            parcel.at[u, j - 1], arrived.at[u, j - 1], hs.at[u, j - 1], hr.at[u, j - 1],
            device_id=(me, (head + j) % n_head), device_id_type=MESH)

    shift = [(n_head - src_ref[k] // group) % n_head for k in range(group)]
    taken = [src_ref[k] % group for k in range(group)]
    slot = [
        sum([(shift[l] == shift[k]).astype(jnp.int32) for l in range(k)], jnp.int32(0))
        for k in range(group)
    ]

    def flag(cond):
        return jnp.where(cond, 1.0, 0.0).astype(jnp.float32)

    units = [w * 2 + half for half in range(2) for w in range(ways)]

    def weigh(u, weights):
        total = jnp.zeros((sub, hd), jnp.float32)
        for c_m in range(group):
            block = own_ref[u * sub:(u + 1) * sub, c_m * hd:(c_m + 1) * hd]
            total = total + block.astype(jnp.float32) * weights[c_m]
        return total.astype(jnp.bfloat16)

    for load in loads[:2]:
        load.wait()
    pl.semaphore_wait(barrier, len(peers))
    for w in range(ways):
        ring(0, w, 0).start()
    for w in range(ways):
        across(0, w, 0, core).start()
    for load in loads[2:4]:
        load.wait()
    for u in units:
        for j in range(1, n_head):
            for c in range(capacity):
                weights = [
                    sum([flag((shift[k] == j) & (slot[k] == c) & (taken[k] == c_m))
                         for k in range(group)], jnp.float32(0))
                    for c_m in range(group)
                ]
                parcel[u, j - 1, c] = weigh(u, weights)
            relay(u, j).start()
    for k in range(group):
        weights = [flag((shift[k] == 0) & (taken[k] == c_m)) for c_m in range(group)]
        for u in units:
            wq[me, u * sub:(u + 1) * sub, k * hd:(k + 1) * hd] = weigh(u, weights)
    for load in loads[4:]:
        load.wait()
    accq[...] = jnp.zeros_like(accq)
    acckv[...] = jnp.zeros_like(acckv)

    def add(p, w, owner):
        xs = x_ref[:, pl.ds(pl.multiple_of(owner * rows + w * piece, 128), piece)]
        acc = (acckv, accq)[p]
        acc[...] += dot(xs, bufs[p][owner, pl.ds(w * piece, piece), :], 1, 0)

    def pass_on(p, w, s):
        ring_in(p, w, s - 1).wait_recv()

        @pl.when(s < m - 1)
        def _():
            ring(p, w, s).start()

        across(p, w, s, core).start()

    def unit_out(u):
        block = pl.ds(u * sub, sub)
        for j in range(1, n_head):
            relay(u, j).wait_recv()
        for k in range(group):
            cols = slice(k * hd, (k + 1) * hd)
            total = wq[me, block, cols].astype(jnp.float32)
            for j in range(1, n_head):
                for c in range(capacity):
                    weight = flag((shift[k] == j) & (slot[k] == c))
                    total = total + arrived[u, j - 1, c].astype(jnp.float32) * weight
            wq[me, block, cols] = total.astype(jnp.bfloat16)
        ring(1 + u % 2, u // 2, 0).start()
        across(1 + u % 2, u // 2, 0, core).start()

    for w in range(ways):
        add(0, w, me)
    for u in units[:ways]:
        unit_out(u)
    for s in range(1, lead + 1):
        for w in range(ways):
            pass_on(0, w, s)
        if s == 1:
            for u in units[ways:]:
                unit_out(u)
    for w in range(ways):
        add(1, w, me)

    def step(s, carry):
        @pl.when(s + lead < m)
        def _():
            for w in range(ways):
                pass_on(0, w, s + lead)

        for p in range(1, parts):
            for w in range(ways):
                pass_on(p, w, s)
        for w in range(ways):
            for p in range(2):
                add(p, w, index_of(pos - signs[w] * s, core))
        for w in range(ways):
            for p in range(parts):
                across(p, w, s - 1, 1 - core).wait_recv()
        for w in range(ways):
            for p in range(2):
                add(p, w, index_of(pos - signs[w] * (s - 1), 1 - core))
        return carry

    lax.fori_loop(1, m, step, 0)
    for w in range(ways):
        for p in range(parts):
            across(p, w, m - 1, 1 - core).wait_recv()
        for p in range(2):
            add(p, w, index_of(pos - signs[w] * (m - 1), 1 - core))

    scale = 1.0 / math.sqrt(hd)
    cosine, sine = cos_ref[...], sin_ref[...]

    def rotate(f):
        return f * cosine + pltpu.roll(f, hd // 2, 1) * sine

    def rotate_back(f):
        return f * cosine - pltpu.roll(f, hd // 2, 1) * sine

    docs = jnp.broadcast_to(doc_ref[...].astype(jnp.float32), (length, length))
    at_key = lax.broadcasted_iota(jnp.int32, (length, length), 1)
    at_query = lax.broadcasted_iota(jnp.int32, (length, length), 0)
    allowed = (at_key <= at_query) & (docs == docs.T)
    key = rotate(acckv[:, :hd]).astype(jnp.bfloat16)
    value = acckv[:, hd:].astype(jnp.bfloat16)
    dkey = jnp.zeros((length, hd), jnp.float32)
    dvalue = jnp.zeros((length, hd), jnp.float32)
    for k in range(group):
        cols = slice(k * hd, (k + 1) * hd)
        query = rotate(accq[:, cols]).astype(jnp.bfloat16)
        given = g_ref[:, cols]
        scores = jnp.where(allowed, dot(query, key, 1, 1) * scale, neg_large)
        weights = jnp.exp(scores - jnp.max(scores, axis=-1, keepdims=True))
        probs = weights / jnp.sum(weights, axis=-1, keepdims=True)
        probs_b = probs.astype(jnp.bfloat16)
        out_ref[:, cols] = dot(probs_b, value, 1, 0).astype(jnp.bfloat16)
        prob_grad = dot(given, value, 1, 1)
        centre = jnp.sum(probs * prob_grad, axis=-1, keepdims=True)
        dscore = (probs * (prob_grad - centre) * scale).astype(jnp.bfloat16)
        dq_ref[:, cols] = rotate_back(dot(dscore, key, 1, 0)).astype(jnp.bfloat16)
        dkey = dkey + dot(dscore, query, 0, 0)
        dvalue = dvalue + dot(probs_b, given, 0, 0)
    dkv_ref[:, :hd] = rotate_back(dkey).astype(jnp.bfloat16)
    dkv_ref[:, hd:] = dvalue.astype(jnp.bfloat16)

    chunks = n_dp // n_head

    def partial(owner):
        return (dot(dq_ref[...], wq[owner], 1, 1) + dot(dkv_ref[...], wkv[owner], 1, 1)).astype(
            jnp.bfloat16)

    def share(j, i):
        return pltpu.make_async_remote_copy(
            psend.at[j - 1, i], precv.at[j - 1, i], ps.at[j - 1, i], pr.at[j - 1, i],
            device_id=(me, (head + j) % n_head), device_id_type=MESH)

    for j in range(1, n_head):
        def send_chunk(i, carry):
            psend[j - 1, i] = partial(((head + j) % n_head) * chunks + i)
            share(j, i).start()
            return carry

        lax.fori_loop(0, chunks, send_chunk, 0)

    def own_chunk(i, carry):
        cols = pl.ds(pl.multiple_of(i * rows, 128), rows)
        grad_ref[:, cols] = partial(head * chunks + i)
        return carry

    lax.fori_loop(0, chunks, own_chunk, 0)

    def finish(i, carry):
        cols = pl.ds(pl.multiple_of(i * rows, 128), rows)
        total = grad_ref[:, cols].astype(jnp.float32)
        for j in range(1, n_head):
            share(j, i).wait_recv()
            total = total + precv[j - 1, i].astype(jnp.float32)
        grad_ref[:, cols] = total.astype(jnp.bfloat16)
        return carry

    lax.fori_loop(0, chunks, finish, 0)

    def drain(s, carry):
        for p in range(parts):
            for w in range(ways):
                @pl.when(s < m - 1)
                def _():
                    ring(p, w, s).wait_send()

                across(p, w, s, core).wait_send()
        return carry

    lax.fori_loop(0, m, drain, 0)
    for j in range(1, n_head):
        for u in units:
            relay(u, j).wait_send()

        def drain_share(i, carry):
            share(j, i).wait_send()
            return carry

        lax.fori_loop(0, chunks, drain_share, 0)


def pair_kernel(
    n_dp, group, capacity,
    src_ref, doc_hbm, cos_hbm, sin_hbm, x_hbm, old_hbm, fresh_hbm, k_hbm, v_hbm, g_hbm,
    out_ref, grad_ref,
    doc_ref, cos_ref, sin_ref, x_ref, own_ref, g_ref, wq, wkv, oq, okv, parcel, arrived, accq, acckv,
    dq_ref, dkv_ref, eq_ref, ekv_ref, psend, precv,
    in_sem, rs, rr, cs, cr, hs, hr, ys, yr, ts, tr, ds, dr, ps, pr,
):
    me, head = lax.axis_index("dp"), lax.axis_index("head")
    rows, hd = k_hbm.shape
    length = x_ref.shape[0]
    lanes, ways, subs = 2, 2, 2
    m = n_dp // lanes
    half = n_dp // 2
    core, chip = me % lanes, me // lanes
    side, level = chip % 2, chip // 2
    pos = (1 - side) * level + side * (m - 1 - level)
    piece = rows // ways
    sub = piece // subs
    lead = min(m // 2, m - 2)
    near = m // 2
    signs = (1, -1)
    bufs = (wkv, wq)
    others = (okv, oq)
    parts = len(bufs) * subs

    def index_of(p, lane):
        p = (p + 2 * m) % m
        far = p // (m // 2)
        return ((1 - far) * 2 * p + far * (2 * (m - 1 - p) + 1)) * lanes + lane

    right, left = index_of(pos + 1, core), index_of(pos - 1, core)
    targets = (right, left)
    partner = index_of(pos, 1 - core)
    across_y = (me, 1 - head)

    loads = [
        pltpu.make_async_copy(k_hbm, wkv.at[me, :, pl.ds(0, hd)], in_sem.at[0]),
        pltpu.make_async_copy(v_hbm, wkv.at[me, :, pl.ds(hd, hd)], in_sem.at[1]),
    ]
    loads += [
        pltpu.make_async_copy(old_hbm.at[:, pl.ds(c * hd, hd)], own_ref.at[c], in_sem.at[2 + c])
        for c in range(group - 1)
    ]
    loads += [
        pltpu.make_async_copy(fresh_hbm, own_ref.at[group - 1], in_sem.at[group + 1]),
        pltpu.make_async_copy(x_hbm, x_ref, in_sem.at[group + 2]),
        pltpu.make_async_copy(g_hbm, g_ref, in_sem.at[group + 3]),
        pltpu.make_async_copy(doc_hbm, doc_ref, in_sem.at[group + 4]),
        pltpu.make_async_copy(cos_hbm, cos_ref, in_sem.at[group + 5]),
        pltpu.make_async_copy(sin_hbm, sin_ref, in_sem.at[group + 6]),
    ]
    for load in loads:
        load.start()

    barrier = pltpu.get_barrier_semaphore()
    peers = [(right, head), (left, head), (partner, head), across_y]
    for peer in peers:
        pl.semaphore_signal(barrier, inc=1, device_id=peer, device_id_type=MESH)

    def remote(src, dst, send, recv, device):
        return pltpu.make_async_remote_copy(
            src, dst, send, recv, device_id=device, device_id_type=MESH)

    def part_of(p, w, owner):
        return bufs[p // subs].at[owner, pl.ds(w * piece + p % subs * sub, sub)]

    def ring(p, w, s):
        ref = part_of(p, w, index_of(pos - signs[w] * s, core))
        return remote(ref, ref, rs.at[w * parts + p, s], rr.at[w * parts + p, s], (targets[w], head))

    def ring_in(p, w, s):
        ref = part_of(p, w, index_of(pos - signs[w] * (s + 1), core))
        return remote(ref, ref, rs.at[w * parts + p, s], rr.at[w * parts + p, s], (targets[w], head))

    def across(p, w, s, lane):
        ref = part_of(p, w, index_of(pos - signs[w] * s, lane))
        return remote(ref, ref, cs.at[w * parts + p, s], cr.at[w * parts + p, s], (partner, head))

    def forward(p, w, s, to):
        owner = index_of(pos - signs[w] * s, core)
        dst = others[p // subs].at[owner - to * half, pl.ds(w * piece + p % subs * sub, sub)]
        return remote(part_of(p, w, owner), dst, ys.at[w * parts + p, s], yr.at[w * parts + p, s], across_y)

    def share(b, w, s, lane):
        owner = index_of(pos - signs[w] * s, lane)
        ref = others[b].at[owner - head * half, pl.ds(w * piece, piece)]
        return remote(ref, ref, ts.at[w * 2 + b, s], tr.at[w * 2 + b, s], (partner, head))

    def for_here(w, s):
        return index_of(pos - signs[w] * s, core) // half == head

    def relay(u):
        return remote(parcel.at[u], arrived.at[u], hs.at[u], hr.at[u], across_y)

    def hand_on(p, w, s):
        @pl.when((s <= near) & jnp.logical_not(for_here(w, s)))
        def _():
            forward(p, w, s, 1 - head).start()

    shift = [(2 - src_ref[k] // group) % 2 for k in range(group)]
    taken = [src_ref[k] % group for k in range(group)]
    slot = [
        sum([(shift[l] == 1).astype(jnp.int32) for l in range(k)], jnp.int32(0)) * shift[k]
        for k in range(group)
    ]
    units = range(ways * subs)

    for load in loads[:2]:
        load.wait()
    pl.semaphore_wait(barrier, len(peers))
    for p in range(subs):
        for w in range(ways):
            ring(p, w, 0).start()
    for p in range(subs):
        for w in range(ways):
            across(p, w, 0, core).start()
    for load in loads[2:2 + group]:
        load.wait()
    for c in range(capacity):
        pick = sum([jnp.where((shift[k] == 1) & (slot[k] == c), taken[k], 0) for k in range(group)], jnp.int32(0))
        for u in units:
            parcel[u, c] = own_ref[pick, u * sub:(u + 1) * sub]
    for u in units:
        relay(u).start()
    for p in range(subs):
        for w in range(ways):
            hand_on(p, w, 0)
    for load in loads[2 + group:]:
        load.wait()

    def add(b, places):
        acc = (acckv, accq)[b]
        total = acc[...]
        for w, owner in places:
            xs = x_ref[:, pl.ds(pl.multiple_of(owner * rows + w * piece, 128), piece)]
            total = total + dot(xs, bufs[b][owner, pl.ds(w * piece, piece), :], 1, 0)
        acc[...] = total

    def pass_on(p, w, s):
        ring_in(p, w, s - 1).wait_recv()

        @pl.when(s < m - 1)
        def _():
            ring(p, w, s).start()

        across(p, w, s, core).start()
        hand_on(p, w, s)

    accq[...] = jnp.zeros_like(accq)
    acckv[...] = jnp.zeros_like(acckv)
    add(0, [(w, me) for w in range(ways)])
    for s in range(1, lead + 1):
        for p in range(subs):
            for w in range(ways):
                pass_on(p, w, s)
        if s == lead - 1:
            for u in units:
                relay(u).wait_recv()
            for u in units:
                block = slice(u * sub, (u + 1) * sub)
                for k in range(group):
                    wq[me, block, k * hd:(k + 1) * hd] = jnp.where(
                        shift[k] == 0, own_ref[taken[k], block], arrived[u, slot[k]])
            for p in range(subs, parts):
                for w in range(ways):
                    ring(p, w, 0).start()
            for p in range(subs, parts):
                for w in range(ways):
                    across(p, w, 0, core).start()
                    hand_on(p, w, 0)
    add(1, [(w, me) for w in range(ways)])

    def step(s, carry):
        @pl.when(s + lead < m)
        def _():
            for p in range(subs):
                for w in range(ways):
                    pass_on(p, w, s + lead)

        for p in range(subs, parts):
            for w in range(ways):
                pass_on(p, w, s)
        for w in range(ways):
            for p in range(parts):
                across(p, w, s - 1, 1 - core).wait_recv()
        places = [(w, index_of(pos - signs[w] * s, core)) for w in range(ways)]
        places += [(w, index_of(pos - signs[w] * (s - 1), 1 - core)) for w in range(ways)]
        for b in range(2):
            add(b, places)
        return carry

    lax.fori_loop(1, m, step, 0)
    for w in range(ways):
        for p in range(parts):
            across(p, w, m - 1, 1 - core).wait_recv()
    for b in range(2):
        add(b, [(w, index_of(pos - signs[w] * (m - 1), 1 - core)) for w in range(ways)])

    scale = 1.0 / math.sqrt(hd)
    cosine, sine = cos_ref[...], sin_ref[...]

    def rotate(f):
        return f * cosine + pltpu.roll(f, hd // 2, 1) * sine

    def rotate_back(f):
        return f * cosine - pltpu.roll(f, hd // 2, 1) * sine

    def swap_q(k):
        cols = pl.ds(k * hd, hd)
        return remote(dq_ref.at[:, cols], eq_ref.at[:, cols], ds.at[k], dr.at[k], across_y)

    swap_kv = remote(dkv_ref, ekv_ref, ds.at[group], dr.at[group], across_y)

    docs = jnp.broadcast_to(doc_ref[...].astype(jnp.float32), (length, length))
    at_key = lax.broadcasted_iota(jnp.int32, (length, length), 1)
    at_query = lax.broadcasted_iota(jnp.int32, (length, length), 0)
    allowed = (at_key <= at_query) & (docs == docs.T)
    key = rotate(acckv[:, :hd]).astype(jnp.bfloat16)
    value = acckv[:, hd:].astype(jnp.bfloat16)
    dkey = jnp.zeros((length, hd), jnp.float32)
    dvalue = jnp.zeros((length, hd), jnp.float32)
    for k in range(group):
        cols = slice(k * hd, (k + 1) * hd)
        query = rotate(accq[:, cols]).astype(jnp.bfloat16)
        given = g_ref[:, cols]
        scores = jnp.where(allowed, dot(query, key, 1, 1) * scale, neg_large)
        weights = jnp.exp(scores - jnp.max(scores, axis=-1, keepdims=True))
        probs = weights / jnp.sum(weights, axis=-1, keepdims=True)
        probs_b = probs.astype(jnp.bfloat16)
        out_ref[:, cols] = dot(probs_b, value, 1, 0).astype(jnp.bfloat16)
        prob_grad = dot(given, value, 1, 1)
        centre = jnp.sum(probs * prob_grad, axis=-1, keepdims=True)
        dscore = (probs * (prob_grad - centre) * scale).astype(jnp.bfloat16)
        dq_ref[:, cols] = rotate_back(dot(dscore, key, 1, 0)).astype(jnp.bfloat16)
        swap_q(k).start()
        dkey = dkey + dot(dscore, query, 0, 0)
        dvalue = dvalue + dot(probs_b, given, 0, 0)
    dkv_ref[:, :hd] = rotate_back(dkey).astype(jnp.bfloat16)
    dkv_ref[:, hd:] = dvalue.astype(jnp.bfloat16)
    swap_kv.start()

    def partial(owner, w):
        block = pl.ds(w * piece, piece)
        return (dot(dq_ref[...], wq[owner, block, :], 1, 1)
                + dot(dkv_ref[...], wkv[owner, block, :], 1, 1)).astype(jnp.bfloat16)

    def partial_other(place, w):
        block = pl.ds(w * piece, piece)
        return (dot(eq_ref[...], oq[place, block, :], 1, 1)
                + dot(ekv_ref[...], okv[place, block, :], 1, 1)).astype(jnp.bfloat16)

    def send_share(w, s, lane):
        at = (w, s - near - 1, lane)
        return remote(psend.at[at], precv.at[at], ps.at[at], pr.at[at], across_y)

    def far_steps(body):
        def loop(s, carry):
            for w in range(ways):
                body(w, s)
            return carry

        lax.fori_loop(near + 1, m, loop, 0)

    def near_steps(body):
        def loop(s, carry):
            for w in range(ways):
                body(w, s)
            return carry

        lax.fori_loop(0, near + 1, loop, 0)

    def send_far(w, s):
        @pl.when(jnp.logical_not(for_here(w, s)))
        def _():
            for lane in range(lanes):
                psend[w, s - near - 1, lane] = partial(index_of(pos - signs[w] * s, lane), w)
                send_share(w, s, lane).start()

    far_steps(send_far)

    def share_near(w, s):
        @pl.when(for_here(w, s))
        def _():
            for p in range(parts):
                forward(p, w, s, head).wait_recv()
            for b in range(2):
                share(b, w, s, core).start()

    near_steps(share_near)

    def columns(owner, w):
        return pl.ds(pl.multiple_of((owner - head * half) * rows + w * piece, 128), piece)

    def own_part(i, carry):
        owner = head * half + i
        for w in range(ways):
            grad_ref[:, columns(owner, w)] = partial(owner, w)
        return carry

    lax.fori_loop(0, half, own_part, 0)

    for k in range(group):
        swap_q(k).wait_recv()
    swap_kv.wait_recv()

    def plus(owner, w, value):
        cols = columns(owner, w)
        grad_ref[:, cols] = (grad_ref[:, cols].astype(jnp.float32) + value.astype(jnp.float32)).astype(jnp.bfloat16)

    def add_near(w, s):
        @pl.when(for_here(w, s))
        def _():
            for b in range(2):
                share(b, w, s, 1 - core).wait_recv()
            for lane in range(lanes):
                owner = index_of(pos - signs[w] * s, lane)
                plus(owner, w, partial_other(owner - head * half, w))

    near_steps(add_near)

    def add_far(w, s):
        @pl.when(for_here(w, s))
        def _():
            for lane in range(lanes):
                send_share(w, s, lane).wait_recv()
                plus(index_of(pos - signs[w] * s, lane), w, precv[w, s - near - 1, lane])

    far_steps(add_far)

    def drain(s, carry):
        for w in range(ways):
            for p in range(parts):
                @pl.when(s < m - 1)
                def _():
                    ring(p, w, s).wait_send()

                across(p, w, s, core).wait_send()
        return carry

    lax.fori_loop(0, m, drain, 0)

    def drain_near(w, s):
        @pl.when(jnp.logical_not(for_here(w, s)))
        def _():
            for p in range(parts):
                forward(p, w, s, 1 - head).wait_send()

        @pl.when(for_here(w, s))
        def _():
            for b in range(2):
                share(b, w, s, core).wait_send()

    near_steps(drain_near)

    def drain_far(w, s):
        @pl.when(jnp.logical_not(for_here(w, s)))
        def _():
            for lane in range(lanes):
                send_share(w, s, lane).wait_send()

    far_steps(drain_far)
    for u in units:
        relay(u).wait_send()
    for k in range(group):
        swap_q(k).wait_send()
    swap_kv.wait_send()


def pair_call(n_dp, x, old, fresh, wk, wv, g, head_source, doc_ids):
    length, width = x.shape
    rows, hd = wk.shape
    group = g.shape[1] // hd
    m, half, ways, subs = n_dp // 2, n_dp // 2, 2, 2
    near = m // 2
    capacity = (group + 1) // 2
    cosine, sine = rotary_tables(length, hd)
    bf, f32 = jnp.bfloat16, jnp.float32
    vm = pl.BlockSpec(memory_space=pltpu.VMEM)
    anyspace = pl.BlockSpec(memory_space=pl.ANY)
    dma = pltpu.SemaphoreType.DMA
    units, unit = ways * subs, rows // (ways * subs)
    parts = 2 * subs
    far = (ways, m - 1 - near, 2)
    return pl.pallas_call(
        functools.partial(pair_kernel, n_dp, group, capacity),
        out_shape=(
            jax.ShapeDtypeStruct((length, group * hd), bf),
            jax.ShapeDtypeStruct((length, width // 2), bf),
        ),
        in_specs=[pl.BlockSpec(memory_space=pltpu.SMEM)] + [anyspace] * 9,
        out_specs=(vm, vm),
        scratch_shapes=[
            pltpu.VMEM((1, length), jnp.int32),
            pltpu.VMEM((length, hd), f32),
            pltpu.VMEM((length, hd), f32),
            pltpu.VMEM((length, width), bf),
            pltpu.VMEM((group, rows, hd), bf),
            pltpu.VMEM((length, group * hd), bf),
            pltpu.VMEM((n_dp, rows, group * hd), bf),
            pltpu.VMEM((n_dp, rows, 2 * hd), bf),
            pltpu.VMEM((half, rows, group * hd), bf),
            pltpu.VMEM((half, rows, 2 * hd), bf),
            pltpu.VMEM((units, capacity, unit, hd), bf),
            pltpu.VMEM((units, capacity, unit, hd), bf),
            pltpu.VMEM((length, group * hd), f32),
            pltpu.VMEM((length, 2 * hd), f32),
            pltpu.VMEM((length, group * hd), bf),
            pltpu.VMEM((length, 2 * hd), bf),
            pltpu.VMEM((length, group * hd), bf),
            pltpu.VMEM((length, 2 * hd), bf),
            pltpu.VMEM(far + (length, rows // ways), bf),
            pltpu.VMEM(far + (length, rows // ways), bf),
            dma((group + 7,)),
            dma((parts * ways, m)),
            dma((parts * ways, m)),
            dma((parts * ways, m)),
            dma((parts * ways, m)),
            dma((units,)),
            dma((units,)),
            dma((parts * ways, near + 1)),
            dma((parts * ways, near + 1)),
            dma((2 * ways, near + 1)),
            dma((2 * ways, near + 1)),
            dma((group + 1,)),
            dma((group + 1,)),
            dma(far),
            dma(far),
        ],
        compiler_params=pltpu.CompilerParams(
            collective_id=0, has_side_effects=True, vmem_limit_bytes=67043328),
    )(head_source, doc_ids.reshape(1, -1), cosine, sine, x, old, fresh, wk, wv, g)


def solution(mesh):
    n_dp, n_head = mesh.shape["dp"], mesh.shape["head"]

    def local(x, old, fresh, wk, wv, g, head_source, doc_ids):
        length, width = x.shape
        rows, hd = wk.shape
        group = g.shape[1] // hd
        ways = 2 if rows % 256 == 0 else 1
        m = n_dp // 2
        if n_head == 2 and rows % 512 == 0 and m % 4 == 0:
            return pair_call(n_dp, x, old, fresh, wk, wv, g, head_source, doc_ids)
        capacity = (group + n_head - 1) // n_head
        chunks = n_dp // n_head
        cosine, sine = rotary_tables(length, hd)
        bf, f32 = jnp.bfloat16, jnp.float32
        vm = pl.BlockSpec(memory_space=pltpu.VMEM)
        anyspace = pl.BlockSpec(memory_space=pl.ANY)
        dma = pltpu.SemaphoreType.DMA
        return pl.pallas_call(
            functools.partial(kernel, n_dp, n_head, group, ways),
            out_shape=(
                jax.ShapeDtypeStruct((length, group * hd), bf),
                jax.ShapeDtypeStruct((length, width // n_head), bf),
            ),
            in_specs=[pl.BlockSpec(memory_space=pltpu.SMEM)] + [anyspace] * 9,
            out_specs=(vm, vm),
            scratch_shapes=[
                pltpu.VMEM((1, length), jnp.int32),
                pltpu.VMEM((length, hd), f32),
                pltpu.VMEM((length, hd), f32),
                pltpu.VMEM((length, width), bf),
                pltpu.VMEM((rows, group * hd), bf),
                pltpu.VMEM((length, group * hd), bf),
                pltpu.VMEM((n_dp, rows, group * hd), bf),
                pltpu.VMEM((n_dp, rows, 2 * hd), bf),
                pltpu.VMEM((2 * ways, n_head - 1, capacity, rows // (2 * ways), hd), bf),
                pltpu.VMEM((2 * ways, n_head - 1, capacity, rows // (2 * ways), hd), bf),
                pltpu.VMEM((length, group * hd), f32),
                pltpu.VMEM((length, 2 * hd), f32),
                pltpu.VMEM((length, group * hd), bf),
                pltpu.VMEM((length, 2 * hd), bf),
                pltpu.VMEM((n_head - 1, chunks, length, rows), bf),
                pltpu.VMEM((n_head - 1, chunks, length, rows), bf),
                dma((9,)),
                dma((3 * ways, m)),
                dma((3 * ways, m)),
                dma((3 * ways, m)),
                dma((3 * ways, m)),
                dma((2 * ways, n_head - 1)),
                dma((2 * ways, n_head - 1)),
                dma((n_head - 1, chunks)),
                dma((n_head - 1, chunks)),
            ],
            compiler_params=pltpu.CompilerParams(
                collective_id=0, has_side_effects=True, vmem_limit_bytes=67043328),
        )(head_source, doc_ids.reshape(1, -1), cosine, sine, x, old, fresh, wk, wv, g)

    in_specs = (
        P("dp", None), P("dp", "head"), P("dp", "head"), P("dp", "head"),
        P("dp", "head"), P("dp", "head"), P(), P("dp"),
    )
    return jax.shard_map(
        local, mesh=mesh, in_specs=in_specs,
        out_specs=(P("dp", "head"), P("dp", "head")), check_vma=False)
```

```python
import functools
import math

import jax
import jax.numpy as jnp
import numpy as np
from jax import lax
from jax.experimental import pallas as pl
from jax.experimental.pallas import tpu as pltpu
from jax.sharding import PartitionSpec as P

theta_base = 500000.0
neg_large = -1e30
MESH = pl.DeviceIdType.MESH


def rotary_tables(length, width):
    half = width // 2
    frequency = theta_base ** (-2.0 * np.arange(half, dtype=np.float64) / width)
    angles = np.arange(length, dtype=np.float64)[:, None] * frequency[None, :]
    cosine, sine = np.cos(angles), np.sin(angles)
    return (
        np.concatenate([cosine, cosine], axis=1).astype(np.float32),
        np.concatenate([-sine, sine], axis=1).astype(np.float32),
    )


def dot(a, b, ca, cb):
    return lax.dot_general(
        a, b, (((ca,), (cb,)), ((), ())), preferred_element_type=jnp.float32
    )


def kernel(
    n_dp, n_head, group, ways,
    src_ref, doc_hbm, cos_hbm, sin_hbm, x_hbm, old_hbm, fresh_hbm, k_hbm, v_hbm, g_hbm,
    out_ref, grad_ref,
    doc_ref, cos_ref, sin_ref, x_ref, own_ref, g_ref, wq, wkv, parcel, arrived, accq, acckv, dq_ref, dkv_ref,
    psend, precv,
    in_sem, rs, rr, cs, cr, hs, hr, ps, pr,
):
    me, head = lax.axis_index("dp"), lax.axis_index("head")
    rows, hd = k_hbm.shape
    length = x_ref.shape[0]
    lanes = 2
    m = n_dp // lanes
    core, chip = me % lanes, me // lanes
    side, level = chip % 2, chip // 2
    pos = (1 - side) * level + side * (m - 1 - level)
    piece = rows // ways
    sub = piece // 2
    lead = min(2, m - 2)
    parts = 3
    capacity = parcel.shape[2]
    signs = (1, -1)[:ways]
    bufs = (wkv, wq)
    spans = ((0, piece), (0, sub), (sub, sub))

    def index_of(p, lane):
        p = (p + 2 * m) % m
        far = p // (m // 2)
        return ((1 - far) * 2 * p + far * (2 * (m - 1 - p) + 1)) * lanes + lane

    right, left = index_of(pos + 1, core), index_of(pos - 1, core)
    targets = (right, left)[:ways]
    partner = index_of(pos, 1 - core)

    loads = [
        pltpu.make_async_copy(k_hbm, wkv.at[me, :, pl.ds(0, hd)], in_sem.at[0]),
        pltpu.make_async_copy(v_hbm, wkv.at[me, :, pl.ds(hd, hd)], in_sem.at[1]),
        pltpu.make_async_copy(old_hbm, own_ref.at[:, pl.ds(0, (group - 1) * hd)], in_sem.at[2]),
        pltpu.make_async_copy(fresh_hbm, own_ref.at[:, pl.ds((group - 1) * hd, hd)], in_sem.at[3]),
        pltpu.make_async_copy(x_hbm, x_ref, in_sem.at[4]),
        pltpu.make_async_copy(g_hbm, g_ref, in_sem.at[5]),
        pltpu.make_async_copy(doc_hbm, doc_ref, in_sem.at[6]),
        pltpu.make_async_copy(cos_hbm, cos_ref, in_sem.at[7]),
        pltpu.make_async_copy(sin_hbm, sin_ref, in_sem.at[8]),
    ]
    for load in loads:
        load.start()

    barrier = pltpu.get_barrier_semaphore()
    peers = [(right, head), (left, head), (partner, head)]
    peers += [(me, (head + j) % n_head) for j in range(1, n_head)]
    for peer in peers:
        pl.semaphore_signal(barrier, inc=1, device_id=peer, device_id_type=MESH)

    def part_of(p, w, owner):
        first, count = spans[p]
        return bufs[min(p, 1)].at[owner, pl.ds(w * piece + first, count)]

    def ring(p, w, s):
        ref = part_of(p, w, index_of(pos - signs[w] * s, core))
        return pltpu.make_async_remote_copy(
            ref, ref, rs.at[w * parts + p, s], rr.at[w * parts + p, s],
            device_id=(targets[w], head), device_id_type=MESH)

    def ring_in(p, w, s):
        ref = part_of(p, w, index_of(pos - signs[w] * (s + 1), core))
        return pltpu.make_async_remote_copy(
            ref, ref, rs.at[w * parts + p, s], rr.at[w * parts + p, s],
            device_id=(targets[w], head), device_id_type=MESH)

    def across(p, w, s, lane):
        ref = part_of(p, w, index_of(pos - signs[w] * s, lane))
        return pltpu.make_async_remote_copy(
            ref, ref, cs.at[w * parts + p, s], cr.at[w * parts + p, s],
            device_id=(partner, head), device_id_type=MESH)

    def relay(u, j):
        return pltpu.make_async_remote_copy(
            parcel.at[u, j - 1], arrived.at[u, j - 1], hs.at[u, j - 1], hr.at[u, j - 1],
            device_id=(me, (head + j) % n_head), device_id_type=MESH)

    shift = [(n_head - src_ref[k] // group) % n_head for k in range(group)]
    taken = [src_ref[k] % group for k in range(group)]
    slot = [
        sum([(shift[l] == shift[k]).astype(jnp.int32) for l in range(k)], jnp.int32(0))
        for k in range(group)
    ]

    def flag(cond):
        return jnp.where(cond, 1.0, 0.0).astype(jnp.float32)

    units = [w * 2 + half for half in range(2) for w in range(ways)]

    def weigh(u, weights):
        total = jnp.zeros((sub, hd), jnp.float32)
        for c_m in range(group):
            block = own_ref[u * sub:(u + 1) * sub, c_m * hd:(c_m + 1) * hd]
            total = total + block.astype(jnp.float32) * weights[c_m]
        return total.astype(jnp.bfloat16)

    for load in loads[:2]:
        load.wait()
    pl.semaphore_wait(barrier, len(peers))
    for w in range(ways):
        ring(0, w, 0).start()
    for w in range(ways):
        across(0, w, 0, core).start()
    for load in loads[2:4]:
        load.wait()
    for u in units:
        for j in range(1, n_head):
            for c in range(capacity):
                weights = [
                    sum([flag((shift[k] == j) & (slot[k] == c) & (taken[k] == c_m))
                         for k in range(group)], jnp.float32(0))
                    for c_m in range(group)
                ]
                parcel[u, j - 1, c] = weigh(u, weights)
            relay(u, j).start()
    for k in range(group):
        weights = [flag((shift[k] == 0) & (taken[k] == c_m)) for c_m in range(group)]
        for u in units:
            wq[me, u * sub:(u + 1) * sub, k * hd:(k + 1) * hd] = weigh(u, weights)
    for load in loads[4:]:
        load.wait()
    accq[...] = jnp.zeros_like(accq)
    acckv[...] = jnp.zeros_like(acckv)

    def add(p, w, owner):
        xs = x_ref[:, pl.ds(pl.multiple_of(owner * rows + w * piece, 128), piece)]
        acc = (acckv, accq)[p]
        acc[...] += dot(xs, bufs[p][owner, pl.ds(w * piece, piece), :], 1, 0)

    def pass_on(p, w, s):
        ring_in(p, w, s - 1).wait_recv()

        @pl.when(s < m - 1)
        def _():
            ring(p, w, s).start()

        across(p, w, s, core).start()

    def unit_out(u):
        block = pl.ds(u * sub, sub)
        for j in range(1, n_head):
            relay(u, j).wait_recv()
        for k in range(group):
            cols = slice(k * hd, (k + 1) * hd)
            total = wq[me, block, cols].astype(jnp.float32)
            for j in range(1, n_head):
                for c in range(capacity):
                    weight = flag((shift[k] == j) & (slot[k] == c))
                    total = total + arrived[u, j - 1, c].astype(jnp.float32) * weight
            wq[me, block, cols] = total.astype(jnp.bfloat16)
        ring(1 + u % 2, u // 2, 0).start()
        across(1 + u % 2, u // 2, 0, core).start()

    for w in range(ways):
        add(0, w, me)
    for u in units[:ways]:
        unit_out(u)
    for s in range(1, lead + 1):
        for w in range(ways):
            pass_on(0, w, s)
        if s == 1:
            for u in units[ways:]:
                unit_out(u)
    for w in range(ways):
        add(1, w, me)

    def step(s, carry):
        @pl.when(s + lead < m)
        def _():
            for w in range(ways):
                pass_on(0, w, s + lead)

        for p in range(1, parts):
            for w in range(ways):
                pass_on(p, w, s)
        for w in range(ways):
            for p in range(2):
                add(p, w, index_of(pos - signs[w] * s, core))
        for w in range(ways):
            for p in range(parts):
                across(p, w, s - 1, 1 - core).wait_recv()
        for w in range(ways):
            for p in range(2):
                add(p, w, index_of(pos - signs[w] * (s - 1), 1 - core))
        return carry

    lax.fori_loop(1, m, step, 0)
    for w in range(ways):
        for p in range(parts):
            across(p, w, m - 1, 1 - core).wait_recv()
        for p in range(2):
            add(p, w, index_of(pos - signs[w] * (m - 1), 1 - core))

    scale = 1.0 / math.sqrt(hd)
    cosine, sine = cos_ref[...], sin_ref[...]

    def rotate(f):
        return f * cosine + pltpu.roll(f, hd // 2, 1) * sine

    def rotate_back(f):
        return f * cosine - pltpu.roll(f, hd // 2, 1) * sine

    docs = jnp.broadcast_to(doc_ref[...].astype(jnp.float32), (length, length))
    at_key = lax.broadcasted_iota(jnp.int32, (length, length), 1)
    at_query = lax.broadcasted_iota(jnp.int32, (length, length), 0)
    allowed = (at_key <= at_query) & (docs == docs.T)
    key = rotate(acckv[:, :hd]).astype(jnp.bfloat16)
    value = acckv[:, hd:].astype(jnp.bfloat16)
    dkey = jnp.zeros((length, hd), jnp.float32)
    dvalue = jnp.zeros((length, hd), jnp.float32)
    for k in range(group):
        cols = slice(k * hd, (k + 1) * hd)
        query = rotate(accq[:, cols]).astype(jnp.bfloat16)
        given = g_ref[:, cols]
        scores = jnp.where(allowed, dot(query, key, 1, 1) * scale, neg_large)
        weights = jnp.exp(scores - jnp.max(scores, axis=-1, keepdims=True))
        probs = weights / jnp.sum(weights, axis=-1, keepdims=True)
        probs_b = probs.astype(jnp.bfloat16)
        out_ref[:, cols] = dot(probs_b, value, 1, 0).astype(jnp.bfloat16)
        prob_grad = dot(given, value, 1, 1)
        centre = jnp.sum(probs * prob_grad, axis=-1, keepdims=True)
        dscore = (probs * (prob_grad - centre) * scale).astype(jnp.bfloat16)
        dq_ref[:, cols] = rotate_back(dot(dscore, key, 1, 0)).astype(jnp.bfloat16)
        dkey = dkey + dot(dscore, query, 0, 0)
        dvalue = dvalue + dot(probs_b, given, 0, 0)
    dkv_ref[:, :hd] = rotate_back(dkey).astype(jnp.bfloat16)
    dkv_ref[:, hd:] = dvalue.astype(jnp.bfloat16)

    chunks = n_dp // n_head

    def partial(owner):
        return (dot(dq_ref[...], wq[owner], 1, 1) + dot(dkv_ref[...], wkv[owner], 1, 1)).astype(
            jnp.bfloat16)

    def share(j, i):
        return pltpu.make_async_remote_copy(
            psend.at[j - 1, i], precv.at[j - 1, i], ps.at[j - 1, i], pr.at[j - 1, i],
            device_id=(me, (head + j) % n_head), device_id_type=MESH)

    for j in range(1, n_head):
        def send_chunk(i, carry):
            psend[j - 1, i] = partial(((head + j) % n_head) * chunks + i)
            share(j, i).start()
            return carry

        lax.fori_loop(0, chunks, send_chunk, 0)

    def own_chunk(i, carry):
        cols = pl.ds(pl.multiple_of(i * rows, 128), rows)
        grad_ref[:, cols] = partial(head * chunks + i)
        return carry

    lax.fori_loop(0, chunks, own_chunk, 0)

    def finish(i, carry):
        cols = pl.ds(pl.multiple_of(i * rows, 128), rows)
        total = grad_ref[:, cols].astype(jnp.float32)
        for j in range(1, n_head):
            share(j, i).wait_recv()
            total = total + precv[j - 1, i].astype(jnp.float32)
        grad_ref[:, cols] = total.astype(jnp.bfloat16)
        return carry

    lax.fori_loop(0, chunks, finish, 0)

    def drain(s, carry):
        for p in range(parts):
            for w in range(ways):
                @pl.when(s < m - 1)
                def _():
                    ring(p, w, s).wait_send()

                across(p, w, s, core).wait_send()
        return carry

    lax.fori_loop(0, m, drain, 0)
    for j in range(1, n_head):
        for u in units:
            relay(u, j).wait_send()

        def drain_share(i, carry):
            share(j, i).wait_send()
            return carry

        lax.fori_loop(0, chunks, drain_share, 0)


def pair_kernel(
    n_dp, group, capacity,
    src_ref, doc_hbm, cos_hbm, sin_hbm, x_hbm, old_hbm, fresh_hbm, k_hbm, v_hbm, g_hbm,
    out_ref, grad_ref,
    doc_ref, cos_ref, sin_ref, x_ref, own_ref, g_ref, wq, wkv, oq, okv, parcel, arrived, accq, acckv,
    dq_ref, dkv_ref, eq_ref, ekv_ref, psend, precv,
    in_sem, rs, rr, cs, cr, hs, hr, ys, yr, ts, tr, ds, dr, ps, pr,
):
    me, head = lax.axis_index("dp"), lax.axis_index("head")
    rows, hd = k_hbm.shape
    length = x_ref.shape[0]
    lanes, ways, subs = 2, 2, 2
    m = n_dp // lanes
    half = n_dp // 2
    core, chip = me % lanes, me // lanes
    side, level = chip % 2, chip // 2
    pos = (1 - side) * level + side * (m - 1 - level)
    piece = rows // ways
    sub = piece // subs
    lead = min(m // 2, m - 2)
    near = m // 2
    signs = (1, -1)
    bufs = (wkv, wq)
    others = (okv, oq)
    parts = len(bufs) * subs

    def index_of(p, lane):
        p = (p + 2 * m) % m
        far = p // (m // 2)
        return ((1 - far) * 2 * p + far * (2 * (m - 1 - p) + 1)) * lanes + lane

    right, left = index_of(pos + 1, core), index_of(pos - 1, core)
    targets = (right, left)
    partner = index_of(pos, 1 - core)
    across_y = (me, 1 - head)

    loads = [
        pltpu.make_async_copy(k_hbm, wkv.at[me, :, pl.ds(0, hd)], in_sem.at[0]),
        pltpu.make_async_copy(v_hbm, wkv.at[me, :, pl.ds(hd, hd)], in_sem.at[1]),
    ]
    loads += [
        pltpu.make_async_copy(old_hbm.at[:, pl.ds(c * hd, hd)], own_ref.at[c], in_sem.at[2 + c])
        for c in range(group - 1)
    ]
    loads += [
        pltpu.make_async_copy(fresh_hbm, own_ref.at[group - 1], in_sem.at[group + 1]),
        pltpu.make_async_copy(x_hbm, x_ref, in_sem.at[group + 2]),
        pltpu.make_async_copy(g_hbm, g_ref, in_sem.at[group + 3]),
        pltpu.make_async_copy(doc_hbm, doc_ref, in_sem.at[group + 4]),
        pltpu.make_async_copy(cos_hbm, cos_ref, in_sem.at[group + 5]),
        pltpu.make_async_copy(sin_hbm, sin_ref, in_sem.at[group + 6]),
    ]
    for load in loads:
        load.start()

    barrier = pltpu.get_barrier_semaphore()
    peers = [(right, head), (left, head), (partner, head), across_y]
    for peer in peers:
        pl.semaphore_signal(barrier, inc=1, device_id=peer, device_id_type=MESH)

    def remote(src, dst, send, recv, device):
        return pltpu.make_async_remote_copy(
            src, dst, send, recv, device_id=device, device_id_type=MESH)

    def part_of(p, w, owner):
        return bufs[p // subs].at[owner, pl.ds(w * piece + p % subs * sub, sub)]

    def ring(p, w, s):
        ref = part_of(p, w, index_of(pos - signs[w] * s, core))
        return remote(ref, ref, rs.at[p // subs], rr.at[p, s], (targets[w], head))

    def ring_in(p, s):
        ref = bufs[p // subs].at[me, pl.ds(0, ways * sub)]
        return remote(ref, ref, rs.at[p // subs], rr.at[p, s], (left, head))

    def across(p, w, s, lane):
        ref = part_of(p, w, index_of(pos - signs[w] * s, lane))
        return remote(ref, ref, cs.at[p // subs], cr.at[p // subs, s], (partner, head))

    def across_in(b, s):
        ref = bufs[b].at[me]
        return remote(ref, ref, cs.at[b], cr.at[b, s], (partner, head))

    def forward(p, w, s, to):
        owner = index_of(pos - signs[w] * s, core)
        dst = others[p // subs].at[owner - to * half, pl.ds(w * piece + p % subs * sub, sub)]
        return remote(part_of(p, w, owner), dst, ys.at[p // subs], yr.at[p // subs], across_y)

    def share(b, w, s, lane):
        owner = index_of(pos - signs[w] * s, lane)
        ref = others[b].at[owner - head * half, pl.ds(w * piece, piece)]
        return remote(ref, ref, ts.at[b], tr.at[b], (partner, head))

    def all_of(b, count, send, recv):
        ref = bufs[b].at[pl.ds(0, count), pl.ds(0, piece)]
        return remote(ref, ref, send.at[b], recv.at[b], across_y)

    def for_here(w, s):
        return index_of(pos - signs[w] * s, core) // half == head

    def relay(u):
        return remote(parcel.at[u], arrived.at[u], hs.at[0], hr.at[0], across_y)

    def hand_on(p, w, s):
        @pl.when((s <= near) & jnp.logical_not(for_here(w, s)))
        def _():
            forward(p, w, s, 1 - head).start()

    shift = [(2 - src_ref[k] // group) % 2 for k in range(group)]
    taken = [src_ref[k] % group for k in range(group)]
    slot = [
        sum([(shift[l] == 1).astype(jnp.int32) for l in range(k)], jnp.int32(0)) * shift[k]
        for k in range(group)
    ]
    units = range(ways * subs)

    for load in loads[:2]:
        load.wait()
    pl.semaphore_wait(barrier, len(peers))
    for p in range(subs):
        for w in range(ways):
            ring(p, w, 0).start()
    for p in range(subs):
        for w in range(ways):
            across(p, w, 0, core).start()
    for load in loads[2:2 + group]:
        load.wait()
    for c in range(capacity):
        pick = sum([jnp.where((shift[k] == 1) & (slot[k] == c), taken[k], 0) for k in range(group)], jnp.int32(0))
        for u in units:
            parcel[u, c] = own_ref[pick, u * sub:(u + 1) * sub]
    for u in units:
        relay(u).start()
    for p in range(subs):
        for w in range(ways):
            hand_on(p, w, 0)
    for load in loads[2 + group:]:
        load.wait()

    def add(b, places):
        acc = (acckv, accq)[b]
        total = acc[...]
        for w, owner in places:
            xs = x_ref[:, pl.ds(pl.multiple_of(owner * rows + w * piece, 128), piece)]
            total = total + dot(xs, bufs[b][owner, pl.ds(w * piece, piece), :], 1, 0)
        acc[...] = total

    def pass_on(p, s):
        ring_in(p, s - 1).wait_recv()

        @pl.when(s < m - 1)
        def _():
            for w in range(ways):
                ring(p, w, s).start()

        for w in range(ways):
            across(p, w, s, core).start()
            hand_on(p, w, s)

    accq[...] = jnp.zeros_like(accq)
    acckv[...] = jnp.zeros_like(acckv)
    add(0, [(w, me) for w in range(ways)])
    for s in range(1, lead + 1):
        for p in range(subs):
            pass_on(p, s)
        if s == lead - 1:
            remote(parcel, arrived, hs.at[0], hr.at[0], across_y).wait_recv()
            for u in units:
                block = slice(u * sub, (u + 1) * sub)
                for k in range(group):
                    wq[me, block, k * hd:(k + 1) * hd] = jnp.where(
                        shift[k] == 0, own_ref[taken[k], block], arrived[u, slot[k]])
            for p in range(subs, parts):
                for w in range(ways):
                    ring(p, w, 0).start()
            for p in range(subs, parts):
                for w in range(ways):
                    across(p, w, 0, core).start()
                    hand_on(p, w, 0)
    add(1, [(w, me) for w in range(ways)])

    def step(s, carry):
        @pl.when(s + lead < m)
        def _():
            for p in range(subs):
                pass_on(p, s + lead)

        for p in range(subs, parts):
            pass_on(p, s)
        for b in range(2):
            across_in(b, s - 1).wait_recv()
        places = [(w, index_of(pos - signs[w] * s, core)) for w in range(ways)]
        places += [(w, index_of(pos - signs[w] * (s - 1), 1 - core)) for w in range(ways)]
        for b in range(2):
            add(b, places)
        return carry

    lax.fori_loop(1, m, step, 0)
    for b in range(2):
        across_in(b, m - 1).wait_recv()
        add(b, [(w, index_of(pos - signs[w] * (m - 1), 1 - core)) for w in range(ways)])

    scale = 1.0 / math.sqrt(hd)
    cosine, sine = cos_ref[...], sin_ref[...]

    def rotate(f):
        return f * cosine + pltpu.roll(f, hd // 2, 1) * sine

    def rotate_back(f):
        return f * cosine - pltpu.roll(f, hd // 2, 1) * sine

    def swap_q(k):
        cols = pl.ds(k * hd, hd)
        return remote(dq_ref.at[:, cols], eq_ref.at[:, cols], ds.at[0], dr.at[0], across_y)

    swap_kv = remote(dkv_ref, ekv_ref, ds.at[1], dr.at[1], across_y)
    swap_all_q = remote(dq_ref, eq_ref, ds.at[0], dr.at[0], across_y)

    docs = jnp.broadcast_to(doc_ref[...].astype(jnp.float32), (length, length))
    at_key = lax.broadcasted_iota(jnp.int32, (length, length), 1)
    at_query = lax.broadcasted_iota(jnp.int32, (length, length), 0)
    allowed = (at_key <= at_query) & (docs == docs.T)
    key = rotate(acckv[:, :hd]).astype(jnp.bfloat16)
    value = acckv[:, hd:].astype(jnp.bfloat16)
    dkey = jnp.zeros((length, hd), jnp.float32)
    dvalue = jnp.zeros((length, hd), jnp.float32)
    for k in range(group):
        cols = slice(k * hd, (k + 1) * hd)
        query = rotate(accq[:, cols]).astype(jnp.bfloat16)
        given = g_ref[:, cols]
        scores = jnp.where(allowed, dot(query, key, 1, 1) * scale, neg_large)
        weights = jnp.exp(scores - jnp.max(scores, axis=-1, keepdims=True))
        probs = weights / jnp.sum(weights, axis=-1, keepdims=True)
        probs_b = probs.astype(jnp.bfloat16)
        out_ref[:, cols] = dot(probs_b, value, 1, 0).astype(jnp.bfloat16)
        prob_grad = dot(given, value, 1, 1)
        centre = jnp.sum(probs * prob_grad, axis=-1, keepdims=True)
        dscore = (probs * (prob_grad - centre) * scale).astype(jnp.bfloat16)
        dq_ref[:, cols] = rotate_back(dot(dscore, key, 1, 0)).astype(jnp.bfloat16)
        swap_q(k).start()
        dkey = dkey + dot(dscore, query, 0, 0)
        dvalue = dvalue + dot(probs_b, given, 0, 0)
    dkv_ref[:, :hd] = rotate_back(dkey).astype(jnp.bfloat16)
    dkv_ref[:, hd:] = dvalue.astype(jnp.bfloat16)
    swap_kv.start()

    def partial(owner, w):
        block = pl.ds(w * piece, piece)
        return (dot(dq_ref[...], wq[owner, block, :], 1, 1)
                + dot(dkv_ref[...], wkv[owner, block, :], 1, 1)).astype(jnp.bfloat16)

    def partial_other(place, w):
        block = pl.ds(w * piece, piece)
        return (dot(eq_ref[...], oq[place, block, :], 1, 1)
                + dot(ekv_ref[...], okv[place, block, :], 1, 1)).astype(jnp.bfloat16)

    def send_share(w, s, lane):
        at = (w, s - near - 1, lane)
        return remote(psend.at[at], precv.at[at], ps.at[0], pr.at[at], across_y)

    def far_steps(body):
        def loop(s, carry):
            for w in range(ways):
                body(w, s)
            return carry

        lax.fori_loop(near + 1, m, loop, 0)

    def near_steps(body):
        def loop(s, carry):
            for w in range(ways):
                body(w, s)
            return carry

        lax.fori_loop(0, near + 1, loop, 0)

    def send_far(w, s):
        @pl.when(jnp.logical_not(for_here(w, s)))
        def _():
            for lane in range(lanes):
                psend[w, s - near - 1, lane] = partial(index_of(pos - signs[w] * s, lane), w)
                send_share(w, s, lane).start()

    far_steps(send_far)

    for b in range(2):
        all_of(b, near + 1, ys, yr).wait_recv()

    def share_near(w, s):
        @pl.when(for_here(w, s))
        def _():
            for b in range(2):
                share(b, w, s, core).start()

    near_steps(share_near)

    def columns(owner, w):
        return pl.ds(pl.multiple_of((owner - head * half) * rows + w * piece, 128), piece)

    def own_part(i, carry):
        owner = head * half + i
        for w in range(ways):
            grad_ref[:, columns(owner, w)] = partial(owner, w)
        return carry

    lax.fori_loop(0, half, own_part, 0)

    swap_all_q.wait_recv()
    swap_kv.wait_recv()
    for b in range(2):
        all_of(b, near + 1, ts, tr).wait_recv()

    def plus(owner, w, value):
        cols = columns(owner, w)
        grad_ref[:, cols] = (grad_ref[:, cols].astype(jnp.float32) + value.astype(jnp.float32)).astype(jnp.bfloat16)

    def add_near(w, s):
        @pl.when(for_here(w, s))
        def _():
            for lane in range(lanes):
                owner = index_of(pos - signs[w] * s, lane)
                plus(owner, w, partial_other(owner - head * half, w))

    near_steps(add_near)

    def add_far(w, s):
        @pl.when(for_here(w, s))
        def _():
            for lane in range(lanes):
                send_share(w, s, lane).wait_recv()
                plus(index_of(pos - signs[w] * s, lane), w, precv[w, s - near - 1, lane])

    far_steps(add_far)

    for b in range(2):
        for count, sent in ((ways * (m - 1), rs), (ways * m, cs), (near + 1, ys), (near + 1, ts)):
            all_of(b, count, sent, sent).wait_send()
    remote(parcel, arrived, hs.at[0], hr.at[0], across_y).wait_send()
    swap_all_q.wait_send()
    swap_kv.wait_send()
    ref = psend.at[:, :, 0]
    remote(ref, ref, ps.at[0], ps.at[0], across_y).wait_send()


def pair_call(n_dp, x, old, fresh, wk, wv, g, head_source, doc_ids):
    length, width = x.shape
    rows, hd = wk.shape
    group = g.shape[1] // hd
    m, half, ways, subs = n_dp // 2, n_dp // 2, 2, 2
    near = m // 2
    capacity = (group + 1) // 2
    cosine, sine = rotary_tables(length, hd)
    bf, f32 = jnp.bfloat16, jnp.float32
    vm = pl.BlockSpec(memory_space=pltpu.VMEM)
    anyspace = pl.BlockSpec(memory_space=pl.ANY)
    dma = pltpu.SemaphoreType.DMA
    units, unit = ways * subs, rows // (ways * subs)
    parts = 2 * subs
    far = (ways, m - 1 - near, 2)
    return pl.pallas_call(
        functools.partial(pair_kernel, n_dp, group, capacity),
        out_shape=(
            jax.ShapeDtypeStruct((length, group * hd), bf),
            jax.ShapeDtypeStruct((length, width // 2), bf),
        ),
        in_specs=[pl.BlockSpec(memory_space=pltpu.SMEM)] + [anyspace] * 9,
        out_specs=(vm, vm),
        scratch_shapes=[
            pltpu.VMEM((1, length), jnp.int32),
            pltpu.VMEM((length, hd), f32),
            pltpu.VMEM((length, hd), f32),
            pltpu.VMEM((length, width), bf),
            pltpu.VMEM((group, rows, hd), bf),
            pltpu.VMEM((length, group * hd), bf),
            pltpu.VMEM((n_dp, rows, group * hd), bf),
            pltpu.VMEM((n_dp, rows, 2 * hd), bf),
            pltpu.VMEM((half, rows, group * hd), bf),
            pltpu.VMEM((half, rows, 2 * hd), bf),
            pltpu.VMEM((units, capacity, unit, hd), bf),
            pltpu.VMEM((units, capacity, unit, hd), bf),
            pltpu.VMEM((length, group * hd), f32),
            pltpu.VMEM((length, 2 * hd), f32),
            pltpu.VMEM((length, group * hd), bf),
            pltpu.VMEM((length, 2 * hd), bf),
            pltpu.VMEM((length, group * hd), bf),
            pltpu.VMEM((length, 2 * hd), bf),
            pltpu.VMEM(far + (length, rows // ways), bf),
            pltpu.VMEM(far + (length, rows // ways), bf),
            dma((group + 7,)),
            dma((2,)),
            dma((parts, m)),
            dma((2,)),
            dma((2, m)),
            dma((1,)),
            dma((1,)),
            dma((2,)),
            dma((2,)),
            dma((2,)),
            dma((2,)),
            dma((2,)),
            dma((2,)),
            dma((1,)),
            dma(far),
        ],
        compiler_params=pltpu.CompilerParams(
            collective_id=0, has_side_effects=True, vmem_limit_bytes=67043328),
    )(head_source, doc_ids.reshape(1, -1), cosine, sine, x, old, fresh, wk, wv, g)


def solution(mesh):
    n_dp, n_head = mesh.shape["dp"], mesh.shape["head"]

    def local(x, old, fresh, wk, wv, g, head_source, doc_ids):
        length, width = x.shape
        rows, hd = wk.shape
        group = g.shape[1] // hd
        ways = 2 if rows % 256 == 0 else 1
        m = n_dp // 2
        if n_head == 2 and rows % 512 == 0 and m % 4 == 0:
            return pair_call(n_dp, x, old, fresh, wk, wv, g, head_source, doc_ids)
        capacity = (group + n_head - 1) // n_head
        chunks = n_dp // n_head
        cosine, sine = rotary_tables(length, hd)
        bf, f32 = jnp.bfloat16, jnp.float32
        vm = pl.BlockSpec(memory_space=pltpu.VMEM)
        anyspace = pl.BlockSpec(memory_space=pl.ANY)
        dma = pltpu.SemaphoreType.DMA
        return pl.pallas_call(
            functools.partial(kernel, n_dp, n_head, group, ways),
            out_shape=(
                jax.ShapeDtypeStruct((length, group * hd), bf),
                jax.ShapeDtypeStruct((length, width // n_head), bf),
            ),
            in_specs=[pl.BlockSpec(memory_space=pltpu.SMEM)] + [anyspace] * 9,
            out_specs=(vm, vm),
            scratch_shapes=[
                pltpu.VMEM((1, length), jnp.int32),
                pltpu.VMEM((length, hd), f32),
                pltpu.VMEM((length, hd), f32),
                pltpu.VMEM((length, width), bf),
                pltpu.VMEM((rows, group * hd), bf),
                pltpu.VMEM((length, group * hd), bf),
                pltpu.VMEM((n_dp, rows, group * hd), bf),
                pltpu.VMEM((n_dp, rows, 2 * hd), bf),
                pltpu.VMEM((2 * ways, n_head - 1, capacity, rows // (2 * ways), hd), bf),
                pltpu.VMEM((2 * ways, n_head - 1, capacity, rows // (2 * ways), hd), bf),
                pltpu.VMEM((length, group * hd), f32),
                pltpu.VMEM((length, 2 * hd), f32),
                pltpu.VMEM((length, group * hd), bf),
                pltpu.VMEM((length, 2 * hd), bf),
                pltpu.VMEM((n_head - 1, chunks, length, rows), bf),
                pltpu.VMEM((n_head - 1, chunks, length, rows), bf),
                dma((9,)),
                dma((3 * ways, m)),
                dma((3 * ways, m)),
                dma((3 * ways, m)),
                dma((3 * ways, m)),
                dma((2 * ways, n_head - 1)),
                dma((2 * ways, n_head - 1)),
                dma((n_head - 1, chunks)),
                dma((n_head - 1, chunks)),
            ],
            compiler_params=pltpu.CompilerParams(
                collective_id=0, has_side_effects=True, vmem_limit_bytes=67043328),
        )(head_source, doc_ids.reshape(1, -1), cosine, sine, x, old, fresh, wk, wv, g)

    in_specs = (
        P("dp", None), P("dp", "head"), P("dp", "head"), P("dp", "head"),
        P("dp", "head"), P("dp", "head"), P(), P("dp"),
    )
    return jax.shard_map(
        local, mesh=mesh, in_specs=in_specs,
        out_specs=(P("dp", "head"), P("dp", "head")), check_vma=False)
```

```python
import functools
import math

import jax
import jax.numpy as jnp
import numpy as np
from jax import lax
from jax.experimental import pallas as pl
from jax.experimental.pallas import tpu as pltpu
from jax.sharding import PartitionSpec as P

theta_base = 500000.0
neg_large = -1e30
MESH = pl.DeviceIdType.MESH


def rotary_tables(length, width):
    half = width // 2
    frequency = theta_base ** (-2.0 * np.arange(half, dtype=np.float64) / width)
    angles = np.arange(length, dtype=np.float64)[:, None] * frequency[None, :]
    cosine, sine = np.cos(angles), np.sin(angles)
    return (
        np.concatenate([cosine, cosine], axis=1).astype(np.float32),
        np.concatenate([-sine, sine], axis=1).astype(np.float32),
    )


def dot(a, b, ca, cb):
    return lax.dot_general(
        a, b, (((ca,), (cb,)), ((), ())), preferred_element_type=jnp.float32
    )


def kernel(
    n_dp, n_head, group, ways,
    src_ref, doc_hbm, cos_hbm, sin_hbm, x_hbm, old_hbm, fresh_hbm, k_hbm, v_hbm, g_hbm,
    out_ref, grad_ref,
    doc_ref, cos_ref, sin_ref, x_ref, own_ref, g_ref, wq, wkv, parcel, arrived, accq, acckv, dq_ref, dkv_ref,
    psend, precv,
    in_sem, rs, rr, cs, cr, hs, hr, ps, pr,
):
    me, head = lax.axis_index("dp"), lax.axis_index("head")
    rows, hd = k_hbm.shape
    length = x_ref.shape[0]
    lanes = 2
    m = n_dp // lanes
    core, chip = me % lanes, me // lanes
    side, level = chip % 2, chip // 2
    pos = (1 - side) * level + side * (m - 1 - level)
    piece = rows // ways
    sub = piece // 2
    lead = min(2, m - 2)
    parts = 3
    capacity = parcel.shape[2]
    signs = (1, -1)[:ways]
    bufs = (wkv, wq)
    spans = ((0, piece), (0, sub), (sub, sub))

    def index_of(p, lane):
        p = (p + 2 * m) % m
        far = p // (m // 2)
        return ((1 - far) * 2 * p + far * (2 * (m - 1 - p) + 1)) * lanes + lane

    right, left = index_of(pos + 1, core), index_of(pos - 1, core)
    targets = (right, left)[:ways]
    partner = index_of(pos, 1 - core)

    loads = [
        pltpu.make_async_copy(k_hbm, wkv.at[me, :, pl.ds(0, hd)], in_sem.at[0]),
        pltpu.make_async_copy(v_hbm, wkv.at[me, :, pl.ds(hd, hd)], in_sem.at[1]),
        pltpu.make_async_copy(old_hbm, own_ref.at[:, pl.ds(0, (group - 1) * hd)], in_sem.at[2]),
        pltpu.make_async_copy(fresh_hbm, own_ref.at[:, pl.ds((group - 1) * hd, hd)], in_sem.at[3]),
        pltpu.make_async_copy(x_hbm, x_ref, in_sem.at[4]),
        pltpu.make_async_copy(g_hbm, g_ref, in_sem.at[5]),
        pltpu.make_async_copy(doc_hbm, doc_ref, in_sem.at[6]),
        pltpu.make_async_copy(cos_hbm, cos_ref, in_sem.at[7]),
        pltpu.make_async_copy(sin_hbm, sin_ref, in_sem.at[8]),
    ]
    for load in loads:
        load.start()

    barrier = pltpu.get_barrier_semaphore()
    peers = [(right, head), (left, head), (partner, head)]
    peers += [(me, (head + j) % n_head) for j in range(1, n_head)]
    for peer in peers:
        pl.semaphore_signal(barrier, inc=1, device_id=peer, device_id_type=MESH)

    def part_of(p, w, owner):
        first, count = spans[p]
        return bufs[min(p, 1)].at[owner, pl.ds(w * piece + first, count)]

    def ring(p, w, s):
        ref = part_of(p, w, index_of(pos - signs[w] * s, core))
        return pltpu.make_async_remote_copy(
            ref, ref, rs.at[w * parts + p, s], rr.at[w * parts + p, s],
            device_id=(targets[w], head), device_id_type=MESH)

    def ring_in(p, w, s):
        ref = part_of(p, w, index_of(pos - signs[w] * (s + 1), core))
        return pltpu.make_async_remote_copy(
            ref, ref, rs.at[w * parts + p, s], rr.at[w * parts + p, s],
            device_id=(targets[w], head), device_id_type=MESH)

    def across(p, w, s, lane):
        ref = part_of(p, w, index_of(pos - signs[w] * s, lane))
        return pltpu.make_async_remote_copy(
            ref, ref, cs.at[w * parts + p, s], cr.at[w * parts + p, s],
            device_id=(partner, head), device_id_type=MESH)

    def relay(u, j):
        return pltpu.make_async_remote_copy(
            parcel.at[u, j - 1], arrived.at[u, j - 1], hs.at[u, j - 1], hr.at[u, j - 1],
            device_id=(me, (head + j) % n_head), device_id_type=MESH)

    shift = [(n_head - src_ref[k] // group) % n_head for k in range(group)]
    taken = [src_ref[k] % group for k in range(group)]
    slot = [
        sum([(shift[l] == shift[k]).astype(jnp.int32) for l in range(k)], jnp.int32(0))
        for k in range(group)
    ]

    def flag(cond):
        return jnp.where(cond, 1.0, 0.0).astype(jnp.float32)

    units = [w * 2 + half for half in range(2) for w in range(ways)]

    def weigh(u, weights):
        total = jnp.zeros((sub, hd), jnp.float32)
        for c_m in range(group):
            block = own_ref[u * sub:(u + 1) * sub, c_m * hd:(c_m + 1) * hd]
            total = total + block.astype(jnp.float32) * weights[c_m]
        return total.astype(jnp.bfloat16)

    for load in loads[:2]:
        load.wait()
    pl.semaphore_wait(barrier, len(peers))
    for w in range(ways):
        ring(0, w, 0).start()
    for w in range(ways):
        across(0, w, 0, core).start()
    for load in loads[2:4]:
        load.wait()
    for u in units:
        for j in range(1, n_head):
            for c in range(capacity):
                weights = [
                    sum([flag((shift[k] == j) & (slot[k] == c) & (taken[k] == c_m))
                         for k in range(group)], jnp.float32(0))
                    for c_m in range(group)
                ]
                parcel[u, j - 1, c] = weigh(u, weights)
            relay(u, j).start()
    for k in range(group):
        weights = [flag((shift[k] == 0) & (taken[k] == c_m)) for c_m in range(group)]
        for u in units:
            wq[me, u * sub:(u + 1) * sub, k * hd:(k + 1) * hd] = weigh(u, weights)
    for load in loads[4:]:
        load.wait()
    accq[...] = jnp.zeros_like(accq)
    acckv[...] = jnp.zeros_like(acckv)

    def add(p, w, owner):
        xs = x_ref[:, pl.ds(pl.multiple_of(owner * rows + w * piece, 128), piece)]
        acc = (acckv, accq)[p]
        acc[...] += dot(xs, bufs[p][owner, pl.ds(w * piece, piece), :], 1, 0)

    def pass_on(p, w, s):
        ring_in(p, w, s - 1).wait_recv()

        @pl.when(s < m - 1)
        def _():
            ring(p, w, s).start()

        across(p, w, s, core).start()

    def unit_out(u):
        block = pl.ds(u * sub, sub)
        for j in range(1, n_head):
            relay(u, j).wait_recv()
        for k in range(group):
            cols = slice(k * hd, (k + 1) * hd)
            total = wq[me, block, cols].astype(jnp.float32)
            for j in range(1, n_head):
                for c in range(capacity):
                    weight = flag((shift[k] == j) & (slot[k] == c))
                    total = total + arrived[u, j - 1, c].astype(jnp.float32) * weight
            wq[me, block, cols] = total.astype(jnp.bfloat16)
        ring(1 + u % 2, u // 2, 0).start()
        across(1 + u % 2, u // 2, 0, core).start()

    for w in range(ways):
        add(0, w, me)
    for u in units[:ways]:
        unit_out(u)
    for s in range(1, lead + 1):
        for w in range(ways):
            pass_on(0, w, s)
        if s == 1:
            for u in units[ways:]:
                unit_out(u)
    for w in range(ways):
        add(1, w, me)

    def step(s, carry):
        @pl.when(s + lead < m)
        def _():
            for w in range(ways):
                pass_on(0, w, s + lead)

        for p in range(1, parts):
            for w in range(ways):
                pass_on(p, w, s)
        for w in range(ways):
            for p in range(2):
                add(p, w, index_of(pos - signs[w] * s, core))
        for w in range(ways):
            for p in range(parts):
                across(p, w, s - 1, 1 - core).wait_recv()
        for w in range(ways):
            for p in range(2):
                add(p, w, index_of(pos - signs[w] * (s - 1), 1 - core))
        return carry

    lax.fori_loop(1, m, step, 0)
    for w in range(ways):
        for p in range(parts):
            across(p, w, m - 1, 1 - core).wait_recv()
        for p in range(2):
            add(p, w, index_of(pos - signs[w] * (m - 1), 1 - core))

    scale = 1.0 / math.sqrt(hd)
    cosine, sine = cos_ref[...], sin_ref[...]

    def rotate(f):
        return f * cosine + pltpu.roll(f, hd // 2, 1) * sine

    def rotate_back(f):
        return f * cosine - pltpu.roll(f, hd // 2, 1) * sine

    docs = jnp.broadcast_to(doc_ref[...].astype(jnp.float32), (length, length))
    at_key = lax.broadcasted_iota(jnp.int32, (length, length), 1)
    at_query = lax.broadcasted_iota(jnp.int32, (length, length), 0)
    allowed = (at_key <= at_query) & (docs == docs.T)
    key = rotate(acckv[:, :hd]).astype(jnp.bfloat16)
    value = acckv[:, hd:].astype(jnp.bfloat16)
    dkey = jnp.zeros((length, hd), jnp.float32)
    dvalue = jnp.zeros((length, hd), jnp.float32)
    for k in range(group):
        cols = slice(k * hd, (k + 1) * hd)
        query = rotate(accq[:, cols]).astype(jnp.bfloat16)
        given = g_ref[:, cols]
        scores = jnp.where(allowed, dot(query, key, 1, 1) * scale, neg_large)
        weights = jnp.exp(scores - jnp.max(scores, axis=-1, keepdims=True))
        probs = weights / jnp.sum(weights, axis=-1, keepdims=True)
        probs_b = probs.astype(jnp.bfloat16)
        out_ref[:, cols] = dot(probs_b, value, 1, 0).astype(jnp.bfloat16)
        prob_grad = dot(given, value, 1, 1)
        centre = jnp.sum(probs * prob_grad, axis=-1, keepdims=True)
        dscore = (probs * (prob_grad - centre) * scale).astype(jnp.bfloat16)
        dq_ref[:, cols] = rotate_back(dot(dscore, key, 1, 0)).astype(jnp.bfloat16)
        dkey = dkey + dot(dscore, query, 0, 0)
        dvalue = dvalue + dot(probs_b, given, 0, 0)
    dkv_ref[:, :hd] = rotate_back(dkey).astype(jnp.bfloat16)
    dkv_ref[:, hd:] = dvalue.astype(jnp.bfloat16)

    chunks = n_dp // n_head

    def partial(owner):
        return (dot(dq_ref[...], wq[owner], 1, 1) + dot(dkv_ref[...], wkv[owner], 1, 1)).astype(
            jnp.bfloat16)

    def share(j, i):
        return pltpu.make_async_remote_copy(
            psend.at[j - 1, i], precv.at[j - 1, i], ps.at[j - 1, i], pr.at[j - 1, i],
            device_id=(me, (head + j) % n_head), device_id_type=MESH)

    for j in range(1, n_head):
        def send_chunk(i, carry):
            psend[j - 1, i] = partial(((head + j) % n_head) * chunks + i)
            share(j, i).start()
            return carry

        lax.fori_loop(0, chunks, send_chunk, 0)

    def own_chunk(i, carry):
        cols = pl.ds(pl.multiple_of(i * rows, 128), rows)
        grad_ref[:, cols] = partial(head * chunks + i)
        return carry

    lax.fori_loop(0, chunks, own_chunk, 0)

    def finish(i, carry):
        cols = pl.ds(pl.multiple_of(i * rows, 128), rows)
        total = grad_ref[:, cols].astype(jnp.float32)
        for j in range(1, n_head):
            share(j, i).wait_recv()
            total = total + precv[j - 1, i].astype(jnp.float32)
        grad_ref[:, cols] = total.astype(jnp.bfloat16)
        return carry

    lax.fori_loop(0, chunks, finish, 0)

    def drain(s, carry):
        for p in range(parts):
            for w in range(ways):
                @pl.when(s < m - 1)
                def _():
                    ring(p, w, s).wait_send()

                across(p, w, s, core).wait_send()
        return carry

    lax.fori_loop(0, m, drain, 0)
    for j in range(1, n_head):
        for u in units:
            relay(u, j).wait_send()

        def drain_share(i, carry):
            share(j, i).wait_send()
            return carry

        lax.fori_loop(0, chunks, drain_share, 0)


def pair_kernel(
    n_dp, group, capacity,
    src_ref, doc_hbm, cos_hbm, sin_hbm, x_hbm, old_hbm, fresh_hbm, k_hbm, v_hbm, g_hbm,
    out_ref, grad_ref,
    doc_ref, cos_ref, sin_ref, x_ref, own_ref, g_ref, wq, wkv, oq, okv, parcel, arrived, accq, acckv,
    dq_ref, dkv_ref, eq_ref, ekv_ref, psend, precv,
    in_sem, rs, rr, cs, cr, hs, hr, ys, yr, ts, tr, ds, dr, ps, pr,
):
    me, head = lax.axis_index("dp"), lax.axis_index("head")
    rows, hd = k_hbm.shape
    length = x_ref.shape[0]
    lanes, ways, subs = 2, 2, 2
    m = n_dp // lanes
    half = n_dp // 2
    core, chip = me % lanes, me // lanes
    side, level = chip % 2, chip // 2
    pos = (1 - side) * level + side * (m - 1 - level)
    piece = rows // ways
    sub = piece // subs
    lead = min(m // 2, m - 2)
    near = m // 2
    signs = (1, -1)
    bufs = (wkv, wq)
    others = (okv, oq)
    parts = len(bufs) * subs

    def index_of(p, lane):
        p = (p + 2 * m) % m
        far = p // (m // 2)
        return ((1 - far) * 2 * p + far * (2 * (m - 1 - p) + 1)) * lanes + lane

    right, left = index_of(pos + 1, core), index_of(pos - 1, core)
    targets = (right, left)
    partner = index_of(pos, 1 - core)
    across_y = (me, 1 - head)

    loads = [
        pltpu.make_async_copy(k_hbm, wkv.at[me, :, pl.ds(0, hd)], in_sem.at[0]),
        pltpu.make_async_copy(v_hbm, wkv.at[me, :, pl.ds(hd, hd)], in_sem.at[1]),
    ]
    loads += [
        pltpu.make_async_copy(old_hbm.at[:, pl.ds(c * hd, hd)], own_ref.at[c], in_sem.at[2 + c])
        for c in range(group - 1)
    ]
    loads += [
        pltpu.make_async_copy(fresh_hbm, own_ref.at[group - 1], in_sem.at[group + 1]),
        pltpu.make_async_copy(x_hbm, x_ref, in_sem.at[group + 2]),
        pltpu.make_async_copy(g_hbm, g_ref, in_sem.at[group + 3]),
        pltpu.make_async_copy(doc_hbm, doc_ref, in_sem.at[group + 4]),
        pltpu.make_async_copy(cos_hbm, cos_ref, in_sem.at[group + 5]),
        pltpu.make_async_copy(sin_hbm, sin_ref, in_sem.at[group + 6]),
    ]
    for load in loads:
        load.start()

    barrier = pltpu.get_barrier_semaphore()
    peers = [(right, head), (left, head), (partner, head), across_y]
    for peer in peers:
        pl.semaphore_signal(barrier, inc=1, device_id=peer, device_id_type=MESH)

    def remote(src, dst, send, recv, device):
        return pltpu.make_async_remote_copy(
            src, dst, send, recv, device_id=device, device_id_type=MESH)

    def part_of(p, w, owner):
        return bufs[p // subs].at[owner, pl.ds(w * piece + p % subs * sub, sub)]

    def ring(p, w, s):
        ref = part_of(p, w, index_of(pos - signs[w] * s, core))
        return remote(ref, ref, rs.at[p // subs], rr.at[p, s], (targets[w], head))

    def ring_in(p, s):
        ref = bufs[p // subs].at[me, pl.ds(0, ways * sub)]
        return remote(ref, ref, rs.at[p // subs], rr.at[p, s], (left, head))

    def across(p, w, s, lane):
        ref = part_of(p, w, index_of(pos - signs[w] * s, lane))
        return remote(ref, ref, cs.at[p // subs], cr.at[p // subs, s], (partner, head))

    def across_in(b, s):
        ref = bufs[b].at[me]
        return remote(ref, ref, cs.at[b], cr.at[b, s], (partner, head))

    def forward(p, w, s, to):
        owner = index_of(pos - signs[w] * s, core)
        dst = others[p // subs].at[owner - to * half, pl.ds(w * piece + p % subs * sub, sub)]
        return remote(part_of(p, w, owner), dst, ys.at[p // subs], yr.at[p // subs], across_y)

    def share(b, w, s, lane):
        owner = index_of(pos - signs[w] * s, lane)
        ref = others[b].at[owner - head * half, pl.ds(w * piece, piece)]
        return remote(ref, ref, ts.at[b], tr.at[b], (partner, head))

    def all_of(b, count, send, recv):
        ref = bufs[b].at[pl.ds(0, count), pl.ds(0, piece)]
        return remote(ref, ref, send.at[b], recv.at[b], across_y)

    def for_here(w, s):
        return index_of(pos - signs[w] * s, core) // half == head

    def relay(u):
        return remote(parcel.at[u], arrived.at[u], hs.at[0], hr.at[0], across_y)

    def hand_on(p, w, s):
        @pl.when((s <= near) & jnp.logical_not(for_here(w, s)))
        def _():
            forward(p, w, s, 1 - head).start()

    shift = [(2 - src_ref[k] // group) % 2 for k in range(group)]
    taken = [src_ref[k] % group for k in range(group)]
    slot = [
        sum([(shift[l] == 1).astype(jnp.int32) for l in range(k)], jnp.int32(0)) * shift[k]
        for k in range(group)
    ]
    units = range(ways * subs)

    for load in loads[:2]:
        load.wait()
    pl.semaphore_wait(barrier, len(peers))
    for p in range(subs):
        for w in range(ways):
            ring(p, w, 0).start()
    for p in range(subs):
        for w in range(ways):
            across(p, w, 0, core).start()
    for load in loads[2:2 + group]:
        load.wait()
    for c in range(capacity):
        pick = sum([jnp.where((shift[k] == 1) & (slot[k] == c), taken[k], 0) for k in range(group)], jnp.int32(0))
        for u in units:
            parcel[u, c] = own_ref[pick, u * sub:(u + 1) * sub]
    for u in units:
        relay(u).start()
    for p in range(subs):
        for w in range(ways):
            hand_on(p, w, 0)
    for load in loads[2 + group:]:
        load.wait()

    def add(b, places):
        acc = (acckv, accq)[b]
        total = acc[...]
        for w, owner in places:
            xs = x_ref[:, pl.ds(pl.multiple_of(owner * rows + w * piece, 128), piece)]
            total = total + dot(xs, bufs[b][owner, pl.ds(w * piece, piece), :], 1, 0)
        acc[...] = total

    def pass_on(p, s):
        ring_in(p, s - 1).wait_recv()

        @pl.when(s < m - 1)
        def _():
            for w in range(ways):
                ring(p, w, s).start()

        for w in range(ways):
            across(p, w, s, core).start()
            hand_on(p, w, s)

    accq[...] = jnp.zeros_like(accq)
    acckv[...] = jnp.zeros_like(acckv)
    add(0, [(w, me) for w in range(ways)])
    for s in range(1, lead + 1):
        for p in range(subs):
            pass_on(p, s)
        if s == lead - 1:
            remote(parcel, arrived, hs.at[0], hr.at[0], across_y).wait_recv()
            for u in units:
                block = slice(u * sub, (u + 1) * sub)
                for k in range(group):
                    wq[me, block, k * hd:(k + 1) * hd] = jnp.where(
                        shift[k] == 0, own_ref[taken[k], block], arrived[u, slot[k]])
            for p in range(subs, parts):
                for w in range(ways):
                    ring(p, w, 0).start()
            for p in range(subs, parts):
                for w in range(ways):
                    across(p, w, 0, core).start()
                    hand_on(p, w, 0)
    add(1, [(w, me) for w in range(ways)])

    def step(s, carry):
        @pl.when(s + lead < m)
        def _():
            for p in range(subs):
                pass_on(p, s + lead)

        for p in range(subs, parts):
            pass_on(p, s)
        for b in range(2):
            across_in(b, s - 1).wait_recv()
        places = [(w, index_of(pos - signs[w] * s, core)) for w in range(ways)]
        places += [(w, index_of(pos - signs[w] * (s - 1), 1 - core)) for w in range(ways)]
        for b in range(2):
            add(b, places)
        return carry

    lax.fori_loop(1, m, step, 0)
    for b in range(2):
        across_in(b, m - 1).wait_recv()
        add(b, [(w, index_of(pos - signs[w] * (m - 1), 1 - core)) for w in range(ways)])

    scale = 1.0 / math.sqrt(hd)
    cosine, sine = cos_ref[...], sin_ref[...]

    def rotate(f):
        return f * cosine + pltpu.roll(f, hd // 2, 1) * sine

    def rotate_back(f):
        return f * cosine - pltpu.roll(f, hd // 2, 1) * sine

    def swap_q(k):
        cols = pl.ds(k * hd, hd)
        return remote(dq_ref.at[:, cols], eq_ref.at[:, cols], ds.at[0], dr.at[0], across_y)

    swap_kv = remote(dkv_ref, ekv_ref, ds.at[1], dr.at[1], across_y)
    swap_all_q = remote(dq_ref, eq_ref, ds.at[0], dr.at[0], across_y)

    docs = jnp.broadcast_to(doc_ref[...].astype(jnp.float32), (length, length))
    at_key = lax.broadcasted_iota(jnp.int32, (length, length), 1)
    at_query = lax.broadcasted_iota(jnp.int32, (length, length), 0)
    allowed = (at_key <= at_query) & (docs == docs.T)
    key = rotate(acckv[:, :hd]).astype(jnp.bfloat16)
    value = acckv[:, hd:].astype(jnp.bfloat16)
    dkey = jnp.zeros((length, hd), jnp.float32)
    dvalue = jnp.zeros((length, hd), jnp.float32)
    for k in range(group):
        cols = slice(k * hd, (k + 1) * hd)
        query = rotate(accq[:, cols]).astype(jnp.bfloat16)
        given = g_ref[:, cols]
        scores = jnp.where(allowed, dot(query, key, 1, 1) * scale, neg_large)
        weights = jnp.exp(scores - jnp.max(scores, axis=-1, keepdims=True))
        probs = weights / jnp.sum(weights, axis=-1, keepdims=True)
        probs_b = probs.astype(jnp.bfloat16)
        out_ref[:, cols] = dot(probs_b, value, 1, 0).astype(jnp.bfloat16)
        prob_grad = dot(given, value, 1, 1)
        centre = jnp.sum(probs * prob_grad, axis=-1, keepdims=True)
        dscore = (probs * (prob_grad - centre) * scale).astype(jnp.bfloat16)
        dq_ref[:, cols] = rotate_back(dot(dscore, key, 1, 0)).astype(jnp.bfloat16)
        swap_q(k).start()
        dkey = dkey + dot(dscore, query, 0, 0)
        dvalue = dvalue + dot(probs_b, given, 0, 0)
    dkv_ref[:, :hd] = rotate_back(dkey).astype(jnp.bfloat16)
    dkv_ref[:, hd:] = dvalue.astype(jnp.bfloat16)
    swap_kv.start()

    def partial(owner, w):
        block = pl.ds(w * piece, piece)
        return (dot(dq_ref[...], wq[owner, block, :], 1, 1)
                + dot(dkv_ref[...], wkv[owner, block, :], 1, 1)).astype(jnp.bfloat16)

    def partial_other(place, w):
        block = pl.ds(w * piece, piece)
        return (dot(eq_ref[...], oq[place, block, :], 1, 1)
                + dot(ekv_ref[...], okv[place, block, :], 1, 1)).astype(jnp.bfloat16)

    def send_share(w, s, lane):
        at = (w, s - near - 1, lane)
        return remote(psend.at[at], precv.at[at], ps.at[0], pr.at[at], across_y)

    def far_steps(body):
        def loop(s, carry):
            for w in range(ways):
                body(w, s)
            return carry

        lax.fori_loop(near + 1, m, loop, 0)

    def near_steps(body):
        def loop(s, carry):
            for w in range(ways):
                body(w, s)
            return carry

        lax.fori_loop(0, near + 1, loop, 0)

    def send_far(w, s):
        @pl.when(jnp.logical_not(for_here(w, s)))
        def _():
            for lane in range(lanes):
                psend[w, s - near - 1, lane] = partial(index_of(pos - signs[w] * s, lane), w)
                send_share(w, s, lane).start()

    far_steps(send_far)

    for b in range(2):
        all_of(b, near + 1, ys, yr).wait_recv()

    def share_near(w, s):
        @pl.when(for_here(w, s))
        def _():
            for b in range(2):
                share(b, w, s, core).start()

    near_steps(share_near)

    def columns(owner, w):
        return pl.ds(pl.multiple_of((owner - head * half) * rows + w * piece, 128), piece)

    def own_part(i, carry):
        owner = head * half + i
        for w in range(ways):
            grad_ref[:, columns(owner, w)] = partial(owner, w)
        return carry

    lax.fori_loop(0, half, own_part, 0)

    swap_all_q.wait_recv()
    swap_kv.wait_recv()
    for b in range(2):
        all_of(b, near + 1, ts, tr).wait_recv()

    def plus(owner, w, value):
        cols = columns(owner, w)
        grad_ref[:, cols] = (grad_ref[:, cols].astype(jnp.float32) + value.astype(jnp.float32)).astype(jnp.bfloat16)

    def add_near(w, s):
        @pl.when(for_here(w, s))
        def _():
            for lane in range(lanes):
                owner = index_of(pos - signs[w] * s, lane)
                plus(owner, w, partial_other(owner - head * half, w))

    near_steps(add_near)

    def add_far(w, s):
        @pl.when(for_here(w, s))
        def _():
            for lane in range(lanes):
                send_share(w, s, lane).wait_recv()
                plus(index_of(pos - signs[w] * s, lane), w, precv[w, s - near - 1, lane])

    far_steps(add_far)

    for b in range(2):
        for count, sent in ((ways * (m - 1), rs), (ways * m, cs), (near + 1, ys), (near + 1, ts)):
            all_of(b, count, sent, sent).wait_send()
    remote(parcel, arrived, hs.at[0], hr.at[0], across_y).wait_send()
    swap_all_q.wait_send()
    swap_kv.wait_send()
    ref = psend.at[:, :, 0]
    remote(ref, ref, ps.at[0], ps.at[0], across_y).wait_send()


def pair_call(n_dp, x, old, fresh, wk, wv, g, head_source, doc_ids):
    length, width = x.shape
    rows, hd = wk.shape
    group = g.shape[1] // hd
    m, half, ways, subs = n_dp // 2, n_dp // 2, 2, 2
    near = m // 2
    capacity = (group + 1) // 2
    cosine, sine = rotary_tables(length, hd)
    bf, f32 = jnp.bfloat16, jnp.float32
    vm = pl.BlockSpec(memory_space=pltpu.VMEM)
    anyspace = pl.BlockSpec(memory_space=pl.ANY)
    dma = pltpu.SemaphoreType.DMA
    units, unit = ways * subs, rows // (ways * subs)
    parts = 2 * subs
    far = (ways, m - 1 - near, 2)
    return pl.pallas_call(
        functools.partial(pair_kernel, n_dp, group, capacity),
        out_shape=(
            pltpu.VMEM((length, group * hd), bf),
            pltpu.VMEM((length, width // 2), bf),
        ),
        in_specs=[pl.BlockSpec(memory_space=pltpu.SMEM)] + [anyspace] * 9,
        out_specs=(vm, vm),
        scratch_shapes=[
            pltpu.VMEM((1, length), jnp.int32),
            pltpu.VMEM((length, hd), f32),
            pltpu.VMEM((length, hd), f32),
            pltpu.VMEM((length, width), bf),
            pltpu.VMEM((group, rows, hd), bf),
            pltpu.VMEM((length, group * hd), bf),
            pltpu.VMEM((n_dp, rows, group * hd), bf),
            pltpu.VMEM((n_dp, rows, 2 * hd), bf),
            pltpu.VMEM((half, rows, group * hd), bf),
            pltpu.VMEM((half, rows, 2 * hd), bf),
            pltpu.VMEM((units, capacity, unit, hd), bf),
            pltpu.VMEM((units, capacity, unit, hd), bf),
            pltpu.VMEM((length, group * hd), f32),
            pltpu.VMEM((length, 2 * hd), f32),
            pltpu.VMEM((length, group * hd), bf),
            pltpu.VMEM((length, 2 * hd), bf),
            pltpu.VMEM((length, group * hd), bf),
            pltpu.VMEM((length, 2 * hd), bf),
            pltpu.VMEM(far + (length, rows // ways), bf),
            pltpu.VMEM(far + (length, rows // ways), bf),
            dma((group + 7,)),
            dma((2,)),
            dma((parts, m)),
            dma((2,)),
            dma((2, m)),
            dma((1,)),
            dma((1,)),
            dma((2,)),
            dma((2,)),
            dma((2,)),
            dma((2,)),
            dma((2,)),
            dma((2,)),
            dma((1,)),
            dma(far),
        ],
        compiler_params=pltpu.CompilerParams(
            collective_id=0, has_side_effects=True, vmem_limit_bytes=48*1024*1024),
    )(*(pltpu.with_memory_space_constraint(jnp.asarray(a), pltpu.HBM) for a in (
        head_source, doc_ids.reshape(1, -1), cosine, sine, x, old, fresh, wk, wv, g)))


def solution(mesh):
    n_dp, n_head = mesh.shape["dp"], mesh.shape["head"]

    def local(x, old, fresh, wk, wv, g, head_source, doc_ids):
        length, width = x.shape
        rows, hd = wk.shape
        group = g.shape[1] // hd
        ways = 2 if rows % 256 == 0 else 1
        m = n_dp // 2
        if n_head == 2 and rows % 512 == 0 and m % 4 == 0:
            return pair_call(n_dp, x, old, fresh, wk, wv, g, head_source, doc_ids)
        capacity = (group + n_head - 1) // n_head
        chunks = n_dp // n_head
        cosine, sine = rotary_tables(length, hd)
        bf, f32 = jnp.bfloat16, jnp.float32
        vm = pl.BlockSpec(memory_space=pltpu.VMEM)
        anyspace = pl.BlockSpec(memory_space=pl.ANY)
        dma = pltpu.SemaphoreType.DMA
        return pl.pallas_call(
            functools.partial(kernel, n_dp, n_head, group, ways),
            out_shape=(
                jax.ShapeDtypeStruct((length, group * hd), bf),
                jax.ShapeDtypeStruct((length, width // n_head), bf),
            ),
            in_specs=[pl.BlockSpec(memory_space=pltpu.SMEM)] + [anyspace] * 9,
            out_specs=(vm, vm),
            scratch_shapes=[
                pltpu.VMEM((1, length), jnp.int32),
                pltpu.VMEM((length, hd), f32),
                pltpu.VMEM((length, hd), f32),
                pltpu.VMEM((length, width), bf),
                pltpu.VMEM((rows, group * hd), bf),
                pltpu.VMEM((length, group * hd), bf),
                pltpu.VMEM((n_dp, rows, group * hd), bf),
                pltpu.VMEM((n_dp, rows, 2 * hd), bf),
                pltpu.VMEM((2 * ways, n_head - 1, capacity, rows // (2 * ways), hd), bf),
                pltpu.VMEM((2 * ways, n_head - 1, capacity, rows // (2 * ways), hd), bf),
                pltpu.VMEM((length, group * hd), f32),
                pltpu.VMEM((length, 2 * hd), f32),
                pltpu.VMEM((length, group * hd), bf),
                pltpu.VMEM((length, 2 * hd), bf),
                pltpu.VMEM((n_head - 1, chunks, length, rows), bf),
                pltpu.VMEM((n_head - 1, chunks, length, rows), bf),
                dma((9,)),
                dma((3 * ways, m)),
                dma((3 * ways, m)),
                dma((3 * ways, m)),
                dma((3 * ways, m)),
                dma((2 * ways, n_head - 1)),
                dma((2 * ways, n_head - 1)),
                dma((n_head - 1, chunks)),
                dma((n_head - 1, chunks)),
            ],
            compiler_params=pltpu.CompilerParams(
                collective_id=0, has_side_effects=True, vmem_limit_bytes=67043328),
        )(head_source, doc_ids.reshape(1, -1), cosine, sine, x, old, fresh, wk, wv, g)

    in_specs = (
        P("dp", None), P("dp", "head"), P("dp", "head"), P("dp", "head"),
        P("dp", "head"), P("dp", "head"), P(), P("dp"),
    )
    return jax.shard_map(
        local, mesh=mesh, in_specs=in_specs,
        out_specs=(P("dp", "head"), P("dp", "head")), check_vma=False)
```

```python
import functools
import math

import jax
import jax.numpy as jnp
import numpy as np
from jax import lax
from jax.experimental import pallas as pl
from jax.experimental.pallas import tpu as pltpu
from jax.sharding import PartitionSpec as P

theta_base = 500000.0
neg_large = -1e30
MESH = pl.DeviceIdType.MESH


def rotary_tables(length, width):
    half = width // 2
    frequency = theta_base ** (-2.0 * np.arange(half, dtype=np.float64) / width)
    angles = np.arange(length, dtype=np.float64)[:, None] * frequency[None, :]
    cosine, sine = np.cos(angles), np.sin(angles)
    return (
        np.concatenate([cosine, cosine], axis=1).astype(np.float32),
        np.concatenate([-sine, sine], axis=1).astype(np.float32),
    )


def dot(a, b, ca, cb):
    return lax.dot_general(
        a, b, (((ca,), (cb,)), ((), ())), preferred_element_type=jnp.float32
    )


def kernel(
    n_dp, n_head, group, ways,
    src_ref, doc_hbm, cos_hbm, sin_hbm, x_hbm, old_hbm, fresh_hbm, k_hbm, v_hbm, g_hbm,
    out_ref, grad_ref,
    doc_ref, cos_ref, sin_ref, x_ref, own_ref, g_ref, wq, wkv, parcel, arrived, accq, acckv, dq_ref, dkv_ref,
    psend, precv,
    in_sem, rs, rr, cs, cr, hs, hr, ps, pr,
):
    me, head = lax.axis_index("dp"), lax.axis_index("head")
    rows, hd = k_hbm.shape
    length = x_ref.shape[0]
    lanes = 2
    m = n_dp // lanes
    core, chip = me % lanes, me // lanes
    side, level = chip % 2, chip // 2
    pos = (1 - side) * level + side * (m - 1 - level)
    piece = rows // ways
    sub = piece // 2
    lead = min(2, m - 2)
    parts = 3
    capacity = parcel.shape[2]
    signs = (1, -1)[:ways]
    bufs = (wkv, wq)
    spans = ((0, piece), (0, sub), (sub, sub))

    def index_of(p, lane):
        p = (p + 2 * m) % m
        far = p // (m // 2)
        return ((1 - far) * 2 * p + far * (2 * (m - 1 - p) + 1)) * lanes + lane

    right, left = index_of(pos + 1, core), index_of(pos - 1, core)
    targets = (right, left)[:ways]
    partner = index_of(pos, 1 - core)

    loads = [
        pltpu.make_async_copy(k_hbm, wkv.at[me, :, pl.ds(0, hd)], in_sem.at[0]),
        pltpu.make_async_copy(v_hbm, wkv.at[me, :, pl.ds(hd, hd)], in_sem.at[1]),
        pltpu.make_async_copy(old_hbm, own_ref.at[:, pl.ds(0, (group - 1) * hd)], in_sem.at[2]),
        pltpu.make_async_copy(fresh_hbm, own_ref.at[:, pl.ds((group - 1) * hd, hd)], in_sem.at[3]),
        pltpu.make_async_copy(x_hbm, x_ref, in_sem.at[4]),
        pltpu.make_async_copy(g_hbm, g_ref, in_sem.at[5]),
        pltpu.make_async_copy(doc_hbm, doc_ref, in_sem.at[6]),
        pltpu.make_async_copy(cos_hbm, cos_ref, in_sem.at[7]),
        pltpu.make_async_copy(sin_hbm, sin_ref, in_sem.at[8]),
    ]
    for load in loads:
        load.start()

    barrier = pltpu.get_barrier_semaphore()
    peers = [(right, head), (left, head), (partner, head)]
    peers += [(me, (head + j) % n_head) for j in range(1, n_head)]
    for peer in peers:
        pl.semaphore_signal(barrier, inc=1, device_id=peer, device_id_type=MESH)

    def part_of(p, w, owner):
        first, count = spans[p]
        return bufs[min(p, 1)].at[owner, pl.ds(w * piece + first, count)]

    def ring(p, w, s):
        ref = part_of(p, w, index_of(pos - signs[w] * s, core))
        return pltpu.make_async_remote_copy(
            ref, ref, rs.at[w * parts + p, s], rr.at[w * parts + p, s],
            device_id=(targets[w], head), device_id_type=MESH)

    def ring_in(p, w, s):
        ref = part_of(p, w, index_of(pos - signs[w] * (s + 1), core))
        return pltpu.make_async_remote_copy(
            ref, ref, rs.at[w * parts + p, s], rr.at[w * parts + p, s],
            device_id=(targets[w], head), device_id_type=MESH)

    def across(p, w, s, lane):
        ref = part_of(p, w, index_of(pos - signs[w] * s, lane))
        return pltpu.make_async_remote_copy(
            ref, ref, cs.at[w * parts + p, s], cr.at[w * parts + p, s],
            device_id=(partner, head), device_id_type=MESH)

    def relay(u, j):
        return pltpu.make_async_remote_copy(
            parcel.at[u, j - 1], arrived.at[u, j - 1], hs.at[u, j - 1], hr.at[u, j - 1],
            device_id=(me, (head + j) % n_head), device_id_type=MESH)

    shift = [(n_head - src_ref[k] // group) % n_head for k in range(group)]
    taken = [src_ref[k] % group for k in range(group)]
    slot = [
        sum([(shift[l] == shift[k]).astype(jnp.int32) for l in range(k)], jnp.int32(0))
        for k in range(group)
    ]

    def flag(cond):
        return jnp.where(cond, 1.0, 0.0).astype(jnp.float32)

    units = [w * 2 + half for half in range(2) for w in range(ways)]

    def weigh(u, weights):
        total = jnp.zeros((sub, hd), jnp.float32)
        for c_m in range(group):
            block = own_ref[u * sub:(u + 1) * sub, c_m * hd:(c_m + 1) * hd]
            total = total + block.astype(jnp.float32) * weights[c_m]
        return total.astype(jnp.bfloat16)

    for load in loads[:2]:
        load.wait()
    pl.semaphore_wait(barrier, len(peers))
    for w in range(ways):
        ring(0, w, 0).start()
    for w in range(ways):
        across(0, w, 0, core).start()
    for load in loads[2:4]:
        load.wait()
    for u in units:
        for j in range(1, n_head):
            for c in range(capacity):
                weights = [
                    sum([flag((shift[k] == j) & (slot[k] == c) & (taken[k] == c_m))
                         for k in range(group)], jnp.float32(0))
                    for c_m in range(group)
                ]
                parcel[u, j - 1, c] = weigh(u, weights)
            relay(u, j).start()
    for k in range(group):
        weights = [flag((shift[k] == 0) & (taken[k] == c_m)) for c_m in range(group)]
        for u in units:
            wq[me, u * sub:(u + 1) * sub, k * hd:(k + 1) * hd] = weigh(u, weights)
    for load in loads[4:]:
        load.wait()
    accq[...] = jnp.zeros_like(accq)
    acckv[...] = jnp.zeros_like(acckv)

    def add(p, w, owner):
        xs = x_ref[:, pl.ds(pl.multiple_of(owner * rows + w * piece, 128), piece)]
        acc = (acckv, accq)[p]
        acc[...] += dot(xs, bufs[p][owner, pl.ds(w * piece, piece), :], 1, 0)

    def pass_on(p, w, s):
        ring_in(p, w, s - 1).wait_recv()

        @pl.when(s < m - 1)
        def _():
            ring(p, w, s).start()

        across(p, w, s, core).start()

    def unit_out(u):
        block = pl.ds(u * sub, sub)
        for j in range(1, n_head):
            relay(u, j).wait_recv()
        for k in range(group):
            cols = slice(k * hd, (k + 1) * hd)
            total = wq[me, block, cols].astype(jnp.float32)
            for j in range(1, n_head):
                for c in range(capacity):
                    weight = flag((shift[k] == j) & (slot[k] == c))
                    total = total + arrived[u, j - 1, c].astype(jnp.float32) * weight
            wq[me, block, cols] = total.astype(jnp.bfloat16)
        ring(1 + u % 2, u // 2, 0).start()
        across(1 + u % 2, u // 2, 0, core).start()

    for w in range(ways):
        add(0, w, me)
    for u in units[:ways]:
        unit_out(u)
    for s in range(1, lead + 1):
        for w in range(ways):
            pass_on(0, w, s)
        if s == 1:
            for u in units[ways:]:
                unit_out(u)
    for w in range(ways):
        add(1, w, me)

    def step(s, carry):
        @pl.when(s + lead < m)
        def _():
            for w in range(ways):
                pass_on(0, w, s + lead)

        for p in range(1, parts):
            for w in range(ways):
                pass_on(p, w, s)
        for w in range(ways):
            for p in range(2):
                add(p, w, index_of(pos - signs[w] * s, core))
        for w in range(ways):
            for p in range(parts):
                across(p, w, s - 1, 1 - core).wait_recv()
        for w in range(ways):
            for p in range(2):
                add(p, w, index_of(pos - signs[w] * (s - 1), 1 - core))
        return carry

    lax.fori_loop(1, m, step, 0)
    for w in range(ways):
        for p in range(parts):
            across(p, w, m - 1, 1 - core).wait_recv()
        for p in range(2):
            add(p, w, index_of(pos - signs[w] * (m - 1), 1 - core))

    scale = 1.0 / math.sqrt(hd)
    cosine, sine = cos_ref[...], sin_ref[...]

    def rotate(f):
        return f * cosine + pltpu.roll(f, hd // 2, 1) * sine

    def rotate_back(f):
        return f * cosine - pltpu.roll(f, hd // 2, 1) * sine

    docs = jnp.broadcast_to(doc_ref[...].astype(jnp.float32), (length, length))
    at_key = lax.broadcasted_iota(jnp.int32, (length, length), 1)
    at_query = lax.broadcasted_iota(jnp.int32, (length, length), 0)
    allowed = (at_key <= at_query) & (docs == docs.T)
    key = rotate(acckv[:, :hd]).astype(jnp.bfloat16)
    value = acckv[:, hd:].astype(jnp.bfloat16)
    dkey = jnp.zeros((length, hd), jnp.float32)
    dvalue = jnp.zeros((length, hd), jnp.float32)
    for k in range(group):
        cols = slice(k * hd, (k + 1) * hd)
        query = rotate(accq[:, cols]).astype(jnp.bfloat16)
        given = g_ref[:, cols]
        scores = jnp.where(allowed, dot(query, key, 1, 1) * scale, neg_large)
        weights = jnp.exp(scores - jnp.max(scores, axis=-1, keepdims=True))
        probs = weights / jnp.sum(weights, axis=-1, keepdims=True)
        probs_b = probs.astype(jnp.bfloat16)
        out_ref[:, cols] = dot(probs_b, value, 1, 0).astype(jnp.bfloat16)
        prob_grad = dot(given, value, 1, 1)
        centre = jnp.sum(probs * prob_grad, axis=-1, keepdims=True)
        dscore = (probs * (prob_grad - centre) * scale).astype(jnp.bfloat16)
        dq_ref[:, cols] = rotate_back(dot(dscore, key, 1, 0)).astype(jnp.bfloat16)
        dkey = dkey + dot(dscore, query, 0, 0)
        dvalue = dvalue + dot(probs_b, given, 0, 0)
    dkv_ref[:, :hd] = rotate_back(dkey).astype(jnp.bfloat16)
    dkv_ref[:, hd:] = dvalue.astype(jnp.bfloat16)

    chunks = n_dp // n_head

    def partial(owner):
        return (dot(dq_ref[...], wq[owner], 1, 1) + dot(dkv_ref[...], wkv[owner], 1, 1)).astype(
            jnp.bfloat16)

    def share(j, i):
        return pltpu.make_async_remote_copy(
            psend.at[j - 1, i], precv.at[j - 1, i], ps.at[j - 1, i], pr.at[j - 1, i],
            device_id=(me, (head + j) % n_head), device_id_type=MESH)

    for j in range(1, n_head):
        def send_chunk(i, carry):
            psend[j - 1, i] = partial(((head + j) % n_head) * chunks + i)
            share(j, i).start()
            return carry

        lax.fori_loop(0, chunks, send_chunk, 0)

    def own_chunk(i, carry):
        cols = pl.ds(pl.multiple_of(i * rows, 128), rows)
        grad_ref[:, cols] = partial(head * chunks + i)
        return carry

    lax.fori_loop(0, chunks, own_chunk, 0)

    def finish(i, carry):
        cols = pl.ds(pl.multiple_of(i * rows, 128), rows)
        total = grad_ref[:, cols].astype(jnp.float32)
        for j in range(1, n_head):
            share(j, i).wait_recv()
            total = total + precv[j - 1, i].astype(jnp.float32)
        grad_ref[:, cols] = total.astype(jnp.bfloat16)
        return carry

    lax.fori_loop(0, chunks, finish, 0)

    def drain(s, carry):
        for p in range(parts):
            for w in range(ways):
                @pl.when(s < m - 1)
                def _():
                    ring(p, w, s).wait_send()

                across(p, w, s, core).wait_send()
        return carry

    lax.fori_loop(0, m, drain, 0)
    for j in range(1, n_head):
        for u in units:
            relay(u, j).wait_send()

        def drain_share(i, carry):
            share(j, i).wait_send()
            return carry

        lax.fori_loop(0, chunks, drain_share, 0)


def pair_kernel(
    n_dp, group, capacity,
    src_ref, doc_hbm, cos_hbm, sin_hbm, x_hbm, old_hbm, fresh_hbm, k_hbm, v_hbm, g_hbm,
    out_ref, grad_ref,
    doc_ref, cos_ref, sin_ref, x_ref, own_ref, g_ref, wq, wkv, oq, okv, parcel, arrived, accq, acckv,
    dq_ref, dkv_ref, eq_ref, ekv_ref, psend, precv,
    in_sem, rs, rr, cs, cr, hs, hr, ys, yr, ts, tr, ds, dr, ps, pr,
):
    me, head = lax.axis_index("dp"), lax.axis_index("head")
    rows, hd = k_hbm.shape
    length = x_ref.shape[0]
    lanes, ways = 2, 2
    m = n_dp // lanes
    half = n_dp // 2
    core, chip = me % lanes, me // lanes
    side, level = chip % 2, chip // 2
    pos = (1 - side) * level + side * (m - 1 - level)
    piece = rows // ways
    kv_parts = [(0, first, piece // 4) for first in range(0, piece, piece // 4)]
    q_parts = [(1, first, piece // 2) for first in range(0, piece, piece // 2)]
    parts = kv_parts + q_parts
    kv_range, q_range = range(len(kv_parts)), range(len(kv_parts), len(parts))
    unit = rows // parcel.shape[0]
    lead = min(m // 2, m - 2)
    far = m // 2 + 1
    count = m - m // 4
    signs = (1, -1)
    bufs = (wkv, wq)
    others = (okv, oq)

    def index_of(p, lane):
        p = (p + 2 * m) % m
        far = p // (m // 2)
        return ((1 - far) * 2 * p + far * (2 * (m - 1 - p) + 1)) * lanes + lane

    right, left = index_of(pos + 1, core), index_of(pos - 1, core)
    targets = (right, left)
    partner = index_of(pos, 1 - core)
    across_y = (me, 1 - head)

    loads = [
        pltpu.make_async_copy(k_hbm, wkv.at[me, :, pl.ds(0, hd)], in_sem.at[0]),
        pltpu.make_async_copy(v_hbm, wkv.at[me, :, pl.ds(hd, hd)], in_sem.at[1]),
    ]
    loads += [
        pltpu.make_async_copy(old_hbm.at[:, pl.ds(c * hd, hd)], own_ref.at[c], in_sem.at[2 + c])
        for c in range(group - 1)
    ]
    loads += [
        pltpu.make_async_copy(fresh_hbm, own_ref.at[group - 1], in_sem.at[group + 1]),
        pltpu.make_async_copy(x_hbm, x_ref, in_sem.at[group + 2]),
        pltpu.make_async_copy(g_hbm, g_ref, in_sem.at[group + 3]),
        pltpu.make_async_copy(doc_hbm, doc_ref, in_sem.at[group + 4]),
        pltpu.make_async_copy(cos_hbm, cos_ref, in_sem.at[group + 5]),
        pltpu.make_async_copy(sin_hbm, sin_ref, in_sem.at[group + 6]),
    ]
    for load in loads:
        load.start()

    barrier = pltpu.get_barrier_semaphore()
    peers = [(right, head), (left, head), (partner, head), across_y]
    for peer in peers:
        pl.semaphore_signal(barrier, inc=1, device_id=peer, device_id_type=MESH)

    def remote(src, dst, send, recv, device):
        return pltpu.make_async_remote_copy(
            src, dst, send, recv, device_id=device, device_id_type=MESH)

    def part_of(p, w, owner):
        b, first, size = parts[p]
        return bufs[b].at[owner, pl.ds(w * piece + first, size)]

    def ring(p, w, s):
        ref = part_of(p, w, index_of(pos - signs[w] * s, core))
        return remote(ref, ref, rs.at[parts[p][0]], rr.at[p, s], (targets[w], head))

    def ring_in(p, s):
        b, _, size = parts[p]
        ref = bufs[b].at[me, pl.ds(0, ways * size)]
        return remote(ref, ref, rs.at[b], rr.at[p, s], (left, head))

    def across(p, w, s, lane):
        ref = part_of(p, w, index_of(pos - signs[w] * s, lane))
        return remote(ref, ref, cs.at[parts[p][0]], cr.at[parts[p][0], s], (partner, head))

    def across_in(b, s):
        ref = bufs[b].at[me]
        return remote(ref, ref, cs.at[b], cr.at[b, s], (partner, head))

    def forward(p, w, s, to):
        owner = index_of(pos - signs[w] * s, core)
        b, first, size = parts[p]
        dst = others[b].at[owner - to * half, pl.ds(w * piece + first, size)]
        return remote(part_of(p, w, owner), dst, ys.at[b], yr.at[b], across_y)

    def share(b, w, s, lane):
        owner = index_of(pos - signs[w] * s, lane)
        ref = others[b].at[owner - head * half, pl.ds(w * piece, piece)]
        return remote(ref, ref, ts.at[b], tr.at[b], (partner, head))

    def all_of(b, count, send, recv):
        ref = bufs[b].at[pl.ds(0, count), pl.ds(0, piece)]
        return remote(ref, ref, send.at[b], recv.at[b], across_y)

    def for_here(w, s):
        return index_of(pos - signs[w] * s, core) // half == head

    def last_forwarded(to):
        begin = (2 * to + 3) * (m // 4)
        steps = [[(signs[w] * (pos - begin - i) + 3 * m) % m for i in range(m // 2)] for w in range(ways)]
        limits = []
        for w in range(ways):
            limit = jnp.int32(-1)
            for s in steps[w]:
                later = sum([(t > s - (v > w)).astype(jnp.int32) for v in range(ways) for t in steps[v]], jnp.int32(0))
                limit = jnp.maximum(limit, jnp.where(later >= m // 4, s, -1))
            limits.append(limit)
        return limits

    limit_out, limit_in = last_forwarded(1 - head), last_forwarded(head)

    def forwarded(w, s):
        return jnp.logical_not(for_here(w, s)) & (s <= limit_out[w])

    def received(w, s):
        return for_here(w, s) & (s <= limit_in[w])

    def shared_out(w, s):
        return jnp.logical_not(for_here(w, s)) & (s > limit_out[w])

    def shared_in(w, s):
        return for_here(w, s) & (s > limit_in[w])

    def relay(u):
        return remote(parcel.at[u], arrived.at[u], hs.at[0], hr.at[0], across_y)

    def hand_on(p, w, s):
        @pl.when(forwarded(w, s))
        def _():
            forward(p, w, s, 1 - head).start()

    shift = [(2 - src_ref[k] // group) % 2 for k in range(group)]
    taken = [src_ref[k] % group for k in range(group)]
    slot = [
        sum([(shift[l] == 1).astype(jnp.int32) for l in range(k)], jnp.int32(0)) * shift[k]
        for k in range(group)
    ]
    units = range(parcel.shape[0])

    for load in loads[:2]:
        load.wait()
    pl.semaphore_wait(barrier, len(peers))
    for p in kv_range:
        for w in range(ways):
            ring(p, w, 0).start()
    for p in kv_range:
        for w in range(ways):
            across(p, w, 0, core).start()
    for load in loads[2:2 + group]:
        load.wait()
    for c in range(capacity):
        pick = sum([jnp.where((shift[k] == 1) & (slot[k] == c), taken[k], 0) for k in range(group)], jnp.int32(0))
        for u in units:
            parcel[u, c] = own_ref[pick, u * unit:(u + 1) * unit]
    for u in units:
        relay(u).start()
    for p in kv_range:
        for w in range(ways):
            hand_on(p, w, 0)
    for load in loads[2 + group:]:
        load.wait()

    def add(b, places):
        acc = (acckv, accq)[b]
        total = acc[...]
        for w, owner in places:
            xs = x_ref[:, pl.ds(pl.multiple_of(owner * rows + w * piece, 128), piece)]
            total = total + dot(xs, bufs[b][owner, pl.ds(w * piece, piece), :], 1, 0)
        acc[...] = total

    def pass_on(p, s):
        ring_in(p, s - 1).wait_recv()

        @pl.when(s < m - 1)
        def _():
            for w in range(ways):
                ring(p, w, s).start()

        for w in range(ways):
            across(p, w, s, core).start()
            hand_on(p, w, s)

    accq[...] = jnp.zeros_like(accq)
    acckv[...] = jnp.zeros_like(acckv)
    add(0, [(w, me) for w in range(ways)])
    for s in range(1, lead + 1):
        for p in kv_range:
            pass_on(p, s)
        if s == lead - 1:
            remote(parcel, arrived, hs.at[0], hr.at[0], across_y).wait_recv()
            for u in units:
                block = slice(u * unit, (u + 1) * unit)
                for k in range(group):
                    wq[me, block, k * hd:(k + 1) * hd] = jnp.where(
                        shift[k] == 0, own_ref[taken[k], block], arrived[u, slot[k]])
            for p in q_range:
                for w in range(ways):
                    ring(p, w, 0).start()
            for p in q_range:
                for w in range(ways):
                    across(p, w, 0, core).start()
                    hand_on(p, w, 0)
    add(1, [(w, me) for w in range(ways)])

    def step(s, carry):
        @pl.when(s + lead < m)
        def _():
            for p in kv_range:
                pass_on(p, s + lead)

        for p in q_range:
            pass_on(p, s)
        for b in range(2):
            across_in(b, s - 1).wait_recv()
        places = [(w, index_of(pos - signs[w] * s, core)) for w in range(ways)]
        places += [(w, index_of(pos - signs[w] * (s - 1), 1 - core)) for w in range(ways)]
        for b in range(2):
            add(b, places)
        return carry

    lax.fori_loop(1, m, step, 0)
    for b in range(2):
        across_in(b, m - 1).wait_recv()
        add(b, [(w, index_of(pos - signs[w] * (m - 1), 1 - core)) for w in range(ways)])

    scale = 1.0 / math.sqrt(hd)
    cosine, sine = cos_ref[...], sin_ref[...]

    def rotate(f):
        return f * cosine + pltpu.roll(f, hd // 2, 1) * sine

    def rotate_back(f):
        return f * cosine - pltpu.roll(f, hd // 2, 1) * sine

    def swap_q(k):
        cols = pl.ds(k * hd, hd)
        return remote(dq_ref.at[:, cols], eq_ref.at[:, cols], ds.at[0], dr.at[0], across_y)

    swap_kv = remote(dkv_ref, ekv_ref, ds.at[1], dr.at[1], across_y)
    swap_all_q = remote(dq_ref, eq_ref, ds.at[0], dr.at[0], across_y)

    docs = jnp.broadcast_to(doc_ref[...].astype(jnp.float32), (length, length))
    at_key = lax.broadcasted_iota(jnp.int32, (length, length), 1)
    at_query = lax.broadcasted_iota(jnp.int32, (length, length), 0)
    allowed = (at_key <= at_query) & (docs == docs.T)
    key = rotate(acckv[:, :hd]).astype(jnp.bfloat16)
    value = acckv[:, hd:].astype(jnp.bfloat16)
    dkey = jnp.zeros((length, hd), jnp.float32)
    dvalue = jnp.zeros((length, hd), jnp.float32)
    for k in range(group):
        cols = slice(k * hd, (k + 1) * hd)
        query = rotate(accq[:, cols]).astype(jnp.bfloat16)
        given = g_ref[:, cols]
        scores = jnp.where(allowed, dot(query, key, 1, 1) * scale, neg_large)
        weights = jnp.exp(scores - jnp.max(scores, axis=-1, keepdims=True))
        probs = weights / jnp.sum(weights, axis=-1, keepdims=True)
        probs_b = probs.astype(jnp.bfloat16)
        out_ref[:, cols] = dot(probs_b, value, 1, 0).astype(jnp.bfloat16)
        prob_grad = dot(given, value, 1, 1)
        centre = jnp.sum(probs * prob_grad, axis=-1, keepdims=True)
        dscore = (probs * (prob_grad - centre) * scale).astype(jnp.bfloat16)
        dq_ref[:, cols] = rotate_back(dot(dscore, key, 1, 0)).astype(jnp.bfloat16)
        swap_q(k).start()
        dkey = dkey + dot(dscore, query, 0, 0)
        dvalue = dvalue + dot(probs_b, given, 0, 0)
    dkv_ref[:, :hd] = rotate_back(dkey).astype(jnp.bfloat16)
    dkv_ref[:, hd:] = dvalue.astype(jnp.bfloat16)
    swap_kv.start()

    def partial(owner, w):
        block = pl.ds(w * piece, piece)
        return (dot(dq_ref[...], wq[owner, block, :], 1, 1)
                + dot(dkv_ref[...], wkv[owner, block, :], 1, 1)).astype(jnp.bfloat16)

    def partial_other(place, w):
        block = pl.ds(w * piece, piece)
        return (dot(eq_ref[...], oq[place, block, :], 1, 1)
                + dot(ekv_ref[...], okv[place, block, :], 1, 1)).astype(jnp.bfloat16)

    def send_share(w, s, lane):
        at = (w, s - far, lane)
        return remote(psend.at[at], precv.at[at], ps.at[0], pr.at[at], across_y)

    def each_step(body, first=0):
        def loop(s, carry):
            for w in range(ways):
                body(w, s)
            return carry

        lax.fori_loop(first, m, loop, 0)

    def send_far(w, s):
        @pl.when(shared_out(w, s))
        def _():
            for lane in range(lanes):
                psend[w, s - far, lane] = partial(index_of(pos - signs[w] * s, lane), w)
                send_share(w, s, lane).start()

    each_step(send_far, far)

    for b in range(2):
        all_of(b, count, ys, yr).wait_recv()

    def share_near(w, s):
        @pl.when(received(w, s))
        def _():
            for b in range(2):
                share(b, w, s, core).start()

    each_step(share_near)

    def columns(owner, w):
        return pl.ds(pl.multiple_of((owner - head * half) * rows + w * piece, 128), piece)

    def own_part(i, carry):
        owner = head * half + i
        for w in range(ways):
            grad_ref[:, columns(owner, w)] = partial(owner, w)
        return carry

    lax.fori_loop(0, half, own_part, 0)

    swap_all_q.wait_recv()
    swap_kv.wait_recv()
    for b in range(2):
        all_of(b, count, ts, tr).wait_recv()

    def plus(owner, w, value):
        cols = columns(owner, w)
        grad_ref[:, cols] = (grad_ref[:, cols].astype(jnp.float32) + value.astype(jnp.float32)).astype(jnp.bfloat16)

    def add_near(w, s):
        @pl.when(received(w, s))
        def _():
            for lane in range(lanes):
                owner = index_of(pos - signs[w] * s, lane)
                plus(owner, w, partial_other(owner - head * half, w))

    each_step(add_near)

    def add_far(w, s):
        @pl.when(shared_in(w, s))
        def _():
            for lane in range(lanes):
                send_share(w, s, lane).wait_recv()
                plus(index_of(pos - signs[w] * s, lane), w, precv[w, s - far, lane])

    each_step(add_far, far)

    for b in range(2):
        for number, sent in ((ways * (m - 1), rs), (ways * m, cs), (count, ys), (count, ts)):
            all_of(b, number, sent, sent).wait_send()
    remote(parcel, arrived, hs.at[0], hr.at[0], across_y).wait_send()
    swap_all_q.wait_send()
    swap_kv.wait_send()
    ref = psend.at[:, pl.ds(0, m // 8)]
    remote(ref, ref, ps.at[0], ps.at[0], across_y).wait_send()


def pair_call(n_dp, x, old, fresh, wk, wv, g, head_source, doc_ids):
    length, width = x.shape
    rows, hd = wk.shape
    group = g.shape[1] // hd
    m, half, ways, units, parts = n_dp // 2, n_dp // 2, 2, 4, 6
    capacity = (group + 1) // 2
    cosine, sine = rotary_tables(length, hd)
    bf, f32 = jnp.bfloat16, jnp.float32
    vm = pl.BlockSpec(memory_space=pltpu.VMEM)
    anyspace = pl.BlockSpec(memory_space=pl.ANY)
    dma = pltpu.SemaphoreType.DMA
    unit = rows // units
    far = (ways, m - 1 - m // 2, 2)
    return pl.pallas_call(
        functools.partial(pair_kernel, n_dp, group, capacity),
        out_shape=(
            pltpu.VMEM((length, group * hd), bf),
            pltpu.VMEM((length, width // 2), bf),
        ),
        in_specs=[pl.BlockSpec(memory_space=pltpu.SMEM)] + [anyspace] * 9,
        out_specs=(vm, vm),
        scratch_shapes=[
            pltpu.VMEM((1, length), jnp.int32),
            pltpu.VMEM((length, hd), f32),
            pltpu.VMEM((length, hd), f32),
            pltpu.VMEM((length, width), bf),
            pltpu.VMEM((group, rows, hd), bf),
            pltpu.VMEM((length, group * hd), bf),
            pltpu.VMEM((n_dp, rows, group * hd), bf),
            pltpu.VMEM((n_dp, rows, 2 * hd), bf),
            pltpu.VMEM((half, rows, group * hd), bf),
            pltpu.VMEM((half, rows, 2 * hd), bf),
            pltpu.VMEM((units, capacity, unit, hd), bf),
            pltpu.VMEM((units, capacity, unit, hd), bf),
            pltpu.VMEM((length, group * hd), f32),
            pltpu.VMEM((length, 2 * hd), f32),
            pltpu.VMEM((length, group * hd), bf),
            pltpu.VMEM((length, 2 * hd), bf),
            pltpu.VMEM((length, group * hd), bf),
            pltpu.VMEM((length, 2 * hd), bf),
            pltpu.VMEM(far + (length, rows // ways), bf),
            pltpu.VMEM(far + (length, rows // ways), bf),
            dma((group + 7,)),
            dma((2,)),
            dma((parts, m)),
            dma((2,)),
            dma((2, m)),
            dma((1,)),
            dma((1,)),
            dma((2,)),
            dma((2,)),
            dma((2,)),
            dma((2,)),
            dma((2,)),
            dma((2,)),
            dma((1,)),
            dma(far),
        ],
        compiler_params=pltpu.CompilerParams(
            collective_id=0, has_side_effects=True, vmem_limit_bytes=48*1024*1024),
    )(*(pltpu.with_memory_space_constraint(jnp.asarray(a), pltpu.HBM) for a in (
        head_source, doc_ids.reshape(1, -1), cosine, sine, x, old, fresh, wk, wv, g)))


def solution(mesh):
    n_dp, n_head = mesh.shape["dp"], mesh.shape["head"]

    def local(x, old, fresh, wk, wv, g, head_source, doc_ids):
        length, width = x.shape
        rows, hd = wk.shape
        group = g.shape[1] // hd
        ways = 2 if rows % 256 == 0 else 1
        m = n_dp // 2
        if n_head == 2 and rows % 512 == 0 and m % 8 == 0:
            return pair_call(n_dp, x, old, fresh, wk, wv, g, head_source, doc_ids)
        capacity = (group + n_head - 1) // n_head
        chunks = n_dp // n_head
        cosine, sine = rotary_tables(length, hd)
        bf, f32 = jnp.bfloat16, jnp.float32
        vm = pl.BlockSpec(memory_space=pltpu.VMEM)
        anyspace = pl.BlockSpec(memory_space=pl.ANY)
        dma = pltpu.SemaphoreType.DMA
        return pl.pallas_call(
            functools.partial(kernel, n_dp, n_head, group, ways),
            out_shape=(
                jax.ShapeDtypeStruct((length, group * hd), bf),
                jax.ShapeDtypeStruct((length, width // n_head), bf),
            ),
            in_specs=[pl.BlockSpec(memory_space=pltpu.SMEM)] + [anyspace] * 9,
            out_specs=(vm, vm),
            scratch_shapes=[
                pltpu.VMEM((1, length), jnp.int32),
                pltpu.VMEM((length, hd), f32),
                pltpu.VMEM((length, hd), f32),
                pltpu.VMEM((length, width), bf),
                pltpu.VMEM((rows, group * hd), bf),
                pltpu.VMEM((length, group * hd), bf),
                pltpu.VMEM((n_dp, rows, group * hd), bf),
                pltpu.VMEM((n_dp, rows, 2 * hd), bf),
                pltpu.VMEM((2 * ways, n_head - 1, capacity, rows // (2 * ways), hd), bf),
                pltpu.VMEM((2 * ways, n_head - 1, capacity, rows // (2 * ways), hd), bf),
                pltpu.VMEM((length, group * hd), f32),
                pltpu.VMEM((length, 2 * hd), f32),
                pltpu.VMEM((length, group * hd), bf),
                pltpu.VMEM((length, 2 * hd), bf),
                pltpu.VMEM((n_head - 1, chunks, length, rows), bf),
                pltpu.VMEM((n_head - 1, chunks, length, rows), bf),
                dma((9,)),
                dma((3 * ways, m)),
                dma((3 * ways, m)),
                dma((3 * ways, m)),
                dma((3 * ways, m)),
                dma((2 * ways, n_head - 1)),
                dma((2 * ways, n_head - 1)),
                dma((n_head - 1, chunks)),
                dma((n_head - 1, chunks)),
            ],
            compiler_params=pltpu.CompilerParams(
                collective_id=0, has_side_effects=True, vmem_limit_bytes=67043328),
        )(head_source, doc_ids.reshape(1, -1), cosine, sine, x, old, fresh, wk, wv, g)

    in_specs = (
        P("dp", None), P("dp", "head"), P("dp", "head"), P("dp", "head"),
        P("dp", "head"), P("dp", "head"), P(), P("dp"),
    )
    return jax.shard_map(
        local, mesh=mesh, in_specs=in_specs,
        out_specs=(P("dp", "head"), P("dp", "head")), check_vma=False)
```

```python
import functools
import math

import jax
import jax.numpy as jnp
import numpy as np
from jax import lax
from jax.experimental import pallas as pl
from jax.experimental.pallas import tpu as pltpu
from jax.sharding import PartitionSpec as P

theta_base = 500000.0
neg_large = -1e30
MESH = pl.DeviceIdType.MESH


def rotary_tables(length, width):
    half = width // 2
    frequency = theta_base ** (-2.0 * np.arange(half, dtype=np.float64) / width)
    angles = np.arange(length, dtype=np.float64)[:, None] * frequency[None, :]
    cosine, sine = np.cos(angles), np.sin(angles)
    return (
        np.concatenate([cosine, cosine], axis=1).astype(np.float32),
        np.concatenate([-sine, sine], axis=1).astype(np.float32),
    )


def dot(a, b, ca, cb):
    return lax.dot_general(
        a, b, (((ca,), (cb,)), ((), ())), preferred_element_type=jnp.float32
    )


def kernel(
    n_dp, n_head, group, ways,
    src_ref, doc_hbm, cos_hbm, sin_hbm, x_hbm, old_hbm, fresh_hbm, k_hbm, v_hbm, g_hbm,
    out_ref, grad_ref,
    doc_ref, cos_ref, sin_ref, x_ref, own_ref, g_ref, wq, wkv, parcel, arrived, accq, acckv, dq_ref, dkv_ref,
    psend, precv,
    in_sem, rs, rr, cs, cr, hs, hr, ps, pr,
):
    me, head = lax.axis_index("dp"), lax.axis_index("head")
    rows, hd = k_hbm.shape
    length = x_ref.shape[0]
    lanes = 2
    m = n_dp // lanes
    core, chip = me % lanes, me // lanes
    side, level = chip % 2, chip // 2
    pos = (1 - side) * level + side * (m - 1 - level)
    piece = rows // ways
    sub = piece // 2
    lead = min(2, m - 2)
    parts = 3
    capacity = parcel.shape[2]
    signs = (1, -1)[:ways]
    bufs = (wkv, wq)
    spans = ((0, piece), (0, sub), (sub, sub))

    def index_of(p, lane):
        p = (p + 2 * m) % m
        far = p // (m // 2)
        return ((1 - far) * 2 * p + far * (2 * (m - 1 - p) + 1)) * lanes + lane

    right, left = index_of(pos + 1, core), index_of(pos - 1, core)
    targets = (right, left)[:ways]
    partner = index_of(pos, 1 - core)

    loads = [
        pltpu.make_async_copy(k_hbm, wkv.at[me, :, pl.ds(0, hd)], in_sem.at[0]),
        pltpu.make_async_copy(v_hbm, wkv.at[me, :, pl.ds(hd, hd)], in_sem.at[1]),
        pltpu.make_async_copy(old_hbm, own_ref.at[:, pl.ds(0, (group - 1) * hd)], in_sem.at[2]),
        pltpu.make_async_copy(fresh_hbm, own_ref.at[:, pl.ds((group - 1) * hd, hd)], in_sem.at[3]),
        pltpu.make_async_copy(x_hbm, x_ref, in_sem.at[4]),
        pltpu.make_async_copy(g_hbm, g_ref, in_sem.at[5]),
        pltpu.make_async_copy(doc_hbm, doc_ref, in_sem.at[6]),
        pltpu.make_async_copy(cos_hbm, cos_ref, in_sem.at[7]),
        pltpu.make_async_copy(sin_hbm, sin_ref, in_sem.at[8]),
    ]
    for load in loads:
        load.start()

    barrier = pltpu.get_barrier_semaphore()
    peers = [(right, head), (left, head), (partner, head)]
    peers += [(me, (head + j) % n_head) for j in range(1, n_head)]
    for peer in peers:
        pl.semaphore_signal(barrier, inc=1, device_id=peer, device_id_type=MESH)

    def part_of(p, w, owner):
        first, count = spans[p]
        return bufs[min(p, 1)].at[owner, pl.ds(w * piece + first, count)]

    def ring(p, w, s):
        ref = part_of(p, w, index_of(pos - signs[w] * s, core))
        return pltpu.make_async_remote_copy(
            ref, ref, rs.at[w * parts + p, s], rr.at[w * parts + p, s],
            device_id=(targets[w], head), device_id_type=MESH)

    def ring_in(p, w, s):
        ref = part_of(p, w, index_of(pos - signs[w] * (s + 1), core))
        return pltpu.make_async_remote_copy(
            ref, ref, rs.at[w * parts + p, s], rr.at[w * parts + p, s],
            device_id=(targets[w], head), device_id_type=MESH)

    def across(p, w, s, lane):
        ref = part_of(p, w, index_of(pos - signs[w] * s, lane))
        return pltpu.make_async_remote_copy(
            ref, ref, cs.at[w * parts + p, s], cr.at[w * parts + p, s],
            device_id=(partner, head), device_id_type=MESH)

    def relay(u, j):
        return pltpu.make_async_remote_copy(
            parcel.at[u, j - 1], arrived.at[u, j - 1], hs.at[u, j - 1], hr.at[u, j - 1],
            device_id=(me, (head + j) % n_head), device_id_type=MESH)

    shift = [(n_head - src_ref[k] // group) % n_head for k in range(group)]
    taken = [src_ref[k] % group for k in range(group)]
    slot = [
        sum([(shift[l] == shift[k]).astype(jnp.int32) for l in range(k)], jnp.int32(0))
        for k in range(group)
    ]

    def flag(cond):
        return jnp.where(cond, 1.0, 0.0).astype(jnp.float32)

    units = [w * 2 + half for half in range(2) for w in range(ways)]

    def weigh(u, weights):
        total = jnp.zeros((sub, hd), jnp.float32)
        for c_m in range(group):
            block = own_ref[u * sub:(u + 1) * sub, c_m * hd:(c_m + 1) * hd]
            total = total + block.astype(jnp.float32) * weights[c_m]
        return total.astype(jnp.bfloat16)

    for load in loads[:2]:
        load.wait()
    pl.semaphore_wait(barrier, len(peers))
    for w in range(ways):
        ring(0, w, 0).start()
    for w in range(ways):
        across(0, w, 0, core).start()
    for load in loads[2:4]:
        load.wait()
    for u in units:
        for j in range(1, n_head):
            for c in range(capacity):
                weights = [
                    sum([flag((shift[k] == j) & (slot[k] == c) & (taken[k] == c_m))
                         for k in range(group)], jnp.float32(0))
                    for c_m in range(group)
                ]
                parcel[u, j - 1, c] = weigh(u, weights)
            relay(u, j).start()
    for k in range(group):
        weights = [flag((shift[k] == 0) & (taken[k] == c_m)) for c_m in range(group)]
        for u in units:
            wq[me, u * sub:(u + 1) * sub, k * hd:(k + 1) * hd] = weigh(u, weights)
    for load in loads[4:]:
        load.wait()
    accq[...] = jnp.zeros_like(accq)
    acckv[...] = jnp.zeros_like(acckv)

    def add(p, w, owner):
        xs = x_ref[:, pl.ds(pl.multiple_of(owner * rows + w * piece, 128), piece)]
        acc = (acckv, accq)[p]
        acc[...] += dot(xs, bufs[p][owner, pl.ds(w * piece, piece), :], 1, 0)

    def pass_on(p, w, s):
        ring_in(p, w, s - 1).wait_recv()

        @pl.when(s < m - 1)
        def _():
            ring(p, w, s).start()

        across(p, w, s, core).start()

    def unit_out(u):
        block = pl.ds(u * sub, sub)
        for j in range(1, n_head):
            relay(u, j).wait_recv()
        for k in range(group):
            cols = slice(k * hd, (k + 1) * hd)
            total = wq[me, block, cols].astype(jnp.float32)
            for j in range(1, n_head):
                for c in range(capacity):
                    weight = flag((shift[k] == j) & (slot[k] == c))
                    total = total + arrived[u, j - 1, c].astype(jnp.float32) * weight
            wq[me, block, cols] = total.astype(jnp.bfloat16)
        ring(1 + u % 2, u // 2, 0).start()
        across(1 + u % 2, u // 2, 0, core).start()

    for w in range(ways):
        add(0, w, me)
    for u in units[:ways]:
        unit_out(u)
    for s in range(1, lead + 1):
        for w in range(ways):
            pass_on(0, w, s)
        if s == 1:
            for u in units[ways:]:
                unit_out(u)
    for w in range(ways):
        add(1, w, me)

    def step(s, carry):
        @pl.when(s + lead < m)
        def _():
            for w in range(ways):
                pass_on(0, w, s + lead)

        for p in range(1, parts):
            for w in range(ways):
                pass_on(p, w, s)
        for w in range(ways):
            for p in range(2):
                add(p, w, index_of(pos - signs[w] * s, core))
        for w in range(ways):
            for p in range(parts):
                across(p, w, s - 1, 1 - core).wait_recv()
        for w in range(ways):
            for p in range(2):
                add(p, w, index_of(pos - signs[w] * (s - 1), 1 - core))
        return carry

    lax.fori_loop(1, m, step, 0)
    for w in range(ways):
        for p in range(parts):
            across(p, w, m - 1, 1 - core).wait_recv()
        for p in range(2):
            add(p, w, index_of(pos - signs[w] * (m - 1), 1 - core))

    scale = 1.0 / math.sqrt(hd)
    cosine, sine = cos_ref[...], sin_ref[...]

    def rotate(f):
        return f * cosine + pltpu.roll(f, hd // 2, 1) * sine

    def rotate_back(f):
        return f * cosine - pltpu.roll(f, hd // 2, 1) * sine

    docs = jnp.broadcast_to(doc_ref[...].astype(jnp.float32), (length, length))
    at_key = lax.broadcasted_iota(jnp.int32, (length, length), 1)
    at_query = lax.broadcasted_iota(jnp.int32, (length, length), 0)
    allowed = (at_key <= at_query) & (docs == docs.T)
    key = rotate(acckv[:, :hd]).astype(jnp.bfloat16)
    value = acckv[:, hd:].astype(jnp.bfloat16)
    dkey = jnp.zeros((length, hd), jnp.float32)
    dvalue = jnp.zeros((length, hd), jnp.float32)
    for k in range(group):
        cols = slice(k * hd, (k + 1) * hd)
        query = rotate(accq[:, cols]).astype(jnp.bfloat16)
        given = g_ref[:, cols]
        scores = jnp.where(allowed, dot(query, key, 1, 1) * scale, neg_large)
        weights = jnp.exp(scores - jnp.max(scores, axis=-1, keepdims=True))
        probs = weights / jnp.sum(weights, axis=-1, keepdims=True)
        probs_b = probs.astype(jnp.bfloat16)
        out_ref[:, cols] = dot(probs_b, value, 1, 0).astype(jnp.bfloat16)
        prob_grad = dot(given, value, 1, 1)
        centre = jnp.sum(probs * prob_grad, axis=-1, keepdims=True)
        dscore = (probs * (prob_grad - centre) * scale).astype(jnp.bfloat16)
        dq_ref[:, cols] = rotate_back(dot(dscore, key, 1, 0)).astype(jnp.bfloat16)
        dkey = dkey + dot(dscore, query, 0, 0)
        dvalue = dvalue + dot(probs_b, given, 0, 0)
    dkv_ref[:, :hd] = rotate_back(dkey).astype(jnp.bfloat16)
    dkv_ref[:, hd:] = dvalue.astype(jnp.bfloat16)

    chunks = n_dp // n_head

    def partial(owner):
        return (dot(dq_ref[...], wq[owner], 1, 1) + dot(dkv_ref[...], wkv[owner], 1, 1)).astype(
            jnp.bfloat16)

    def share(j, i):
        return pltpu.make_async_remote_copy(
            psend.at[j - 1, i], precv.at[j - 1, i], ps.at[j - 1, i], pr.at[j - 1, i],
            device_id=(me, (head + j) % n_head), device_id_type=MESH)

    for j in range(1, n_head):
        def send_chunk(i, carry):
            psend[j - 1, i] = partial(((head + j) % n_head) * chunks + i)
            share(j, i).start()
            return carry

        lax.fori_loop(0, chunks, send_chunk, 0)

    def own_chunk(i, carry):
        cols = pl.ds(pl.multiple_of(i * rows, 128), rows)
        grad_ref[:, cols] = partial(head * chunks + i)
        return carry

    lax.fori_loop(0, chunks, own_chunk, 0)

    def finish(i, carry):
        cols = pl.ds(pl.multiple_of(i * rows, 128), rows)
        total = grad_ref[:, cols].astype(jnp.float32)
        for j in range(1, n_head):
            share(j, i).wait_recv()
            total = total + precv[j - 1, i].astype(jnp.float32)
        grad_ref[:, cols] = total.astype(jnp.bfloat16)
        return carry

    lax.fori_loop(0, chunks, finish, 0)

    def drain(s, carry):
        for p in range(parts):
            for w in range(ways):
                @pl.when(s < m - 1)
                def _():
                    ring(p, w, s).wait_send()

                across(p, w, s, core).wait_send()
        return carry

    lax.fori_loop(0, m, drain, 0)
    for j in range(1, n_head):
        for u in units:
            relay(u, j).wait_send()

        def drain_share(i, carry):
            share(j, i).wait_send()
            return carry

        lax.fori_loop(0, chunks, drain_share, 0)


def pair_kernel(
    n_dp, group, capacity,
    src_ref, doc_hbm, cos_hbm, sin_hbm, x_hbm, old_hbm, fresh_hbm, k_hbm, v_hbm, g_hbm,
    out_ref, grad_ref,
    doc_ref, cos_ref, sin_ref, x_ref, own_ref, g_ref, wkv, wqa, wqb, okv, oqa, oqb, parcel, arrived_0, arrived_1, arrived_2, arrived_3, accq, acckv,
    dq_ref, dkv_ref, eq_ref, ekv_ref, psend, precv,
    in_sem, rs, rr, cs, cr, hs, hr, ys, yr, ts, tr, ds, dr, ps, pr,
):
    me, head = lax.axis_index("dp"), lax.axis_index("head")
    rows, hd = k_hbm.shape
    length = x_ref.shape[0]
    lanes, ways = 2, 2
    m = n_dp // lanes
    half = n_dp // 2
    core, chip = me % lanes, me // lanes
    side, level = chip % 2, chip // 2
    pos = (1 - side) * level + side * (m - 1 - level)
    piece = rows // ways
    kv_parts = [(0, first, piece // 4) for first in range(0, piece, piece // 4)]
    qa_parts = [(1, first, piece // 2) for first in range(0, piece, piece // 2)]
    qb_parts = [(2, first, piece // 2) for first in range(0, piece, piece // 2)]
    parts = kv_parts + qa_parts + qb_parts
    kv_range = range(len(kv_parts))
    qa_range = range(len(kv_parts), len(kv_parts) + len(qa_parts))
    qb_range = range(len(kv_parts) + len(qa_parts), len(parts))
    unit = rows // parcel.shape[0]
    lead = 3
    count = m - m // 4
    signs = (1, -1)
    arrived = (arrived_0, arrived_1, arrived_2, arrived_3)
    lag = 1
    bufs = (wkv, wqa, wqb)
    others = (okv, oqa, oqb)
    first_heads = wqa.shape[2] // hd
    width_a = wqa.shape[2]

    def index_of(p, lane):
        p = jnp.where(p < 0, p + m, p)
        p = jnp.where(p >= m, p - m, p)
        return jnp.where(p < m // 2, 2 * p, 2 * (m - 1 - p) + 1) * lanes + lane

    right, left = index_of(pos + 1, core), index_of(pos - 1, core)
    targets = (right, left)
    partner = index_of(pos, 1 - core)
    across_y = (me, 1 - head)

    loads = [
        pltpu.make_async_copy(k_hbm, wkv.at[me, :, pl.ds(0, hd)], in_sem.at[0]),
        pltpu.make_async_copy(v_hbm, wkv.at[me, :, pl.ds(hd, hd)], in_sem.at[1]),
    ]
    loads += [
        pltpu.make_async_copy(old_hbm.at[:, pl.ds(c * hd, hd)], own_ref.at[c], in_sem.at[2 + c])
        for c in range(group - 1)
    ]
    loads += [
        pltpu.make_async_copy(fresh_hbm, own_ref.at[group - 1], in_sem.at[group + 1]),
        pltpu.make_async_copy(x_hbm, x_ref, in_sem.at[group + 2]),
        pltpu.make_async_copy(g_hbm, g_ref, in_sem.at[group + 3]),
        pltpu.make_async_copy(doc_hbm, doc_ref, in_sem.at[group + 4]),
        pltpu.make_async_copy(cos_hbm, cos_ref, in_sem.at[group + 5]),
        pltpu.make_async_copy(sin_hbm, sin_ref, in_sem.at[group + 6]),
    ]
    for load in loads:
        load.start()

    barrier = pltpu.get_barrier_semaphore()
    peers = [(right, head), (left, head), (partner, head), across_y]
    for peer in peers:
        pl.semaphore_signal(barrier, inc=1, device_id=peer, device_id_type=MESH)

    def remote(src, dst, send, recv, device):
        return pltpu.make_async_remote_copy(
            src, dst, send, recv, device_id=device, device_id_type=MESH)

    def part_of(p, w, owner):
        b, first, size = parts[p]
        return bufs[b].at[owner, pl.ds(w * piece + first, size)]

    def ring(p, w, s, owner):
        ref = part_of(p, w, owner)
        return remote(ref, ref, rs.at[parts[p][0]], rr.at[p, s], (targets[w], head))

    def ring_in(p, s):
        b, _, size = parts[p]
        ref = bufs[b].at[me, pl.ds(0, ways * size)]
        return remote(ref, ref, rs.at[b], rr.at[p, s], (left, head))

    def across(p, w, s, owner):
        ref = part_of(p, w, owner)
        return remote(ref, ref, cs.at[parts[p][0]], cr.at[parts[p][0], s], (partner, head))

    def across_in(b, s):
        ref = bufs[b].at[me]
        return remote(ref, ref, cs.at[b], cr.at[b, s], (partner, head))

    def forward(p, w, owner):
        b, first, size = parts[p]
        dst = others[b].at[owner - (1 - head) * half, pl.ds(w * piece + first, size)]
        return remote(part_of(p, w, owner), dst, ys.at[b], yr.at[b], across_y)

    def owner_at(w, s, lane):
        return index_of(pos - (1 - 2 * w) * s, lane)

    def share(b, w, s):
        ref = others[b].at[owner_at(w, s, core) - head * half, pl.ds(pl.multiple_of(w * piece, piece), piece)]
        return remote(ref, ref, ts.at[b], tr.at[b], (partner, head))

    def all_of(b, count, send, recv):
        ref = bufs[b].at[pl.ds(0, count), pl.ds(0, piece)]
        return remote(ref, ref, send.at[b], recv.at[b], across_y)

    def for_here(w, s):
        return (index_of(pos - signs[w] * s, 0) >= half) == (head == 1)

    def relay(u):
        return remote(parcel.at[u], arrived[u], hs.at[0], hr.at[u], across_y)

    shift = [(2 - src_ref[k] // group) % 2 for k in range(group)]
    taken = [src_ref[k] % group for k in range(group)]
    slot = [
        sum([(shift[l] == 1).astype(jnp.int32) for l in range(k)], jnp.int32(0)) * shift[k]
        for k in range(group)
    ]
    units = [w * 2 + late for late in range(2) for w in range(ways)]

    for load in loads[:2]:
        load.wait()
    pl.semaphore_wait(barrier, len(peers))
    for p in kv_range:
        for w in range(ways):
            ring(p, w, 0, me).start()
    for p in kv_range:
        for w in range(ways):
            across(p, w, 0, me).start()
    for load in loads[2:2 + group]:
        load.wait()
    for c in range(capacity):
        pick = sum([jnp.where((shift[k] == 1) & (slot[k] == c), taken[k], 0) for k in range(group)], jnp.int32(0))
        for u in units:
            parcel[u, c] = own_ref[pick, u * unit:(u + 1) * unit]
    for u in units:
        relay(u).start()
    def by_arrival(to):
        begin = (2 * to + 3) * (m // 4)
        places = [(w, lax.rem(signs[w] * (pos - begin - i) + 3 * m, m)) for w in range(ways) for i in range(m // 2)]
        later = [
            sum([jnp.where(t > s - (v > w), 1, 0) for v, t in places], jnp.int32(0)) for w, s in places
        ]
        order = []
        for r in range(m):
            order.append((
                sum([jnp.where(late == r, w, 0) for late, (w, _) in zip(later, places)], jnp.int32(0)),
                sum([jnp.where(late == r, s, 0) for late, (_, s) in zip(later, places)], jnp.int32(0)),
            ))
        limits = [jnp.int32(-1)] * ways
        for late, (w, s) in zip(later, places):
            limits[w] = jnp.maximum(limits[w], jnp.where(late >= m // 4, s, -1))
        return order, limits

    (order_out, limit_out), (order_in, _) = by_arrival(1 - head), by_arrival(head)
    far_out, far_in, near_in = order_out[:m // 4], order_in[:m // 4], order_in[m // 4:]

    def forwarded(w, s):
        return jnp.logical_not(for_here(w, s)) & (s <= limit_out[w])

    def hand_on(some, w, owner, wanted):
        @pl.when(wanted)
        def _():
            for p in some:
                forward(p, w, owner).start()

    for w in range(ways):
        hand_on(kv_range, w, me, forwarded(w, 0))
    for load in loads[2 + group:]:
        load.wait()

    accs = (acckv, accq.at[:, pl.ds(0, width_a)], accq.at[:, pl.ds(width_a, group * hd - width_a)])

    def add(b, s):
        across_in(b, s).wait_recv()
        total = accs[b][...]
        for lane in range(lanes):
            for w in range(ways):
                owner = index_of(pos - signs[w] * s, lane)
                xs = x_ref[:, pl.ds(pl.multiple_of(owner * rows + w * piece, 128), piece)]
                total = total + dot(xs, bufs[b][owner, pl.ds(w * piece, piece), :], 1, 0)
        accs[b][...] = total

    def begin(some, w):
        for p in some:
            ring(p, w, 0, me).start()
        for p in some:
            across(p, w, 0, me).start()
        hand_on(some, w, me, forwarded(w, 0))

    def pass_on(some, s):
        owners = [index_of(pos - signs[w] * s, core) for w in range(ways)]
        wanted = [forwarded(w, s) for w in range(ways)]
        for p in some:
            ring_in(p, s - 1).wait_recv()

            @pl.when(s < m - 1)
            def _():
                for w in range(ways):
                    ring(p, w, s, owners[w]).start()

            for w in range(ways):
                across(p, w, s, owners[w]).start()
                hand_on([p], w, owners[w], wanted[w])

    accq[...] = jnp.zeros_like(accq)
    acckv[...] = jnp.zeros_like(acckv)
    add(0, 0)

    def assemble(u):
        relay(u).wait_recv()
        block = slice(u * unit, (u + 1) * unit)
        for k in range(group):
            b, at = (1, k) if k < first_heads else (2, k - first_heads)
            bufs[b][me, block, at * hd:(at + 1) * hd] = jnp.where(
                shift[k] == 0, own_ref[taken[k], block], arrived[u][slot[k]])
        begin([qa_range[u % 2]], u // 2)

    pass_on(kv_range, 1)
    assemble(units[0])
    assemble(units[1])
    pass_on(kv_range, 2)
    assemble(units[2])
    assemble(units[3])
    for w in range(ways):
        begin(qb_range, w)
    pass_on(kv_range, 3)

    def step(s, carry):
        add(0, s)

        @pl.when(s > 0)
        def _():
            add(1, s - 1)

        @pl.when(s > lag)
        def _():
            add(2, s - 1 - lag)

        @pl.when(s + lead < m)
        def _():
            pass_on(kv_range, s + lead)

        @pl.when(s > lag)
        def _():
            pass_on(qb_range, s - lag)

        pass_on(qa_range, s)
        return carry

    lax.fori_loop(1, m, step, 0)
    add(1, m - 1)
    for s in range(m - lag, m - 1):
        add(2, s - 1)
        pass_on(qb_range, s)
    scale = 1.0 / math.sqrt(hd)
    cosine, sine = cos_ref[...], sin_ref[...]

    def rotate(f):
        return f * cosine + pltpu.roll(f, hd // 2, 1) * sine

    def rotate_back(f):
        return f * cosine - pltpu.roll(f, hd // 2, 1) * sine

    def swap_q(first, size):
        cols = pl.ds(first, size)
        return remote(dq_ref.at[:, cols], eq_ref.at[:, cols], ds.at[0], dr.at[0], across_y)

    swap_kv = remote(dkv_ref, ekv_ref, ds.at[1], dr.at[1], across_y)
    swap_all_q = remote(dq_ref, eq_ref, ds.at[0], dr.at[0], across_y)

    docs = jnp.broadcast_to(doc_ref[...].astype(jnp.float32), (length, length))
    at_key = lax.broadcasted_iota(jnp.int32, (length, length), 1)
    at_query = lax.broadcasted_iota(jnp.int32, (length, length), 0)
    allowed = (at_key <= at_query) & (docs == docs.T)
    key = rotate(acckv[:, :hd]).astype(jnp.bfloat16)
    value = acckv[:, hd:].astype(jnp.bfloat16)

    def attend(heads):
        cols = [slice(k * hd, (k + 1) * hd) for k in heads]
        block = [slice(i * length, (i + 1) * length) for i in range(len(heads))]
        query = jnp.concatenate([rotate(accq[:, c]).astype(jnp.bfloat16) for c in cols], axis=0)
        given = jnp.concatenate([g_ref[:, c] for c in cols], axis=0)
        mask = jnp.concatenate([allowed] * len(heads), axis=0)
        scores = jnp.where(mask, dot(query, key, 1, 1) * scale, neg_large)
        weights = jnp.exp(scores - jnp.max(scores, axis=-1, keepdims=True))
        probs = weights / jnp.sum(weights, axis=-1, keepdims=True)
        probs_b = probs.astype(jnp.bfloat16)
        prob_grad = dot(given, value, 1, 1)
        centre = jnp.sum(probs * prob_grad, axis=-1, keepdims=True)
        dscore = (probs * (prob_grad - centre) * scale).astype(jnp.bfloat16)
        dquery = dot(dscore, key, 1, 0)
        for c, r in zip(cols, block):
            dq_ref[:, c] = rotate_back(dquery[r]).astype(jnp.bfloat16)
        swap_q(heads[0] * hd, len(heads) * hd).start()
        attended = dot(probs_b, value, 1, 0).astype(jnp.bfloat16)
        for c, r in zip(cols, block):
            out_ref[:, c] = attended[r]
        return dot(dscore, query, 0, 0), dot(probs_b, given, 0, 0)

    dkey, dvalue = attend(range(first_heads))
    add(2, m - 2)
    pass_on(qb_range, m - 1)
    add(2, m - 1)
    late_dkey, late_dvalue = attend(range(first_heads, group))
    dkey, dvalue = dkey + late_dkey, dvalue + late_dvalue
    dkv_ref[:, :hd] = rotate_back(dkey).astype(jnp.bfloat16)
    dkv_ref[:, hd:] = dvalue.astype(jnp.bfloat16)
    swap_kv.start()

    def partial(dq, dkv, weights, place, w):
        block = pl.ds(pl.multiple_of(w * piece, piece), piece)
        wk, wa, wb = weights
        return (dot(dq[:, :width_a], wa[place, block, :], 1, 1)
                + dot(dq[:, width_a:], wb[place, block, :], 1, 1)
                + dot(dkv[...], wk[place, block, :], 1, 1)).astype(jnp.bfloat16)

    def send_share(r, lane):
        return remote(psend.at[r, lane], precv.at[r, lane], ps.at[0], pr.at[r, lane], across_y)

    for r, (w, s) in enumerate(far_out):
        for lane in range(lanes):
            psend[r, lane] = partial(dq_ref, dkv_ref, bufs, owner_at(w, s, lane), w)
            send_share(r, lane).start()

    for b in range(3):
        all_of(b, count, ys, yr).wait_recv()
    for w, s in near_in:
        for b in range(3):
            share(b, w, s).start()

    def columns(place, w):
        return pl.ds(pl.multiple_of(place * rows + w * piece, piece), piece)

    def own_part(i, carry):
        for place in (2 * i, 2 * i + 1):
            for w in range(ways):
                grad_ref[:, columns(place, w)] = partial(dq_ref, dkv_ref, bufs, head * half + place, w)
        return carry

    lax.fori_loop(0, half // 2, own_part, 0)
    swap_all_q.wait_recv()
    swap_kv.wait_recv()
    for b in range(3):
        all_of(b, count, ts, tr).wait_recv()

    def plus(place, w, value):
        cols = columns(place, w)
        grad_ref[:, cols] = (grad_ref[:, cols].astype(jnp.float32) + value.astype(jnp.float32)).astype(jnp.bfloat16)

    for w, s in near_in:
        for lane in range(lanes):
            place = owner_at(w, s, lane) - head * half
            plus(place, w, partial(eq_ref, ekv_ref, others, place, w))
    for r, (w, s) in enumerate(far_in):
        for lane in range(lanes):
            send_share(r, lane).wait_recv()
            plus(owner_at(w, s, lane) - head * half, w, precv[r, lane])

    for b in range(3):
        for number, sent in ((ways * (m - 1), rs), (ways * m, cs), (count, ys), (count, ts)):
            all_of(b, number, sent, sent).wait_send()
    remote(parcel, parcel, hs.at[0], hr.at[0], across_y).wait_send()
    swap_all_q.wait_send()
    swap_kv.wait_send()
    remote(psend, psend, ps.at[0], ps.at[0], across_y).wait_send()


def pair_call(n_dp, x, old, fresh, wk, wv, g, head_source, doc_ids):
    length, width = x.shape
    rows, hd = wk.shape
    group = g.shape[1] // hd
    m, half, ways, units, parts = n_dp // 2, n_dp // 2, 2, 4, 8
    late = 2 * hd
    early = group * hd - late
    capacity = (group + 1) // 2
    cosine, sine = rotary_tables(length, hd)
    bf, f32 = jnp.bfloat16, jnp.float32
    vm = pl.BlockSpec(memory_space=pltpu.VMEM)
    anyspace = pl.BlockSpec(memory_space=pl.ANY)
    dma = pltpu.SemaphoreType.DMA
    unit = rows // units
    far = (m // 4, 2)
    return pl.pallas_call(
        functools.partial(pair_kernel, n_dp, group, capacity),
        out_shape=(
            pltpu.VMEM((length, group * hd), bf),
            pltpu.VMEM((length, width // 2), bf),
        ),
        in_specs=[pl.BlockSpec(memory_space=pltpu.SMEM)] + [anyspace] * 9,
        out_specs=(vm, vm),
        scratch_shapes=[
            pltpu.VMEM((1, length), jnp.int32),
            pltpu.VMEM((length, hd), f32),
            pltpu.VMEM((length, hd), f32),
            pltpu.VMEM((length, width), bf),
            pltpu.VMEM((group, rows, hd), bf),
            pltpu.VMEM((length, group * hd), bf),
            pltpu.VMEM((n_dp, rows, 2 * hd), bf),
            pltpu.VMEM((n_dp, rows, early), bf),
            pltpu.VMEM((n_dp, rows, late), bf),
            pltpu.VMEM((half, rows, 2 * hd), bf),
            pltpu.VMEM((half, rows, early), bf),
            pltpu.VMEM((half, rows, late), bf),
            pltpu.VMEM((units, capacity, unit, hd), bf),
            pltpu.VMEM((capacity, unit, hd), bf),
            pltpu.VMEM((capacity, unit, hd), bf),
            pltpu.VMEM((capacity, unit, hd), bf),
            pltpu.VMEM((capacity, unit, hd), bf),
            pltpu.VMEM((length, group * hd), f32),
            pltpu.VMEM((length, 2 * hd), f32),
            pltpu.VMEM((length, group * hd), bf),
            pltpu.VMEM((length, 2 * hd), bf),
            pltpu.VMEM((length, group * hd), bf),
            pltpu.VMEM((length, 2 * hd), bf),
            pltpu.VMEM(far + (length, rows // ways), bf),
            pltpu.VMEM(far + (length, rows // ways), bf),
            dma((group + 7,)),
            dma((3,)),
            dma((parts, m)),
            dma((3,)),
            dma((3, m)),
            dma((1,)),
            dma((units,)),
            dma((3,)),
            dma((3,)),
            dma((3,)),
            dma((3,)),
            dma((2,)),
            dma((2,)),
            dma((1,)),
            dma(far),
        ],
        compiler_params=pltpu.CompilerParams(
            collective_id=0, has_side_effects=True, vmem_limit_bytes=48*1024*1024),
    )(*(pltpu.with_memory_space_constraint(jnp.asarray(a), pltpu.HBM) for a in (
        head_source, doc_ids.reshape(1, -1), cosine, sine, x, old, fresh, wk, wv, g)))


def solution(mesh):
    n_dp, n_head = mesh.shape["dp"], mesh.shape["head"]

    def local(x, old, fresh, wk, wv, g, head_source, doc_ids):
        length, width = x.shape
        rows, hd = wk.shape
        group = g.shape[1] // hd
        ways = 2 if rows % 256 == 0 else 1
        m = n_dp // 2
        if n_head == 2 and group > 2 and rows % 512 == 0 and m % 8 == 0:
            return pair_call(n_dp, x, old, fresh, wk, wv, g, head_source, doc_ids)
        capacity = (group + n_head - 1) // n_head
        chunks = n_dp // n_head
        cosine, sine = rotary_tables(length, hd)
        bf, f32 = jnp.bfloat16, jnp.float32
        vm = pl.BlockSpec(memory_space=pltpu.VMEM)
        anyspace = pl.BlockSpec(memory_space=pl.ANY)
        dma = pltpu.SemaphoreType.DMA
        return pl.pallas_call(
            functools.partial(kernel, n_dp, n_head, group, ways),
            out_shape=(
                jax.ShapeDtypeStruct((length, group * hd), bf),
                jax.ShapeDtypeStruct((length, width // n_head), bf),
            ),
            in_specs=[pl.BlockSpec(memory_space=pltpu.SMEM)] + [anyspace] * 9,
            out_specs=(vm, vm),
            scratch_shapes=[
                pltpu.VMEM((1, length), jnp.int32),
                pltpu.VMEM((length, hd), f32),
                pltpu.VMEM((length, hd), f32),
                pltpu.VMEM((length, width), bf),
                pltpu.VMEM((rows, group * hd), bf),
                pltpu.VMEM((length, group * hd), bf),
                pltpu.VMEM((n_dp, rows, group * hd), bf),
                pltpu.VMEM((n_dp, rows, 2 * hd), bf),
                pltpu.VMEM((2 * ways, n_head - 1, capacity, rows // (2 * ways), hd), bf),
                pltpu.VMEM((2 * ways, n_head - 1, capacity, rows // (2 * ways), hd), bf),
                pltpu.VMEM((length, group * hd), f32),
                pltpu.VMEM((length, 2 * hd), f32),
                pltpu.VMEM((length, group * hd), bf),
                pltpu.VMEM((length, 2 * hd), bf),
                pltpu.VMEM((n_head - 1, chunks, length, rows), bf),
                pltpu.VMEM((n_head - 1, chunks, length, rows), bf),
                dma((9,)),
                dma((3 * ways, m)),
                dma((3 * ways, m)),
                dma((3 * ways, m)),
                dma((3 * ways, m)),
                dma((2 * ways, n_head - 1)),
                dma((2 * ways, n_head - 1)),
                dma((n_head - 1, chunks)),
                dma((n_head - 1, chunks)),
            ],
            compiler_params=pltpu.CompilerParams(
                collective_id=0, has_side_effects=True, vmem_limit_bytes=67043328),
        )(head_source, doc_ids.reshape(1, -1), cosine, sine, x, old, fresh, wk, wv, g)

    in_specs = (
        P("dp", None), P("dp", "head"), P("dp", "head"), P("dp", "head"),
        P("dp", "head"), P("dp", "head"), P(), P("dp"),
    )
    return jax.shard_map(
        local, mesh=mesh, in_specs=in_specs,
        out_specs=(P("dp", "head"), P("dp", "head")), check_vma=False)
```

```python
import functools
import math

import jax
import jax.numpy as jnp
import numpy as np
from jax import lax
from jax.experimental import pallas as pl
from jax.experimental.pallas import tpu as pltpu
from jax.sharding import PartitionSpec as P

theta_base = 500000.0
neg_large = -1e30
MESH = pl.DeviceIdType.MESH


def rotary_tables(length, width):
    half = width // 2
    frequency = theta_base ** (-2.0 * np.arange(half, dtype=np.float64) / width)
    angles = np.arange(length, dtype=np.float64)[:, None] * frequency[None, :]
    cosine, sine = np.cos(angles), np.sin(angles)
    return (
        np.concatenate([cosine, cosine], axis=1).astype(np.float32),
        np.concatenate([-sine, sine], axis=1).astype(np.float32),
    )


def dot(a, b, ca, cb):
    return lax.dot_general(
        a, b, (((ca,), (cb,)), ((), ())), preferred_element_type=jnp.float32
    )


def kernel(
    n_dp, n_head, group, ways,
    src_ref, doc_hbm, cos_hbm, sin_hbm, x_hbm, old_hbm, fresh_hbm, k_hbm, v_hbm, g_hbm,
    out_ref, grad_ref,
    doc_ref, cos_ref, sin_ref, x_ref, own_ref, g_ref, wq, wkv, parcel, arrived, accq, acckv, dq_ref, dkv_ref,
    psend, precv,
    in_sem, rs, rr, cs, cr, hs, hr, ps, pr,
):
    me, head = lax.axis_index("dp"), lax.axis_index("head")
    rows, hd = k_hbm.shape
    length = x_ref.shape[0]
    lanes = 2
    m = n_dp // lanes
    core, chip = me % lanes, me // lanes
    side, level = chip % 2, chip // 2
    pos = (1 - side) * level + side * (m - 1 - level)
    piece = rows // ways
    sub = piece // 2
    lead = min(2, m - 2)
    parts = 3
    capacity = parcel.shape[2]
    signs = (1, -1)[:ways]
    bufs = (wkv, wq)
    spans = ((0, piece), (0, sub), (sub, sub))

    def index_of(p, lane):
        p = (p + 2 * m) % m
        far = p // (m // 2)
        return ((1 - far) * 2 * p + far * (2 * (m - 1 - p) + 1)) * lanes + lane

    right, left = index_of(pos + 1, core), index_of(pos - 1, core)
    targets = (right, left)[:ways]
    partner = index_of(pos, 1 - core)

    loads = [
        pltpu.make_async_copy(k_hbm, wkv.at[me, :, pl.ds(0, hd)], in_sem.at[0]),
        pltpu.make_async_copy(v_hbm, wkv.at[me, :, pl.ds(hd, hd)], in_sem.at[1]),
        pltpu.make_async_copy(old_hbm, own_ref.at[:, pl.ds(0, (group - 1) * hd)], in_sem.at[2]),
        pltpu.make_async_copy(fresh_hbm, own_ref.at[:, pl.ds((group - 1) * hd, hd)], in_sem.at[3]),
        pltpu.make_async_copy(x_hbm, x_ref, in_sem.at[4]),
        pltpu.make_async_copy(g_hbm, g_ref, in_sem.at[5]),
        pltpu.make_async_copy(doc_hbm, doc_ref, in_sem.at[6]),
        pltpu.make_async_copy(cos_hbm, cos_ref, in_sem.at[7]),
        pltpu.make_async_copy(sin_hbm, sin_ref, in_sem.at[8]),
    ]
    for load in loads:
        load.start()

    barrier = pltpu.get_barrier_semaphore()
    peers = [(right, head), (left, head), (partner, head)]
    peers += [(me, (head + j) % n_head) for j in range(1, n_head)]
    for peer in peers:
        pl.semaphore_signal(barrier, inc=1, device_id=peer, device_id_type=MESH)

    def part_of(p, w, owner):
        first, count = spans[p]
        return bufs[min(p, 1)].at[owner, pl.ds(w * piece + first, count)]

    def ring(p, w, s):
        ref = part_of(p, w, index_of(pos - signs[w] * s, core))
        return pltpu.make_async_remote_copy(
            ref, ref, rs.at[w * parts + p, s], rr.at[w * parts + p, s],
            device_id=(targets[w], head), device_id_type=MESH)

    def ring_in(p, w, s):
        ref = part_of(p, w, index_of(pos - signs[w] * (s + 1), core))
        return pltpu.make_async_remote_copy(
            ref, ref, rs.at[w * parts + p, s], rr.at[w * parts + p, s],
            device_id=(targets[w], head), device_id_type=MESH)

    def across(p, w, s, lane):
        ref = part_of(p, w, index_of(pos - signs[w] * s, lane))
        return pltpu.make_async_remote_copy(
            ref, ref, cs.at[w * parts + p, s], cr.at[w * parts + p, s],
            device_id=(partner, head), device_id_type=MESH)

    def relay(u, j):
        return pltpu.make_async_remote_copy(
            parcel.at[u, j - 1], arrived.at[u, j - 1], hs.at[u, j - 1], hr.at[u, j - 1],
            device_id=(me, (head + j) % n_head), device_id_type=MESH)

    shift = [(n_head - src_ref[k] // group) % n_head for k in range(group)]
    taken = [src_ref[k] % group for k in range(group)]
    slot = [
        sum([(shift[l] == shift[k]).astype(jnp.int32) for l in range(k)], jnp.int32(0))
        for k in range(group)
    ]

    def flag(cond):
        return jnp.where(cond, 1.0, 0.0).astype(jnp.float32)

    units = [w * 2 + half for half in range(2) for w in range(ways)]

    def weigh(u, weights):
        total = jnp.zeros((sub, hd), jnp.float32)
        for c_m in range(group):
            block = own_ref[u * sub:(u + 1) * sub, c_m * hd:(c_m + 1) * hd]
            total = total + block.astype(jnp.float32) * weights[c_m]
        return total.astype(jnp.bfloat16)

    for load in loads[:2]:
        load.wait()
    pl.semaphore_wait(barrier, len(peers))
    for w in range(ways):
        ring(0, w, 0).start()
    for w in range(ways):
        across(0, w, 0, core).start()
    for load in loads[2:4]:
        load.wait()
    for u in units:
        for j in range(1, n_head):
            for c in range(capacity):
                weights = [
                    sum([flag((shift[k] == j) & (slot[k] == c) & (taken[k] == c_m))
                         for k in range(group)], jnp.float32(0))
                    for c_m in range(group)
                ]
                parcel[u, j - 1, c] = weigh(u, weights)
            relay(u, j).start()
    for k in range(group):
        weights = [flag((shift[k] == 0) & (taken[k] == c_m)) for c_m in range(group)]
        for u in units:
            wq[me, u * sub:(u + 1) * sub, k * hd:(k + 1) * hd] = weigh(u, weights)
    for load in loads[4:]:
        load.wait()
    accq[...] = jnp.zeros_like(accq)
    acckv[...] = jnp.zeros_like(acckv)

    def add(p, w, owner):
        xs = x_ref[:, pl.ds(pl.multiple_of(owner * rows + w * piece, 128), piece)]
        acc = (acckv, accq)[p]
        acc[...] += dot(xs, bufs[p][owner, pl.ds(w * piece, piece), :], 1, 0)

    def pass_on(p, w, s):
        ring_in(p, w, s - 1).wait_recv()

        @pl.when(s < m - 1)
        def _():
            ring(p, w, s).start()

        across(p, w, s, core).start()

    def unit_out(u):
        block = pl.ds(u * sub, sub)
        for j in range(1, n_head):
            relay(u, j).wait_recv()
        for k in range(group):
            cols = slice(k * hd, (k + 1) * hd)
            total = wq[me, block, cols].astype(jnp.float32)
            for j in range(1, n_head):
                for c in range(capacity):
                    weight = flag((shift[k] == j) & (slot[k] == c))
                    total = total + arrived[u, j - 1, c].astype(jnp.float32) * weight
            wq[me, block, cols] = total.astype(jnp.bfloat16)
        ring(1 + u % 2, u // 2, 0).start()
        across(1 + u % 2, u // 2, 0, core).start()

    for w in range(ways):
        add(0, w, me)
    for u in units[:ways]:
        unit_out(u)
    for s in range(1, lead + 1):
        for w in range(ways):
            pass_on(0, w, s)
        if s == 1:
            for u in units[ways:]:
                unit_out(u)
    for w in range(ways):
        add(1, w, me)

    def step(s, carry):
        @pl.when(s + lead < m)
        def _():
            for w in range(ways):
                pass_on(0, w, s + lead)

        for p in range(1, parts):
            for w in range(ways):
                pass_on(p, w, s)
        for w in range(ways):
            for p in range(2):
                add(p, w, index_of(pos - signs[w] * s, core))
        for w in range(ways):
            for p in range(parts):
                across(p, w, s - 1, 1 - core).wait_recv()
        for w in range(ways):
            for p in range(2):
                add(p, w, index_of(pos - signs[w] * (s - 1), 1 - core))
        return carry

    lax.fori_loop(1, m, step, 0)
    for w in range(ways):
        for p in range(parts):
            across(p, w, m - 1, 1 - core).wait_recv()
        for p in range(2):
            add(p, w, index_of(pos - signs[w] * (m - 1), 1 - core))

    scale = 1.0 / math.sqrt(hd)
    cosine, sine = cos_ref[...], sin_ref[...]

    def rotate(f):
        return f * cosine + pltpu.roll(f, hd // 2, 1) * sine

    def rotate_back(f):
        return f * cosine - pltpu.roll(f, hd // 2, 1) * sine

    docs = jnp.broadcast_to(doc_ref[...].astype(jnp.float32), (length, length))
    at_key = lax.broadcasted_iota(jnp.int32, (length, length), 1)
    at_query = lax.broadcasted_iota(jnp.int32, (length, length), 0)
    allowed = (at_key <= at_query) & (docs == docs.T)
    key = rotate(acckv[:, :hd]).astype(jnp.bfloat16)
    value = acckv[:, hd:].astype(jnp.bfloat16)
    dkey = jnp.zeros((length, hd), jnp.float32)
    dvalue = jnp.zeros((length, hd), jnp.float32)
    for k in range(group):
        cols = slice(k * hd, (k + 1) * hd)
        query = rotate(accq[:, cols]).astype(jnp.bfloat16)
        given = g_ref[:, cols]
        scores = jnp.where(allowed, dot(query, key, 1, 1) * scale, neg_large)
        weights = jnp.exp(scores - jnp.max(scores, axis=-1, keepdims=True))
        probs = weights / jnp.sum(weights, axis=-1, keepdims=True)
        probs_b = probs.astype(jnp.bfloat16)
        out_ref[:, cols] = dot(probs_b, value, 1, 0).astype(jnp.bfloat16)
        prob_grad = dot(given, value, 1, 1)
        centre = jnp.sum(probs * prob_grad, axis=-1, keepdims=True)
        dscore = (probs * (prob_grad - centre) * scale).astype(jnp.bfloat16)
        dq_ref[:, cols] = rotate_back(dot(dscore, key, 1, 0)).astype(jnp.bfloat16)
        dkey = dkey + dot(dscore, query, 0, 0)
        dvalue = dvalue + dot(probs_b, given, 0, 0)
    dkv_ref[:, :hd] = rotate_back(dkey).astype(jnp.bfloat16)
    dkv_ref[:, hd:] = dvalue.astype(jnp.bfloat16)

    chunks = n_dp // n_head

    def partial(owner):
        return (dot(dq_ref[...], wq[owner], 1, 1) + dot(dkv_ref[...], wkv[owner], 1, 1)).astype(
            jnp.bfloat16)

    def share(j, i):
        return pltpu.make_async_remote_copy(
            psend.at[j - 1, i], precv.at[j - 1, i], ps.at[j - 1, i], pr.at[j - 1, i],
            device_id=(me, (head + j) % n_head), device_id_type=MESH)

    for j in range(1, n_head):
        def send_chunk(i, carry):
            psend[j - 1, i] = partial(((head + j) % n_head) * chunks + i)
            share(j, i).start()
            return carry

        lax.fori_loop(0, chunks, send_chunk, 0)

    def own_chunk(i, carry):
        cols = pl.ds(pl.multiple_of(i * rows, 128), rows)
        grad_ref[:, cols] = partial(head * chunks + i)
        return carry

    lax.fori_loop(0, chunks, own_chunk, 0)

    def finish(i, carry):
        cols = pl.ds(pl.multiple_of(i * rows, 128), rows)
        total = grad_ref[:, cols].astype(jnp.float32)
        for j in range(1, n_head):
            share(j, i).wait_recv()
            total = total + precv[j - 1, i].astype(jnp.float32)
        grad_ref[:, cols] = total.astype(jnp.bfloat16)
        return carry

    lax.fori_loop(0, chunks, finish, 0)

    def drain(s, carry):
        for p in range(parts):
            for w in range(ways):
                @pl.when(s < m - 1)
                def _():
                    ring(p, w, s).wait_send()

                across(p, w, s, core).wait_send()
        return carry

    lax.fori_loop(0, m, drain, 0)
    for j in range(1, n_head):
        for u in units:
            relay(u, j).wait_send()

        def drain_share(i, carry):
            share(j, i).wait_send()
            return carry

        lax.fori_loop(0, chunks, drain_share, 0)


def pair_kernel(
    n_dp, group, capacity,
    src_hbm, doc_hbm, cos_hbm, sin_hbm, x_hbm, old_hbm, fresh_hbm, k_hbm, v_hbm, g_hbm,
    out_ref, grad_ref,
    src_ref, doc_ref, cos_ref, sin_ref, x_ref, own_ref, g_ref, wkv, wqa, wqb, okv, oqa, oqb, parcel, arrived_0, arrived_1, arrived_2, arrived_3, accq, acckv,
    dq_ref, dkv_ref, eq_ref, ekv_ref, psend, precv,
    in_sem, rs, rr, cs, cr, hs, hr, ys, yr, ts, tr, ds, dr, ps, pr,
):
    me, head = lax.axis_index("dp"), lax.axis_index("head")
    rows, hd = k_hbm.shape
    length = x_ref.shape[0]
    lanes, ways = 2, 2
    m = n_dp // lanes
    half = n_dp // 2
    core, chip = me % lanes, me // lanes
    side, level = chip % 2, chip // 2
    pos = (1 - side) * level + side * (m - 1 - level)
    piece = rows // ways
    kv_parts = [(0, first, piece // 2) for first in range(0, piece, piece // 2)]
    qa_parts = [(1, first, piece // 2) for first in range(0, piece, piece // 2)]
    qb_parts = [(2, first, piece // 1) for first in range(0, piece, piece // 1)]
    parts = kv_parts + qa_parts + qb_parts
    kv_range = range(len(kv_parts))
    qa_range = range(len(kv_parts), len(kv_parts) + len(qa_parts))
    qb_range = range(len(kv_parts) + len(qa_parts), len(parts))
    unit = rows // parcel.shape[0]
    lead = 3
    count = m - m // 4
    signs = (1, -1)
    arrived = (arrived_0, arrived_1, arrived_2, arrived_3)
    bufs = (wkv, wqa, wqb)
    others = (okv, oqa, oqb)
    first_heads = wqa.shape[2] // hd
    width_a = wqa.shape[2]

    def index_of(p, lane):
        p = jnp.where(p < 0, p + m, p)
        p = jnp.where(p >= m, p - m, p)
        return jnp.where(p < m // 2, 2 * p, 2 * (m - 1 - p) + 1) * lanes + lane

    right, left = index_of(pos + 1, core), index_of(pos - 1, core)
    targets = (right, left)
    partner = index_of(pos, 1 - core)
    across_y = (me, 1 - head)

    barrier = pltpu.get_barrier_semaphore()
    peers = [(right, head), (left, head), (partner, head), across_y]
    for peer in peers:
        pl.semaphore_signal(barrier, inc=1, device_id=peer, device_id_type=MESH)

    loads = [
        pltpu.make_async_copy(k_hbm, wkv.at[me, :, pl.ds(0, hd)], in_sem.at[0]),
        pltpu.make_async_copy(v_hbm, wkv.at[me, :, pl.ds(hd, hd)], in_sem.at[1]),
    ]
    loads += [
        pltpu.make_async_copy(old_hbm.at[:, pl.ds(c * hd, hd)], own_ref.at[c], in_sem.at[2 + c])
        for c in range(group - 1)
    ]
    loads += [
        pltpu.make_async_copy(fresh_hbm, own_ref.at[group - 1], in_sem.at[group + 1]),
        pltpu.make_async_copy(src_hbm, src_ref, in_sem.at[group + 7]),
        pltpu.make_async_copy(x_hbm, x_ref, in_sem.at[group + 2]),
        pltpu.make_async_copy(g_hbm, g_ref, in_sem.at[group + 3]),
        pltpu.make_async_copy(doc_hbm, doc_ref, in_sem.at[group + 4]),
        pltpu.make_async_copy(cos_hbm, cos_ref, in_sem.at[group + 5]),
        pltpu.make_async_copy(sin_hbm, sin_ref, in_sem.at[group + 6]),
    ]
    for load in loads:
        load.start()

    def remote(src, dst, send, recv, device):
        return pltpu.make_async_remote_copy(
            src, dst, send, recv, device_id=device, device_id_type=MESH)

    def part_of(p, w, owner):
        b, first, size = parts[p]
        return bufs[b].at[owner, pl.ds(w * piece + first, size)]

    def ring(p, w, s, owner):
        ref = part_of(p, w, owner)
        return remote(ref, ref, rs.at[parts[p][0]], rr.at[p, s], (targets[w], head))

    def ring_in(p, s):
        b, _, size = parts[p]
        ref = bufs[b].at[me, pl.ds(0, ways * size)]
        return remote(ref, ref, rs.at[b], rr.at[p, s], (left, head))

    def across(p, w, s, owner):
        ref = part_of(p, w, owner)
        return remote(ref, ref, cs.at[parts[p][0]], cr.at[parts[p][0], s], (partner, head))

    def across_in(b, s):
        ref = bufs[b].at[me]
        return remote(ref, ref, cs.at[b], cr.at[b, s], (partner, head))

    def forward(p, w, owner):
        b, first, size = parts[p]
        dst = others[b].at[owner - (1 - head) * half, pl.ds(w * piece + first, size)]
        return remote(part_of(p, w, owner), dst, ys.at[b], yr.at[b], across_y)

    def owner_at(w, s, lane):
        return index_of(pos - (1 - 2 * w) * s, lane)

    def share(b, w, s):
        ref = others[b].at[owner_at(w, s, core) - head * half, pl.ds(pl.multiple_of(w * piece, piece), piece)]
        return remote(ref, ref, ts.at[b], tr.at[b], (partner, head))

    def all_of(b, count, send, recv):
        ref = bufs[b].at[pl.ds(0, count), pl.ds(0, piece)]
        return remote(ref, ref, send.at[b], recv.at[b], across_y)

    def for_here(w, s):
        return (index_of(pos - signs[w] * s, 0) >= half) == (head == 1)

    def relay(u):
        return remote(parcel.at[u], arrived[u], hs.at[0], hr.at[u], across_y)

    units = [w * 2 + late for late in range(2) for w in range(ways)]

    for load in loads[:2]:
        load.wait()
    pl.semaphore_wait(barrier, len(peers))
    for p in kv_range:
        for w in range(ways):
            ring(p, w, 0, me).start()
    for p in kv_range:
        for w in range(ways):
            across(p, w, 0, me).start()
    for load in loads[2:3 + group]:
        load.wait()
    shift = [(2 - src_ref[0, k] // group) % 2 for k in range(group)]
    taken = [src_ref[0, k] % group for k in range(group)]
    slot = [
        sum([(shift[l] == 1).astype(jnp.int32) for l in range(k)], jnp.int32(0)) * shift[k]
        for k in range(group)
    ]
    picks = [
        sum([jnp.where((shift[k] == 1) & (slot[k] == c), taken[k], 0) for k in range(group)], jnp.int32(0))
        for c in range(capacity)
    ]
    for u in units:
        for c in range(capacity):
            parcel[u, c] = own_ref[picks[c], u * unit:(u + 1) * unit]
        relay(u).start()

    def by_arrival(to):
        begin = (2 * to + 3) * (m // 4)
        places = [(w, lax.rem(signs[w] * (pos - begin - i) + 3 * m, m)) for w in range(ways) for i in range(m // 2)]
        later = [
            sum([jnp.where(t > s - (v > w), 1, 0) for v, t in places], jnp.int32(0)) for w, s in places
        ]
        order = []
        for r in range(m):
            order.append((
                sum([jnp.where(late == r, w, 0) for late, (w, _) in zip(later, places)], jnp.int32(0)),
                sum([jnp.where(late == r, s, 0) for late, (_, s) in zip(later, places)], jnp.int32(0)),
            ))
        limits = [jnp.int32(-1)] * ways
        for late, (w, s) in zip(later, places):
            limits[w] = jnp.maximum(limits[w], jnp.where(late >= m // 4, s, -1))
        return order, limits

    (order_out, limit_out), (order_in, _) = by_arrival(1 - head), by_arrival(head)
    far_out, far_in, near_in = order_out[:m // 4], order_in[:m // 4], order_in[m // 4:]

    def forwarded(w, s):
        return jnp.logical_not(for_here(w, s)) & (s <= limit_out[w])

    def hand_on(some, w, owner, wanted):
        @pl.when(wanted)
        def _():
            for p in some:
                forward(p, w, owner).start()

    for w in range(ways):
        hand_on(kv_range, w, me, forwarded(w, 0))
    for load in loads[3 + group:]:
        load.wait()

    accs = (acckv, accq.at[:, pl.ds(0, width_a)], accq.at[:, pl.ds(width_a, group * hd - width_a)])

    def add_lanes(b, s, some):
        total = accs[b][...]
        for lane in some:
            for w in range(ways):
                owner = index_of(pos - signs[w] * s, lane)
                xs = x_ref[:, pl.ds(pl.multiple_of(owner * rows + w * piece, 128), piece)]
                total = total + dot(xs, bufs[b][owner, pl.ds(w * piece, piece), :], 1, 0)
        accs[b][...] = total

    def add(b, s):
        across_in(b, s).wait_recv()
        add_lanes(b, s, range(lanes))

    def begin(some, w):
        for p in some:
            ring(p, w, 0, me).start()
        for p in some:
            across(p, w, 0, me).start()
        hand_on(some, w, me, forwarded(w, 0))

    def pass_on(some, s):
        owners = [index_of(pos - signs[w] * s, core) for w in range(ways)]
        wanted = [forwarded(w, s) for w in range(ways)]
        for p in some:
            ring_in(p, s - 1).wait_recv()

            @pl.when(s < m - 1)
            def _():
                for w in range(ways):
                    ring(p, w, s, owners[w]).start()

            for w in range(ways):
                across(p, w, s, owners[w]).start()
                hand_on([p], w, owners[w], wanted[w])

    accq[...] = jnp.zeros_like(accq)
    acckv[...] = jnp.zeros_like(acckv)
    add(0, 0)

    def assemble(u):
        relay(u).wait_recv()
        block = slice(u * unit, (u + 1) * unit)
        for k in range(group):
            b, at = (1, k) if k < first_heads else (2, k - first_heads)
            bufs[b][me, block, at * hd:(at + 1) * hd] = jnp.where(
                shift[k] == 0, own_ref[taken[k], block], arrived[u][slot[k]])
        begin([qa_range[u % 2]], u // 2)

    pass_on(kv_range, 1)
    assemble(units[0])
    assemble(units[1])
    pass_on(kv_range, 2)
    assemble(units[2])
    assemble(units[3])
    for w in range(ways):
        begin(qb_range, w)
    pass_on(kv_range, 3)

    def step(s, carry):
        add(0, s)

        @pl.when(s > 0)
        def _():
            add(1, s - 1)

        @pl.when(s > 1)
        def _():
            add(2, s - 2)

        @pl.when(s + lead < m)
        def _():
            pass_on(kv_range, s + lead)

        @pl.when(s > 1)
        def _():
            pass_on(qb_range, s - 1)

        pass_on(qa_range, s)
        return carry

    lax.fori_loop(1, m, step, 0)
    add(2, m - 2)
    add_lanes(1, m - 1, [core])
    across_in(1, m - 1).wait_recv()
    add_lanes(1, m - 1, [1 - core])
    scale = 1.0 / math.sqrt(hd)
    cosine, sine = cos_ref[...], sin_ref[...]

    def rotate(f):
        return f * cosine + pltpu.roll(f, hd // 2, 1) * sine

    def rotate_back(f):
        return f * cosine - pltpu.roll(f, hd // 2, 1) * sine

    def swap_q(first, size):
        cols = pl.ds(first, size)
        return remote(dq_ref.at[:, cols], eq_ref.at[:, cols], ds.at[0], dr.at[0], across_y)

    swap_kv = remote(dkv_ref, ekv_ref, ds.at[1], dr.at[1], across_y)
    swap_all_q = remote(dq_ref, eq_ref, ds.at[0], dr.at[0], across_y)

    docs = jnp.broadcast_to(doc_ref[...].astype(jnp.float32), (length, length))
    at_key = lax.broadcasted_iota(jnp.int32, (length, length), 1)
    at_query = lax.broadcasted_iota(jnp.int32, (length, length), 0)
    allowed = (at_key <= at_query) & (docs == docs.T)
    key = rotate(acckv[:, :hd]).astype(jnp.bfloat16)
    value = acckv[:, hd:].astype(jnp.bfloat16)

    def attend(heads):
        cols = [slice(k * hd, (k + 1) * hd) for k in heads]
        block = [slice(i * length, (i + 1) * length) for i in range(len(heads))]
        query = jnp.concatenate([rotate(accq[:, c]).astype(jnp.bfloat16) for c in cols], axis=0)
        given = jnp.concatenate([g_ref[:, c] for c in cols], axis=0)
        mask = jnp.concatenate([allowed] * len(heads), axis=0)
        scores = jnp.where(mask, dot(query, key, 1, 1) * scale, neg_large)
        weights = jnp.exp(scores - jnp.max(scores, axis=-1, keepdims=True))
        probs = weights / jnp.sum(weights, axis=-1, keepdims=True)
        probs_b = probs.astype(jnp.bfloat16)
        prob_grad = dot(given, value, 1, 1)
        centre = jnp.sum(probs * prob_grad, axis=-1, keepdims=True)
        dscore = (probs * (prob_grad - centre) * scale).astype(jnp.bfloat16)
        dquery = dot(dscore, key, 1, 0)
        for c, r in zip(cols, block):
            dq_ref[:, c] = rotate_back(dquery[r]).astype(jnp.bfloat16)
        swap_q(heads[0] * hd, len(heads) * hd).start()
        attended = dot(probs_b, value, 1, 0).astype(jnp.bfloat16)
        for c, r in zip(cols, block):
            out_ref[:, c] = attended[r]
        return dot(dscore, query, 0, 0), dot(probs_b, given, 0, 0)

    dkey, dvalue = attend(range(first_heads))
    pass_on(qb_range, m - 1)
    add_lanes(2, m - 1, [core])
    across_in(2, m - 1).wait_recv()
    add_lanes(2, m - 1, [1 - core])
    late_dkey, late_dvalue = attend(range(first_heads, group))
    dkey, dvalue = dkey + late_dkey, dvalue + late_dvalue
    dkv_ref[:, :hd] = rotate_back(dkey).astype(jnp.bfloat16)
    dkv_ref[:, hd:] = dvalue.astype(jnp.bfloat16)
    swap_kv.start()

    def partial(dq, dkv, weights, place, w):
        block = pl.ds(pl.multiple_of(w * piece, piece), piece)
        wk, wa, wb = weights
        return (dot(dq[:, :width_a], wa[place, block, :], 1, 1)
                + dot(dq[:, width_a:], wb[place, block, :], 1, 1)
                + dot(dkv[...], wk[place, block, :], 1, 1)).astype(jnp.bfloat16)

    def send_share(r, lane):
        return remote(psend.at[r, lane], precv.at[r, lane], ps.at[0], pr.at[r, lane], across_y)

    for r, (w, s) in enumerate(far_out):
        for lane in range(lanes):
            psend[r, lane] = partial(dq_ref, dkv_ref, bufs, owner_at(w, s, lane), w)
            send_share(r, lane).start()

    for b in range(3):
        all_of(b, count, ys, yr).wait_recv()
    for w, s in near_in:
        for b in range(3):
            share(b, w, s).start()

    def columns(place, w):
        return pl.ds(pl.multiple_of(place * rows + w * piece, piece), piece)

    def own_part(i, carry):
        for place in (2 * i, 2 * i + 1):
            for w in range(ways):
                grad_ref[:, columns(place, w)] = partial(dq_ref, dkv_ref, bufs, head * half + place, w)
        return carry

    lax.fori_loop(0, half // 2, own_part, 0)
    swap_all_q.wait_recv()
    swap_kv.wait_recv()
    for b in range(3):
        all_of(b, count, ts, tr).wait_recv()

    def plus(place, w, value):
        cols = columns(place, w)
        grad_ref[:, cols] = (grad_ref[:, cols].astype(jnp.float32) + value.astype(jnp.float32)).astype(jnp.bfloat16)

    for w, s in near_in:
        for lane in range(lanes):
            place = owner_at(w, s, lane) - head * half
            plus(place, w, partial(eq_ref, ekv_ref, others, place, w))
    for r, (w, s) in enumerate(far_in):
        for lane in range(lanes):
            send_share(r, lane).wait_recv()
            plus(owner_at(w, s, lane) - head * half, w, precv[r, lane])

    for b in range(3):
        for number, sent in ((ways * (m - 1), rs), (ways * m, cs), (count, ys), (count, ts)):
            all_of(b, number, sent, sent).wait_send()
    remote(parcel, parcel, hs.at[0], hr.at[0], across_y).wait_send()
    swap_all_q.wait_send()
    swap_kv.wait_send()
    remote(psend, psend, ps.at[0], ps.at[0], across_y).wait_send()


def put_out(attended_ref, grad_ref, out_hbm, grad_hbm, sem):
    copies = [
        pltpu.make_async_copy(attended_ref, out_hbm, sem.at[0]),
        pltpu.make_async_copy(grad_ref, grad_hbm, sem.at[1]),
    ]
    for copy in copies:
        copy.start()
    for copy in copies:
        copy.wait()


def pair_call(n_dp, x, old, fresh, wk, wv, g, head_source, doc_ids):
    length, width = x.shape
    rows, hd = wk.shape
    group = g.shape[1] // hd
    m, half, ways, units, parts = n_dp // 2, n_dp // 2, 2, 4, 5
    late = 2 * hd
    early = group * hd - late
    capacity = (group + 1) // 2
    cosine, sine = rotary_tables(length, hd)
    bf, f32 = jnp.bfloat16, jnp.float32
    vm = pl.BlockSpec(memory_space=pltpu.VMEM)
    anyspace = pl.BlockSpec(memory_space=pl.ANY)
    dma = pltpu.SemaphoreType.DMA
    unit = rows // units
    far = (m // 4, 2)
    attended, grad = pl.pallas_call(
        functools.partial(pair_kernel, n_dp, group, capacity),
        out_shape=(
            pltpu.VMEM((length, group * hd), bf),
            pltpu.VMEM((length, width // 2), bf),
        ),
        in_specs=[anyspace] * 10,
        out_specs=(vm, vm),
        scratch_shapes=[
            pltpu.SMEM((1, head_source.shape[0]), jnp.int32),
            pltpu.VMEM((1, length), jnp.int32),
            pltpu.VMEM((length, hd), f32),
            pltpu.VMEM((length, hd), f32),
            pltpu.VMEM((length, width), bf),
            pltpu.VMEM((group, rows, hd), bf),
            pltpu.VMEM((length, group * hd), bf),
            pltpu.VMEM((n_dp, rows, 2 * hd), bf),
            pltpu.VMEM((n_dp, rows, early), bf),
            pltpu.VMEM((n_dp, rows, late), bf),
            pltpu.VMEM((half, rows, 2 * hd), bf),
            pltpu.VMEM((half, rows, early), bf),
            pltpu.VMEM((half, rows, late), bf),
            pltpu.VMEM((units, capacity, unit, hd), bf),
            pltpu.VMEM((capacity, unit, hd), bf),
            pltpu.VMEM((capacity, unit, hd), bf),
            pltpu.VMEM((capacity, unit, hd), bf),
            pltpu.VMEM((capacity, unit, hd), bf),
            pltpu.VMEM((length, group * hd), f32),
            pltpu.VMEM((length, 2 * hd), f32),
            pltpu.VMEM((length, group * hd), bf),
            pltpu.VMEM((length, 2 * hd), bf),
            pltpu.VMEM((length, group * hd), bf),
            pltpu.VMEM((length, 2 * hd), bf),
            pltpu.VMEM(far + (length, rows // ways), bf),
            pltpu.VMEM(far + (length, rows // ways), bf),
            dma((group + 8,)),
            dma((3,)),
            dma((parts, m)),
            dma((3,)),
            dma((3, m)),
            dma((1,)),
            dma((units,)),
            dma((3,)),
            dma((3,)),
            dma((3,)),
            dma((3,)),
            dma((2,)),
            dma((2,)),
            dma((1,)),
            dma(far),
        ],
        compiler_params=pltpu.CompilerParams(
            collective_id=0, has_side_effects=True, vmem_limit_bytes=48*1024*1024),
    )(*(pltpu.with_memory_space_constraint(jnp.asarray(a), pltpu.HBM) for a in (
        head_source.reshape(1, -1), doc_ids.reshape(1, -1), cosine, sine, x, old, fresh, wk, wv, g)))
    return pl.pallas_call(
        put_out,
        out_shape=(pltpu.HBM(attended.shape, bf), pltpu.HBM(grad.shape, bf)),
        in_specs=[vm, vm],
        out_specs=(anyspace, anyspace),
        scratch_shapes=[dma((2,))],
        compiler_params=pltpu.CompilerParams(vmem_limit_bytes=1024 * 1024),
    )(pltpu.with_memory_space_constraint(attended, pltpu.VMEM), pltpu.with_memory_space_constraint(grad, pltpu.VMEM))


def solution(mesh):
    n_dp, n_head = mesh.shape["dp"], mesh.shape["head"]

    def local(x, old, fresh, wk, wv, g, head_source, doc_ids):
        length, width = x.shape
        rows, hd = wk.shape
        group = g.shape[1] // hd
        ways = 2 if rows % 256 == 0 else 1
        m = n_dp // 2
        if n_head == 2 and group > 2 and rows % 512 == 0 and m % 8 == 0:
            return pair_call(n_dp, x, old, fresh, wk, wv, g, head_source, doc_ids)
        capacity = (group + n_head - 1) // n_head
        chunks = n_dp // n_head
        cosine, sine = rotary_tables(length, hd)
        bf, f32 = jnp.bfloat16, jnp.float32
        vm = pl.BlockSpec(memory_space=pltpu.VMEM)
        anyspace = pl.BlockSpec(memory_space=pl.ANY)
        dma = pltpu.SemaphoreType.DMA
        return pl.pallas_call(
            functools.partial(kernel, n_dp, n_head, group, ways),
            out_shape=(
                jax.ShapeDtypeStruct((length, group * hd), bf),
                jax.ShapeDtypeStruct((length, width // n_head), bf),
            ),
            in_specs=[pl.BlockSpec(memory_space=pltpu.SMEM)] + [anyspace] * 9,
            out_specs=(vm, vm),
            scratch_shapes=[
                pltpu.VMEM((1, length), jnp.int32),
                pltpu.VMEM((length, hd), f32),
                pltpu.VMEM((length, hd), f32),
                pltpu.VMEM((length, width), bf),
                pltpu.VMEM((rows, group * hd), bf),
                pltpu.VMEM((length, group * hd), bf),
                pltpu.VMEM((n_dp, rows, group * hd), bf),
                pltpu.VMEM((n_dp, rows, 2 * hd), bf),
                pltpu.VMEM((2 * ways, n_head - 1, capacity, rows // (2 * ways), hd), bf),
                pltpu.VMEM((2 * ways, n_head - 1, capacity, rows // (2 * ways), hd), bf),
                pltpu.VMEM((length, group * hd), f32),
                pltpu.VMEM((length, 2 * hd), f32),
                pltpu.VMEM((length, group * hd), bf),
                pltpu.VMEM((length, 2 * hd), bf),
                pltpu.VMEM((n_head - 1, chunks, length, rows), bf),
                pltpu.VMEM((n_head - 1, chunks, length, rows), bf),
                dma((9,)),
                dma((3 * ways, m)),
                dma((3 * ways, m)),
                dma((3 * ways, m)),
                dma((3 * ways, m)),
                dma((2 * ways, n_head - 1)),
                dma((2 * ways, n_head - 1)),
                dma((n_head - 1, chunks)),
                dma((n_head - 1, chunks)),
            ],
            compiler_params=pltpu.CompilerParams(
                collective_id=0, has_side_effects=True, vmem_limit_bytes=67043328),
        )(head_source, doc_ids.reshape(1, -1), cosine, sine, x, old, fresh, wk, wv, g)

    in_specs = (
        P("dp", None), P("dp", "head"), P("dp", "head"), P("dp", "head"),
        P("dp", "head"), P("dp", "head"), P(), P("dp"),
    )
    return jax.shard_map(
        local, mesh=mesh, in_specs=in_specs,
        out_specs=(P("dp", "head"), P("dp", "head")), check_vma=False)
```

```python
import functools
import math

import jax
import jax.numpy as jnp
import numpy as np
from jax import lax
from jax.experimental import pallas as pl
from jax.experimental.pallas import tpu as pltpu
from jax.sharding import PartitionSpec as P

theta_base = 500000.0
neg_large = -1e30
MESH = pl.DeviceIdType.MESH


def rotary_tables(length, width):
    half = width // 2
    frequency = theta_base ** (-2.0 * np.arange(half, dtype=np.float64) / width)
    angles = np.arange(length, dtype=np.float64)[:, None] * frequency[None, :]
    cosine, sine = np.cos(angles), np.sin(angles)
    return (
        np.concatenate([cosine, cosine], axis=1).astype(np.float32),
        np.concatenate([-sine, sine], axis=1).astype(np.float32),
    )


def dot(a, b, ca, cb):
    return lax.dot_general(
        a, b, (((ca,), (cb,)), ((), ())), preferred_element_type=jnp.float32
    )


def kernel(
    n_dp, n_head, group, ways,
    src_ref, doc_hbm, cos_hbm, sin_hbm, x_hbm, old_hbm, fresh_hbm, k_hbm, v_hbm, g_hbm,
    out_ref, grad_ref,
    doc_ref, cos_ref, sin_ref, x_ref, own_ref, g_ref, wq, wkv, parcel, arrived, accq, acckv, dq_ref, dkv_ref,
    psend, precv,
    in_sem, rs, rr, cs, cr, hs, hr, ps, pr,
):
    me, head = lax.axis_index("dp"), lax.axis_index("head")
    rows, hd = k_hbm.shape
    length = x_ref.shape[0]
    lanes = 2
    m = n_dp // lanes
    core, chip = me % lanes, me // lanes
    side, level = chip % 2, chip // 2
    pos = (1 - side) * level + side * (m - 1 - level)
    piece = rows // ways
    sub = piece // 2
    lead = min(2, m - 2)
    parts = 3
    capacity = parcel.shape[2]
    signs = (1, -1)[:ways]
    bufs = (wkv, wq)
    spans = ((0, piece), (0, sub), (sub, sub))

    def index_of(p, lane):
        p = (p + 2 * m) % m
        far = p // (m // 2)
        return ((1 - far) * 2 * p + far * (2 * (m - 1 - p) + 1)) * lanes + lane

    right, left = index_of(pos + 1, core), index_of(pos - 1, core)
    targets = (right, left)[:ways]
    partner = index_of(pos, 1 - core)

    loads = [
        pltpu.make_async_copy(k_hbm, wkv.at[me, :, pl.ds(0, hd)], in_sem.at[0]),
        pltpu.make_async_copy(v_hbm, wkv.at[me, :, pl.ds(hd, hd)], in_sem.at[1]),
        pltpu.make_async_copy(old_hbm, own_ref.at[:, pl.ds(0, (group - 1) * hd)], in_sem.at[2]),
        pltpu.make_async_copy(fresh_hbm, own_ref.at[:, pl.ds((group - 1) * hd, hd)], in_sem.at[3]),
        pltpu.make_async_copy(x_hbm, x_ref, in_sem.at[4]),
        pltpu.make_async_copy(g_hbm, g_ref, in_sem.at[5]),
        pltpu.make_async_copy(doc_hbm, doc_ref, in_sem.at[6]),
        pltpu.make_async_copy(cos_hbm, cos_ref, in_sem.at[7]),
        pltpu.make_async_copy(sin_hbm, sin_ref, in_sem.at[8]),
    ]
    for load in loads:
        load.start()

    barrier = pltpu.get_barrier_semaphore()
    peers = [(right, head), (left, head), (partner, head)]
    peers += [(me, (head + j) % n_head) for j in range(1, n_head)]
    for peer in peers:
        pl.semaphore_signal(barrier, inc=1, device_id=peer, device_id_type=MESH)

    def part_of(p, w, owner):
        first, count = spans[p]
        return bufs[min(p, 1)].at[owner, pl.ds(w * piece + first, count)]

    def ring(p, w, s):
        ref = part_of(p, w, index_of(pos - signs[w] * s, core))
        return pltpu.make_async_remote_copy(
            ref, ref, rs.at[w * parts + p, s], rr.at[w * parts + p, s],
            device_id=(targets[w], head), device_id_type=MESH)

    def ring_in(p, w, s):
        ref = part_of(p, w, index_of(pos - signs[w] * (s + 1), core))
        return pltpu.make_async_remote_copy(
            ref, ref, rs.at[w * parts + p, s], rr.at[w * parts + p, s],
            device_id=(targets[w], head), device_id_type=MESH)

    def across(p, w, s, lane):
        ref = part_of(p, w, index_of(pos - signs[w] * s, lane))
        return pltpu.make_async_remote_copy(
            ref, ref, cs.at[w * parts + p, s], cr.at[w * parts + p, s],
            device_id=(partner, head), device_id_type=MESH)

    def relay(u, j):
        return pltpu.make_async_remote_copy(
            parcel.at[u, j - 1], arrived.at[u, j - 1], hs.at[u, j - 1], hr.at[u, j - 1],
            device_id=(me, (head + j) % n_head), device_id_type=MESH)

    shift = [(n_head - src_ref[k] // group) % n_head for k in range(group)]
    taken = [src_ref[k] % group for k in range(group)]
    slot = [
        sum([(shift[l] == shift[k]).astype(jnp.int32) for l in range(k)], jnp.int32(0))
        for k in range(group)
    ]

    def flag(cond):
        return jnp.where(cond, 1.0, 0.0).astype(jnp.float32)

    units = [w * 2 + half for half in range(2) for w in range(ways)]

    def weigh(u, weights):
        total = jnp.zeros((sub, hd), jnp.float32)
        for c_m in range(group):
            block = own_ref[u * sub:(u + 1) * sub, c_m * hd:(c_m + 1) * hd]
            total = total + block.astype(jnp.float32) * weights[c_m]
        return total.astype(jnp.bfloat16)

    for load in loads[:2]:
        load.wait()
    pl.semaphore_wait(barrier, len(peers))
    for w in range(ways):
        ring(0, w, 0).start()
    for w in range(ways):
        across(0, w, 0, core).start()
    for load in loads[2:4]:
        load.wait()
    for u in units:
        for j in range(1, n_head):
            for c in range(capacity):
                weights = [
                    sum([flag((shift[k] == j) & (slot[k] == c) & (taken[k] == c_m))
                         for k in range(group)], jnp.float32(0))
                    for c_m in range(group)
                ]
                parcel[u, j - 1, c] = weigh(u, weights)
            relay(u, j).start()
    for k in range(group):
        weights = [flag((shift[k] == 0) & (taken[k] == c_m)) for c_m in range(group)]
        for u in units:
            wq[me, u * sub:(u + 1) * sub, k * hd:(k + 1) * hd] = weigh(u, weights)
    for load in loads[4:]:
        load.wait()
    accq[...] = jnp.zeros_like(accq)
    acckv[...] = jnp.zeros_like(acckv)

    def add(p, w, owner):
        xs = x_ref[:, pl.ds(pl.multiple_of(owner * rows + w * piece, 128), piece)]
        acc = (acckv, accq)[p]
        acc[...] += dot(xs, bufs[p][owner, pl.ds(w * piece, piece), :], 1, 0)

    def pass_on(p, w, s):
        ring_in(p, w, s - 1).wait_recv()

        @pl.when(s < m - 1)
        def _():
            ring(p, w, s).start()

        across(p, w, s, core).start()

    def unit_out(u):
        block = pl.ds(u * sub, sub)
        for j in range(1, n_head):
            relay(u, j).wait_recv()
        for k in range(group):
            cols = slice(k * hd, (k + 1) * hd)
            total = wq[me, block, cols].astype(jnp.float32)
            for j in range(1, n_head):
                for c in range(capacity):
                    weight = flag((shift[k] == j) & (slot[k] == c))
                    total = total + arrived[u, j - 1, c].astype(jnp.float32) * weight
            wq[me, block, cols] = total.astype(jnp.bfloat16)
        ring(1 + u % 2, u // 2, 0).start()
        across(1 + u % 2, u // 2, 0, core).start()

    for w in range(ways):
        add(0, w, me)
    for u in units[:ways]:
        unit_out(u)
    for s in range(1, lead + 1):
        for w in range(ways):
            pass_on(0, w, s)
        if s == 1:
            for u in units[ways:]:
                unit_out(u)
    for w in range(ways):
        add(1, w, me)

    def step(s, carry):
        @pl.when(s + lead < m)
        def _():
            for w in range(ways):
                pass_on(0, w, s + lead)

        for p in range(1, parts):
            for w in range(ways):
                pass_on(p, w, s)
        for w in range(ways):
            for p in range(2):
                add(p, w, index_of(pos - signs[w] * s, core))
        for w in range(ways):
            for p in range(parts):
                across(p, w, s - 1, 1 - core).wait_recv()
        for w in range(ways):
            for p in range(2):
                add(p, w, index_of(pos - signs[w] * (s - 1), 1 - core))
        return carry

    lax.fori_loop(1, m, step, 0)
    for w in range(ways):
        for p in range(parts):
            across(p, w, m - 1, 1 - core).wait_recv()
        for p in range(2):
            add(p, w, index_of(pos - signs[w] * (m - 1), 1 - core))

    scale = 1.0 / math.sqrt(hd)
    cosine, sine = cos_ref[...], sin_ref[...]

    def rotate(f):
        return f * cosine + pltpu.roll(f, hd // 2, 1) * sine

    def rotate_back(f):
        return f * cosine - pltpu.roll(f, hd // 2, 1) * sine

    docs = jnp.broadcast_to(doc_ref[...].astype(jnp.float32), (length, length))
    at_key = lax.broadcasted_iota(jnp.int32, (length, length), 1)
    at_query = lax.broadcasted_iota(jnp.int32, (length, length), 0)
    allowed = (at_key <= at_query) & (docs == docs.T)
    key = rotate(acckv[:, :hd]).astype(jnp.bfloat16)
    value = acckv[:, hd:].astype(jnp.bfloat16)
    dkey = jnp.zeros((length, hd), jnp.float32)
    dvalue = jnp.zeros((length, hd), jnp.float32)
    for k in range(group):
        cols = slice(k * hd, (k + 1) * hd)
        query = rotate(accq[:, cols]).astype(jnp.bfloat16)
        given = g_ref[:, cols]
        scores = jnp.where(allowed, dot(query, key, 1, 1) * scale, neg_large)
        weights = jnp.exp(scores - jnp.max(scores, axis=-1, keepdims=True))
        probs = weights / jnp.sum(weights, axis=-1, keepdims=True)
        probs_b = probs.astype(jnp.bfloat16)
        out_ref[:, cols] = dot(probs_b, value, 1, 0).astype(jnp.bfloat16)
        prob_grad = dot(given, value, 1, 1)
        centre = jnp.sum(probs * prob_grad, axis=-1, keepdims=True)
        dscore = (probs * (prob_grad - centre) * scale).astype(jnp.bfloat16)
        dq_ref[:, cols] = rotate_back(dot(dscore, key, 1, 0)).astype(jnp.bfloat16)
        dkey = dkey + dot(dscore, query, 0, 0)
        dvalue = dvalue + dot(probs_b, given, 0, 0)
    dkv_ref[:, :hd] = rotate_back(dkey).astype(jnp.bfloat16)
    dkv_ref[:, hd:] = dvalue.astype(jnp.bfloat16)

    chunks = n_dp // n_head

    def partial(owner):
        return (dot(dq_ref[...], wq[owner], 1, 1) + dot(dkv_ref[...], wkv[owner], 1, 1)).astype(
            jnp.bfloat16)

    def share(j, i):
        return pltpu.make_async_remote_copy(
            psend.at[j - 1, i], precv.at[j - 1, i], ps.at[j - 1, i], pr.at[j - 1, i],
            device_id=(me, (head + j) % n_head), device_id_type=MESH)

    for j in range(1, n_head):
        def send_chunk(i, carry):
            psend[j - 1, i] = partial(((head + j) % n_head) * chunks + i)
            share(j, i).start()
            return carry

        lax.fori_loop(0, chunks, send_chunk, 0)

    def own_chunk(i, carry):
        cols = pl.ds(pl.multiple_of(i * rows, 128), rows)
        grad_ref[:, cols] = partial(head * chunks + i)
        return carry

    lax.fori_loop(0, chunks, own_chunk, 0)

    def finish(i, carry):
        cols = pl.ds(pl.multiple_of(i * rows, 128), rows)
        total = grad_ref[:, cols].astype(jnp.float32)
        for j in range(1, n_head):
            share(j, i).wait_recv()
            total = total + precv[j - 1, i].astype(jnp.float32)
        grad_ref[:, cols] = total.astype(jnp.bfloat16)
        return carry

    lax.fori_loop(0, chunks, finish, 0)

    def drain(s, carry):
        for p in range(parts):
            for w in range(ways):
                @pl.when(s < m - 1)
                def _():
                    ring(p, w, s).wait_send()

                across(p, w, s, core).wait_send()
        return carry

    lax.fori_loop(0, m, drain, 0)
    for j in range(1, n_head):
        for u in units:
            relay(u, j).wait_send()

        def drain_share(i, carry):
            share(j, i).wait_send()
            return carry

        lax.fori_loop(0, chunks, drain_share, 0)


def pair_kernel(
    n_dp, group, capacity,
    src_hbm, doc_hbm, cos_hbm, sin_hbm, x_hbm, old_hbm, fresh_hbm, k_hbm, v_hbm, g_hbm,
    out_ref, grad_ref,
    src_ref, doc_ref, cos_ref, sin_ref, x_ref, own_ref, g_ref, wkv, wqa, wqb, okv, oqa, oqb, parcel, arrived_0, arrived_1, arrived_2, arrived_3, accq, acckv,
    dq_ref, dkv_ref, eq_ref, ekv_ref, psend, precv,
    in_sem, rs, rr, cs, cr, hs, hr, ys, yr, ts, tr, ds, dr, ps, pr,
):
    me, head = lax.axis_index("dp"), lax.axis_index("head")
    rows, hd = k_hbm.shape
    length = x_ref.shape[0]
    lanes, ways = 2, 2
    m = n_dp // lanes
    half = n_dp // 2
    core, chip = me % lanes, me // lanes
    side, level = chip % 2, chip // 2
    pos = (1 - side) * level + side * (m - 1 - level)
    piece = rows // ways
    kv_parts = [(0, first, piece // 2) for first in range(0, piece, piece // 2)]
    qa_parts = [(1, first, piece // 2) for first in range(0, piece, piece // 2)]
    qb_parts = [(2, first, piece // 1) for first in range(0, piece, piece // 1)]
    parts = kv_parts + qa_parts + qb_parts
    kv_range = range(len(kv_parts))
    qa_range = range(len(kv_parts), len(kv_parts) + len(qa_parts))
    qb_range = range(len(kv_parts) + len(qa_parts), len(parts))
    unit = rows // parcel.shape[0]
    lead = 3
    count = m - m // 4
    signs = (1, -1)
    arrived = (arrived_0, arrived_1, arrived_2, arrived_3)
    bufs = (wkv, wqa, wqb)
    others = (okv, oqa, oqb)
    first_heads = wqa.shape[2] // hd
    width_a = wqa.shape[2]

    def index_of(p, lane):
        p = jnp.where(p < 0, p + m, p)
        p = jnp.where(p >= m, p - m, p)
        return jnp.where(p < m // 2, 2 * p, 2 * (m - 1 - p) + 1) * lanes + lane

    right, left = index_of(pos + 1, core), index_of(pos - 1, core)
    targets = (right, left)
    partner = index_of(pos, 1 - core)
    across_y = (me, 1 - head)

    barrier = pltpu.get_barrier_semaphore()
    peers = [(right, head), (left, head), (partner, head), across_y]
    for peer in peers:
        pl.semaphore_signal(barrier, inc=1, device_id=peer, device_id_type=MESH)

    loads = [
        pltpu.make_async_copy(k_hbm, wkv.at[me, :, pl.ds(0, hd)], in_sem.at[0]),
        pltpu.make_async_copy(v_hbm, wkv.at[me, :, pl.ds(hd, hd)], in_sem.at[1]),
    ]
    loads += [
        pltpu.make_async_copy(old_hbm.at[:, pl.ds(c * hd, hd)], own_ref.at[c], in_sem.at[2 + c])
        for c in range(group - 1)
    ]
    loads += [
        pltpu.make_async_copy(fresh_hbm, own_ref.at[group - 1], in_sem.at[group + 1]),
        pltpu.make_async_copy(src_hbm, src_ref, in_sem.at[group + 7]),
        pltpu.make_async_copy(x_hbm, x_ref, in_sem.at[group + 2]),
        pltpu.make_async_copy(g_hbm, g_ref, in_sem.at[group + 3]),
        pltpu.make_async_copy(doc_hbm, doc_ref, in_sem.at[group + 4]),
        pltpu.make_async_copy(cos_hbm, cos_ref, in_sem.at[group + 5]),
        pltpu.make_async_copy(sin_hbm, sin_ref, in_sem.at[group + 6]),
    ]
    for load in loads:
        load.start()

    def remote(src, dst, send, recv, device):
        return pltpu.make_async_remote_copy(
            src, dst, send, recv, device_id=device, device_id_type=MESH)

    def part_of(p, w, owner):
        b, first, size = parts[p]
        return bufs[b].at[owner, pl.ds(w * piece + first, size)]

    def ring(p, w, s, owner):
        ref = part_of(p, w, owner)
        return remote(ref, ref, rs.at[parts[p][0]], rr.at[p, s], (targets[w], head))

    def ring_in(p, s):
        b, _, size = parts[p]
        ref = bufs[b].at[me, pl.ds(0, ways * size)]
        return remote(ref, ref, rs.at[b], rr.at[p, s], (left, head))

    def across(p, w, s, owner):
        ref = part_of(p, w, owner)
        return remote(ref, ref, cs.at[parts[p][0]], cr.at[parts[p][0], s], (partner, head))

    def across_in(b, s):
        ref = bufs[b].at[me]
        return remote(ref, ref, cs.at[b], cr.at[b, s], (partner, head))

    def forward(p, w, owner):
        b, first, size = parts[p]
        dst = others[b].at[owner - (1 - head) * half, pl.ds(w * piece + first, size)]
        return remote(part_of(p, w, owner), dst, ys.at[b], yr.at[b], across_y)

    def owner_at(w, s, lane):
        return index_of(pos - (1 - 2 * w) * s, lane)

    def share(b, w, s):
        ref = others[b].at[owner_at(w, s, core) - head * half, pl.ds(pl.multiple_of(w * piece, piece), piece)]
        return remote(ref, ref, ts.at[b], tr.at[b], (partner, head))

    def all_of(b, count, send, recv):
        ref = bufs[b].at[pl.ds(0, count), pl.ds(0, piece)]
        return remote(ref, ref, send.at[b], recv.at[b], across_y)

    def for_here(w, s):
        return (index_of(pos - signs[w] * s, 0) >= half) == (head == 1)

    def relay(u):
        return remote(parcel.at[u], arrived[u], hs.at[0], hr.at[u], across_y)

    units = [w * 2 + late for late in range(2) for w in range(ways)]

    for load in loads[:2]:
        load.wait()
    pl.semaphore_wait(barrier, len(peers))
    for p in kv_range:
        for w in range(ways):
            ring(p, w, 0, me).start()
    for p in kv_range:
        for w in range(ways):
            across(p, w, 0, me).start()
    for load in loads[2:3 + group]:
        load.wait()
    shift = [(2 - src_ref[0, k] // group) % 2 for k in range(group)]
    taken = [src_ref[0, k] % group for k in range(group)]
    slot = [
        sum([(shift[l] == 1).astype(jnp.int32) for l in range(k)], jnp.int32(0)) * shift[k]
        for k in range(group)
    ]
    picks = [
        sum([jnp.where((shift[k] == 1) & (slot[k] == c), taken[k], 0) for k in range(group)], jnp.int32(0))
        for c in range(capacity)
    ]
    for u in units:
        for c in range(capacity):
            parcel[u, c] = own_ref[picks[c], u * unit:(u + 1) * unit]
        relay(u).start()

    def by_arrival(to):
        begin = (2 * to + 3) * (m // 4)
        places = [(w, lax.rem(signs[w] * (pos - begin - i) + 3 * m, m)) for w in range(ways) for i in range(m // 2)]
        later = [
            sum([jnp.where(t > s - (v > w), 1, 0) for v, t in places], jnp.int32(0)) for w, s in places
        ]
        order = []
        for r in range(m):
            order.append((
                sum([jnp.where(late == r, w, 0) for late, (w, _) in zip(later, places)], jnp.int32(0)),
                sum([jnp.where(late == r, s, 0) for late, (_, s) in zip(later, places)], jnp.int32(0)),
            ))
        limits = [jnp.int32(-1)] * ways
        for late, (w, s) in zip(later, places):
            limits[w] = jnp.maximum(limits[w], jnp.where(late >= m // 4, s, -1))
        return order, limits

    (order_out, limit_out), (order_in, _) = by_arrival(1 - head), by_arrival(head)
    far_out, far_in, near_in = order_out[:m // 4], order_in[:m // 4], order_in[m // 4:]

    def forwarded(w, s):
        return jnp.logical_not(for_here(w, s)) & (s <= limit_out[w])

    def hand_on(some, w, owner, wanted):
        @pl.when(wanted)
        def _():
            for p in some:
                forward(p, w, owner).start()

    for w in range(ways):
        hand_on(kv_range, w, me, forwarded(w, 0))
    for load in loads[3 + group:]:
        load.wait()

    accs = (acckv, accq.at[:, pl.ds(0, width_a)], accq.at[:, pl.ds(width_a, group * hd - width_a)])

    def add_lanes(b, s, some):
        total = accs[b][...]
        for lane in some:
            for w in range(ways):
                owner = index_of(pos - signs[w] * s, lane)
                xs = x_ref[:, pl.ds(pl.multiple_of(owner * rows + w * piece, 128), piece)]
                total = total + dot(xs, bufs[b][owner, pl.ds(w * piece, piece), :], 1, 0)
        accs[b][...] = total

    def add(b, s):
        across_in(b, s).wait_recv()
        add_lanes(b, s, range(lanes))

    def begin(some, w):
        for p in some:
            ring(p, w, 0, me).start()
        for p in some:
            across(p, w, 0, me).start()
        hand_on(some, w, me, forwarded(w, 0))

    def pass_on(some, s):
        owners = [index_of(pos - signs[w] * s, core) for w in range(ways)]
        wanted = [forwarded(w, s) for w in range(ways)]
        for p in some:
            ring_in(p, s - 1).wait_recv()

            @pl.when(s < m - 1)
            def _():
                for w in range(ways):
                    ring(p, w, s, owners[w]).start()

            for w in range(ways):
                across(p, w, s, owners[w]).start()
                hand_on([p], w, owners[w], wanted[w])

    accq[...] = jnp.zeros_like(accq)
    acckv[...] = jnp.zeros_like(acckv)
    add(0, 0)

    def assemble(u):
        relay(u).wait_recv()
        block = slice(u * unit, (u + 1) * unit)
        for k in range(group):
            b, at = (1, k) if k < first_heads else (2, k - first_heads)
            bufs[b][me, block, at * hd:(at + 1) * hd] = jnp.where(
                shift[k] == 0, own_ref[taken[k], block], arrived[u][slot[k]])
        begin([qa_range[u % 2]], u // 2)

    pass_on(kv_range, 1)
    assemble(units[0])
    assemble(units[1])
    pass_on(kv_range, 2)
    assemble(units[2])
    assemble(units[3])
    for w in range(ways):
        begin(qb_range, w)
    pass_on(kv_range, 3)

    def step(s, carry):
        add(0, s)

        @pl.when(s > 0)
        def _():
            add(1, s - 1)

        @pl.when(s > 1)
        def _():
            add(2, s - 2)

        @pl.when(s + lead < m)
        def _():
            pass_on(kv_range, s + lead)

        @pl.when(s > 1)
        def _():
            pass_on(qb_range, s - 1)

        pass_on(qa_range, s)
        return carry

    lax.fori_loop(1, m, step, 0)
    add(2, m - 2)
    add_lanes(1, m - 1, [core])
    scale = 1.0 / math.sqrt(hd)
    cosine, sine = cos_ref[...], sin_ref[...]

    def rotate(f):
        return f * cosine + pltpu.roll(f, hd // 2, 1) * sine

    def rotate_back(f):
        return f * cosine - pltpu.roll(f, hd // 2, 1) * sine

    def swap_q(first, size):
        cols = pl.ds(first, size)
        return remote(dq_ref.at[:, cols], eq_ref.at[:, cols], ds.at[0], dr.at[0], across_y)

    swap_kv = remote(dkv_ref, ekv_ref, ds.at[1], dr.at[1], across_y)
    swap_all_q = remote(dq_ref, eq_ref, ds.at[0], dr.at[0], across_y)

    docs = jnp.broadcast_to(doc_ref[...].astype(jnp.float32), (length, length))
    at_key = lax.broadcasted_iota(jnp.int32, (length, length), 1)
    at_query = lax.broadcasted_iota(jnp.int32, (length, length), 0)
    allowed = (at_key <= at_query) & (docs == docs.T)
    key = rotate(acckv[:, :hd]).astype(jnp.bfloat16)
    value = acckv[:, hd:].astype(jnp.bfloat16)

    def prepare(heads):
        given = jnp.concatenate([g_ref[:, k * hd:(k + 1) * hd] for k in heads], axis=0)
        return given, dot(given, value, 1, 1)

    def attend(heads, given, prob_grad):
        cols = [slice(k * hd, (k + 1) * hd) for k in heads]
        block = [slice(i * length, (i + 1) * length) for i in range(len(heads))]
        query = jnp.concatenate([rotate(accq[:, c]).astype(jnp.bfloat16) for c in cols], axis=0)
        mask = jnp.concatenate([allowed] * len(heads), axis=0)
        scores = jnp.where(mask, dot(query, key, 1, 1) * scale, neg_large)
        weights = jnp.exp(scores - jnp.max(scores, axis=-1, keepdims=True))
        probs = weights / jnp.sum(weights, axis=-1, keepdims=True)
        probs_b = probs.astype(jnp.bfloat16)
        centre = jnp.sum(probs * prob_grad, axis=-1, keepdims=True)
        dscore = (probs * (prob_grad - centre) * scale).astype(jnp.bfloat16)
        dquery = dot(dscore, key, 1, 0)
        for c, r in zip(cols, block):
            dq_ref[:, c] = rotate_back(dquery[r]).astype(jnp.bfloat16)
        swap_q(heads[0] * hd, len(heads) * hd).start()
        attended = dot(probs_b, value, 1, 0).astype(jnp.bfloat16)
        for c, r in zip(cols, block):
            out_ref[:, c] = attended[r]
        return dot(dscore, query, 0, 0), dot(probs_b, given, 0, 0)

    early, late = prepare(range(first_heads)), prepare(range(first_heads, group))
    across_in(1, m - 1).wait_recv()
    add_lanes(1, m - 1, [1 - core])
    dkey, dvalue = attend(range(first_heads), *early)
    pass_on(qb_range, m - 1)
    add_lanes(2, m - 1, [core])
    across_in(2, m - 1).wait_recv()
    add_lanes(2, m - 1, [1 - core])
    late_dkey, late_dvalue = attend(range(first_heads, group), *late)
    dkey, dvalue = dkey + late_dkey, dvalue + late_dvalue
    dkv_ref[:, :hd] = rotate_back(dkey).astype(jnp.bfloat16)
    dkv_ref[:, hd:] = dvalue.astype(jnp.bfloat16)
    swap_kv.start()

    def partial(dq, dkv, weights, place, w):
        block = pl.ds(pl.multiple_of(w * piece, piece), piece)
        wk, wa, wb = weights
        return (dot(dq[:, :width_a], wa[place, block, :], 1, 1)
                + dot(dq[:, width_a:], wb[place, block, :], 1, 1)
                + dot(dkv[...], wk[place, block, :], 1, 1)).astype(jnp.bfloat16)

    def send_share(r, lane):
        return remote(psend.at[r, lane], precv.at[r, lane], ps.at[0], pr.at[r, lane], across_y)

    for r, (w, s) in enumerate(far_out):
        for lane in range(lanes):
            psend[r, lane] = partial(dq_ref, dkv_ref, bufs, owner_at(w, s, lane), w)
            send_share(r, lane).start()

    for b in range(3):
        all_of(b, count, ys, yr).wait_recv()
    for w, s in near_in:
        for b in range(3):
            share(b, w, s).start()

    def columns(place, w):
        return pl.ds(pl.multiple_of(place * rows + w * piece, piece), piece)

    def own_part(i, carry):
        for place in (2 * i, 2 * i + 1):
            for w in range(ways):
                grad_ref[:, columns(place, w)] = partial(dq_ref, dkv_ref, bufs, head * half + place, w)
        return carry

    lax.fori_loop(0, half // 2, own_part, 0)
    swap_all_q.wait_recv()
    swap_kv.wait_recv()
    for b in range(3):
        all_of(b, count, ts, tr).wait_recv()

    def plus(place, w, value):
        cols = columns(place, w)
        grad_ref[:, cols] = (grad_ref[:, cols].astype(jnp.float32) + value.astype(jnp.float32)).astype(jnp.bfloat16)

    for w, s in near_in:
        for lane in range(lanes):
            place = owner_at(w, s, lane) - head * half
            plus(place, w, partial(eq_ref, ekv_ref, others, place, w))
    for r, (w, s) in enumerate(far_in):
        for lane in range(lanes):
            send_share(r, lane).wait_recv()
            plus(owner_at(w, s, lane) - head * half, w, precv[r, lane])

    for b in range(3):
        for number, sent in ((ways * (m - 1), rs), (ways * m, cs), (count, ys), (count, ts)):
            all_of(b, number, sent, sent).wait_send()
    remote(parcel, parcel, hs.at[0], hr.at[0], across_y).wait_send()
    swap_all_q.wait_send()
    swap_kv.wait_send()
    remote(psend, psend, ps.at[0], ps.at[0], across_y).wait_send()


def put_out(attended_ref, grad_ref, out_hbm, grad_hbm, sem):
    copies = [
        pltpu.make_async_copy(attended_ref, out_hbm, sem.at[0]),
        pltpu.make_async_copy(grad_ref, grad_hbm, sem.at[1]),
    ]
    for copy in copies:
        copy.start()
    for copy in copies:
        copy.wait()


def pair_call(n_dp, x, old, fresh, wk, wv, g, head_source, doc_ids):
    length, width = x.shape
    rows, hd = wk.shape
    group = g.shape[1] // hd
    m, half, ways, units, parts = n_dp // 2, n_dp // 2, 2, 4, 5
    late = 2 * hd
    early = group * hd - late
    capacity = (group + 1) // 2
    cosine, sine = rotary_tables(length, hd)
    bf, f32 = jnp.bfloat16, jnp.float32
    vm = pl.BlockSpec(memory_space=pltpu.VMEM)
    anyspace = pl.BlockSpec(memory_space=pl.ANY)
    dma = pltpu.SemaphoreType.DMA
    unit = rows // units
    far = (m // 4, 2)
    attended, grad = pl.pallas_call(
        functools.partial(pair_kernel, n_dp, group, capacity),
        out_shape=(
            pltpu.VMEM((length, group * hd), bf),
            pltpu.VMEM((length, width // 2), bf),
        ),
        in_specs=[anyspace] * 10,
        out_specs=(vm, vm),
        scratch_shapes=[
            pltpu.SMEM((1, head_source.shape[0]), jnp.int32),
            pltpu.VMEM((1, length), jnp.int32),
            pltpu.VMEM((length, hd), f32),
            pltpu.VMEM((length, hd), f32),
            pltpu.VMEM((length, width), bf),
            pltpu.VMEM((group, rows, hd), bf),
            pltpu.VMEM((length, group * hd), bf),
            pltpu.VMEM((n_dp, rows, 2 * hd), bf),
            pltpu.VMEM((n_dp, rows, early), bf),
            pltpu.VMEM((n_dp, rows, late), bf),
            pltpu.VMEM((half, rows, 2 * hd), bf),
            pltpu.VMEM((half, rows, early), bf),
            pltpu.VMEM((half, rows, late), bf),
            pltpu.VMEM((units, capacity, unit, hd), bf),
            pltpu.VMEM((capacity, unit, hd), bf),
            pltpu.VMEM((capacity, unit, hd), bf),
            pltpu.VMEM((capacity, unit, hd), bf),
            pltpu.VMEM((capacity, unit, hd), bf),
            pltpu.VMEM((length, group * hd), f32),
            pltpu.VMEM((length, 2 * hd), f32),
            pltpu.VMEM((length, group * hd), bf),
            pltpu.VMEM((length, 2 * hd), bf),
            pltpu.VMEM((length, group * hd), bf),
            pltpu.VMEM((length, 2 * hd), bf),
            pltpu.VMEM(far + (length, rows // ways), bf),
            pltpu.VMEM(far + (length, rows // ways), bf),
            dma((group + 8,)),
            dma((3,)),
            dma((parts, m)),
            dma((3,)),
            dma((3, m)),
            dma((1,)),
            dma((units,)),
            dma((3,)),
            dma((3,)),
            dma((3,)),
            dma((3,)),
            dma((2,)),
            dma((2,)),
            dma((1,)),
            dma(far),
        ],
        compiler_params=pltpu.CompilerParams(
            collective_id=0, has_side_effects=True, vmem_limit_bytes=48*1024*1024),
    )(*(pltpu.with_memory_space_constraint(jnp.asarray(a), pltpu.HBM) for a in (
        head_source.reshape(1, -1), doc_ids.reshape(1, -1), cosine, sine, x, old, fresh, wk, wv, g)))
    return pl.pallas_call(
        put_out,
        out_shape=(pltpu.HBM(attended.shape, bf), pltpu.HBM(grad.shape, bf)),
        in_specs=[vm, vm],
        out_specs=(anyspace, anyspace),
        scratch_shapes=[dma((2,))],
        compiler_params=pltpu.CompilerParams(vmem_limit_bytes=1024 * 1024),
    )(pltpu.with_memory_space_constraint(attended, pltpu.VMEM), pltpu.with_memory_space_constraint(grad, pltpu.VMEM))


def solution(mesh):
    n_dp, n_head = mesh.shape["dp"], mesh.shape["head"]

    def local(x, old, fresh, wk, wv, g, head_source, doc_ids):
        length, width = x.shape
        rows, hd = wk.shape
        group = g.shape[1] // hd
        ways = 2 if rows % 256 == 0 else 1
        m = n_dp // 2
        if n_head == 2 and group > 2 and rows % 512 == 0 and m % 8 == 0:
            return pair_call(n_dp, x, old, fresh, wk, wv, g, head_source, doc_ids)
        capacity = (group + n_head - 1) // n_head
        chunks = n_dp // n_head
        cosine, sine = rotary_tables(length, hd)
        bf, f32 = jnp.bfloat16, jnp.float32
        vm = pl.BlockSpec(memory_space=pltpu.VMEM)
        anyspace = pl.BlockSpec(memory_space=pl.ANY)
        dma = pltpu.SemaphoreType.DMA
        return pl.pallas_call(
            functools.partial(kernel, n_dp, n_head, group, ways),
            out_shape=(
                jax.ShapeDtypeStruct((length, group * hd), bf),
                jax.ShapeDtypeStruct((length, width // n_head), bf),
            ),
            in_specs=[pl.BlockSpec(memory_space=pltpu.SMEM)] + [anyspace] * 9,
            out_specs=(vm, vm),
            scratch_shapes=[
                pltpu.VMEM((1, length), jnp.int32),
                pltpu.VMEM((length, hd), f32),
                pltpu.VMEM((length, hd), f32),
                pltpu.VMEM((length, width), bf),
                pltpu.VMEM((rows, group * hd), bf),
                pltpu.VMEM((length, group * hd), bf),
                pltpu.VMEM((n_dp, rows, group * hd), bf),
                pltpu.VMEM((n_dp, rows, 2 * hd), bf),
                pltpu.VMEM((2 * ways, n_head - 1, capacity, rows // (2 * ways), hd), bf),
                pltpu.VMEM((2 * ways, n_head - 1, capacity, rows // (2 * ways), hd), bf),
                pltpu.VMEM((length, group * hd), f32),
                pltpu.VMEM((length, 2 * hd), f32),
                pltpu.VMEM((length, group * hd), bf),
                pltpu.VMEM((length, 2 * hd), bf),
                pltpu.VMEM((n_head - 1, chunks, length, rows), bf),
                pltpu.VMEM((n_head - 1, chunks, length, rows), bf),
                dma((9,)),
                dma((3 * ways, m)),
                dma((3 * ways, m)),
                dma((3 * ways, m)),
                dma((3 * ways, m)),
                dma((2 * ways, n_head - 1)),
                dma((2 * ways, n_head - 1)),
                dma((n_head - 1, chunks)),
                dma((n_head - 1, chunks)),
            ],
            compiler_params=pltpu.CompilerParams(
                collective_id=0, has_side_effects=True, vmem_limit_bytes=67043328),
        )(head_source, doc_ids.reshape(1, -1), cosine, sine, x, old, fresh, wk, wv, g)

    in_specs = (
        P("dp", None), P("dp", "head"), P("dp", "head"), P("dp", "head"),
        P("dp", "head"), P("dp", "head"), P(), P("dp"),
    )
    return jax.shard_map(
        local, mesh=mesh, in_specs=in_specs,
        out_specs=(P("dp", "head"), P("dp", "head")), check_vma=False)
```

```python
import functools
import math

import jax
import jax.numpy as jnp
import numpy as np
from jax import lax
from jax.experimental import pallas as pl
from jax.experimental.pallas import tpu as pltpu
from jax.sharding import PartitionSpec as P

theta_base = 500000.0
neg_large = -1e30
MESH = pl.DeviceIdType.MESH


def rotary_tables(length, width):
    half = width // 2
    frequency = theta_base ** (-2.0 * np.arange(half, dtype=np.float64) / width)
    angles = np.arange(length, dtype=np.float64)[:, None] * frequency[None, :]
    cosine, sine = np.cos(angles), np.sin(angles)
    return (
        np.concatenate([cosine, cosine], axis=1).astype(np.float32),
        np.concatenate([-sine, sine], axis=1).astype(np.float32),
    )


def dot(a, b, ca, cb):
    return lax.dot_general(
        a, b, (((ca,), (cb,)), ((), ())), preferred_element_type=jnp.float32
    )


def kernel(
    n_dp, n_head, group, ways,
    src_ref, doc_hbm, cos_hbm, sin_hbm, x_hbm, old_hbm, fresh_hbm, k_hbm, v_hbm, g_hbm,
    out_ref, grad_ref,
    doc_ref, cos_ref, sin_ref, x_ref, own_ref, g_ref, wq, wkv, parcel, arrived, accq, acckv, dq_ref, dkv_ref,
    psend, precv,
    in_sem, rs, rr, cs, cr, hs, hr, ps, pr,
):
    me, head = lax.axis_index("dp"), lax.axis_index("head")
    rows, hd = k_hbm.shape
    length = x_ref.shape[0]
    lanes = 2
    m = n_dp // lanes
    core, chip = me % lanes, me // lanes
    side, level = chip % 2, chip // 2
    pos = (1 - side) * level + side * (m - 1 - level)
    piece = rows // ways
    sub = piece // 2
    lead = min(2, m - 2)
    parts = 3
    capacity = parcel.shape[2]
    signs = (1, -1)[:ways]
    bufs = (wkv, wq)
    spans = ((0, piece), (0, sub), (sub, sub))

    def index_of(p, lane):
        p = (p + 2 * m) % m
        far = p // (m // 2)
        return ((1 - far) * 2 * p + far * (2 * (m - 1 - p) + 1)) * lanes + lane

    right, left = index_of(pos + 1, core), index_of(pos - 1, core)
    targets = (right, left)[:ways]
    partner = index_of(pos, 1 - core)

    loads = [
        pltpu.make_async_copy(k_hbm, wkv.at[me, :, pl.ds(0, hd)], in_sem.at[0]),
        pltpu.make_async_copy(v_hbm, wkv.at[me, :, pl.ds(hd, hd)], in_sem.at[1]),
        pltpu.make_async_copy(old_hbm, own_ref.at[:, pl.ds(0, (group - 1) * hd)], in_sem.at[2]),
        pltpu.make_async_copy(fresh_hbm, own_ref.at[:, pl.ds((group - 1) * hd, hd)], in_sem.at[3]),
        pltpu.make_async_copy(x_hbm, x_ref, in_sem.at[4]),
        pltpu.make_async_copy(g_hbm, g_ref, in_sem.at[5]),
        pltpu.make_async_copy(doc_hbm, doc_ref, in_sem.at[6]),
        pltpu.make_async_copy(cos_hbm, cos_ref, in_sem.at[7]),
        pltpu.make_async_copy(sin_hbm, sin_ref, in_sem.at[8]),
    ]
    for load in loads:
        load.start()

    barrier = pltpu.get_barrier_semaphore()
    peers = [(right, head), (left, head), (partner, head)]
    peers += [(me, (head + j) % n_head) for j in range(1, n_head)]
    for peer in peers:
        pl.semaphore_signal(barrier, inc=1, device_id=peer, device_id_type=MESH)

    def part_of(p, w, owner):
        first, count = spans[p]
        return bufs[min(p, 1)].at[owner, pl.ds(w * piece + first, count)]

    def ring(p, w, s):
        ref = part_of(p, w, index_of(pos - signs[w] * s, core))
        return pltpu.make_async_remote_copy(
            ref, ref, rs.at[w * parts + p, s], rr.at[w * parts + p, s],
            device_id=(targets[w], head), device_id_type=MESH)

    def ring_in(p, w, s):
        ref = part_of(p, w, index_of(pos - signs[w] * (s + 1), core))
        return pltpu.make_async_remote_copy(
            ref, ref, rs.at[w * parts + p, s], rr.at[w * parts + p, s],
            device_id=(targets[w], head), device_id_type=MESH)

    def across(p, w, s, lane):
        ref = part_of(p, w, index_of(pos - signs[w] * s, lane))
        return pltpu.make_async_remote_copy(
            ref, ref, cs.at[w * parts + p, s], cr.at[w * parts + p, s],
            device_id=(partner, head), device_id_type=MESH)

    def relay(u, j):
        return pltpu.make_async_remote_copy(
            parcel.at[u, j - 1], arrived.at[u, j - 1], hs.at[u, j - 1], hr.at[u, j - 1],
            device_id=(me, (head + j) % n_head), device_id_type=MESH)

    shift = [(n_head - src_ref[k] // group) % n_head for k in range(group)]
    taken = [src_ref[k] % group for k in range(group)]
    slot = [
        sum([(shift[l] == shift[k]).astype(jnp.int32) for l in range(k)], jnp.int32(0))
        for k in range(group)
    ]

    def flag(cond):
        return jnp.where(cond, 1.0, 0.0).astype(jnp.float32)

    units = [w * 2 + half for half in range(2) for w in range(ways)]

    def weigh(u, weights):
        total = jnp.zeros((sub, hd), jnp.float32)
        for c_m in range(group):
            block = own_ref[u * sub:(u + 1) * sub, c_m * hd:(c_m + 1) * hd]
            total = total + block.astype(jnp.float32) * weights[c_m]
        return total.astype(jnp.bfloat16)

    for load in loads[:2]:
        load.wait()
    pl.semaphore_wait(barrier, len(peers))
    for w in range(ways):
        ring(0, w, 0).start()
    for w in range(ways):
        across(0, w, 0, core).start()
    for load in loads[2:4]:
        load.wait()
    for u in units:
        for j in range(1, n_head):
            for c in range(capacity):
                weights = [
                    sum([flag((shift[k] == j) & (slot[k] == c) & (taken[k] == c_m))
                         for k in range(group)], jnp.float32(0))
                    for c_m in range(group)
                ]
                parcel[u, j - 1, c] = weigh(u, weights)
            relay(u, j).start()
    for k in range(group):
        weights = [flag((shift[k] == 0) & (taken[k] == c_m)) for c_m in range(group)]
        for u in units:
            wq[me, u * sub:(u + 1) * sub, k * hd:(k + 1) * hd] = weigh(u, weights)
    for load in loads[4:]:
        load.wait()
    accq[...] = jnp.zeros_like(accq)
    acckv[...] = jnp.zeros_like(acckv)

    def add(p, w, owner):
        xs = x_ref[:, pl.ds(pl.multiple_of(owner * rows + w * piece, 128), piece)]
        acc = (acckv, accq)[p]
        acc[...] += dot(xs, bufs[p][owner, pl.ds(w * piece, piece), :], 1, 0)

    def pass_on(p, w, s):
        ring_in(p, w, s - 1).wait_recv()

        @pl.when(s < m - 1)
        def _():
            ring(p, w, s).start()

        across(p, w, s, core).start()

    def unit_out(u):
        block = pl.ds(u * sub, sub)
        for j in range(1, n_head):
            relay(u, j).wait_recv()
        for k in range(group):
            cols = slice(k * hd, (k + 1) * hd)
            total = wq[me, block, cols].astype(jnp.float32)
            for j in range(1, n_head):
                for c in range(capacity):
                    weight = flag((shift[k] == j) & (slot[k] == c))
                    total = total + arrived[u, j - 1, c].astype(jnp.float32) * weight
            wq[me, block, cols] = total.astype(jnp.bfloat16)
        ring(1 + u % 2, u // 2, 0).start()
        across(1 + u % 2, u // 2, 0, core).start()

    for w in range(ways):
        add(0, w, me)
    for u in units[:ways]:
        unit_out(u)
    for s in range(1, lead + 1):
        for w in range(ways):
            pass_on(0, w, s)
        if s == 1:
            for u in units[ways:]:
                unit_out(u)
    for w in range(ways):
        add(1, w, me)

    def step(s, carry):
        @pl.when(s + lead < m)
        def _():
            for w in range(ways):
                pass_on(0, w, s + lead)

        for p in range(1, parts):
            for w in range(ways):
                pass_on(p, w, s)
        for w in range(ways):
            for p in range(2):
                add(p, w, index_of(pos - signs[w] * s, core))
        for w in range(ways):
            for p in range(parts):
                across(p, w, s - 1, 1 - core).wait_recv()
        for w in range(ways):
            for p in range(2):
                add(p, w, index_of(pos - signs[w] * (s - 1), 1 - core))
        return carry

    lax.fori_loop(1, m, step, 0)
    for w in range(ways):
        for p in range(parts):
            across(p, w, m - 1, 1 - core).wait_recv()
        for p in range(2):
            add(p, w, index_of(pos - signs[w] * (m - 1), 1 - core))

    scale = 1.0 / math.sqrt(hd)
    cosine, sine = cos_ref[...], sin_ref[...]

    def rotate(f):
        return f * cosine + pltpu.roll(f, hd // 2, 1) * sine

    def rotate_back(f):
        return f * cosine - pltpu.roll(f, hd // 2, 1) * sine

    docs = jnp.broadcast_to(doc_ref[...].astype(jnp.float32), (length, length))
    at_key = lax.broadcasted_iota(jnp.int32, (length, length), 1)
    at_query = lax.broadcasted_iota(jnp.int32, (length, length), 0)
    allowed = (at_key <= at_query) & (docs == docs.T)
    key = rotate(acckv[:, :hd]).astype(jnp.bfloat16)
    value = acckv[:, hd:].astype(jnp.bfloat16)
    dkey = jnp.zeros((length, hd), jnp.float32)
    dvalue = jnp.zeros((length, hd), jnp.float32)
    for k in range(group):
        cols = slice(k * hd, (k + 1) * hd)
        query = rotate(accq[:, cols]).astype(jnp.bfloat16)
        given = g_ref[:, cols]
        scores = jnp.where(allowed, dot(query, key, 1, 1) * scale, neg_large)
        weights = jnp.exp(scores - jnp.max(scores, axis=-1, keepdims=True))
        probs = weights / jnp.sum(weights, axis=-1, keepdims=True)
        probs_b = probs.astype(jnp.bfloat16)
        out_ref[:, cols] = dot(probs_b, value, 1, 0).astype(jnp.bfloat16)
        prob_grad = dot(given, value, 1, 1)
        centre = jnp.sum(probs * prob_grad, axis=-1, keepdims=True)
        dscore = (probs * (prob_grad - centre) * scale).astype(jnp.bfloat16)
        dq_ref[:, cols] = rotate_back(dot(dscore, key, 1, 0)).astype(jnp.bfloat16)
        dkey = dkey + dot(dscore, query, 0, 0)
        dvalue = dvalue + dot(probs_b, given, 0, 0)
    dkv_ref[:, :hd] = rotate_back(dkey).astype(jnp.bfloat16)
    dkv_ref[:, hd:] = dvalue.astype(jnp.bfloat16)

    chunks = n_dp // n_head

    def partial(owner):
        return (dot(dq_ref[...], wq[owner], 1, 1) + dot(dkv_ref[...], wkv[owner], 1, 1)).astype(
            jnp.bfloat16)

    def share(j, i):
        return pltpu.make_async_remote_copy(
            psend.at[j - 1, i], precv.at[j - 1, i], ps.at[j - 1, i], pr.at[j - 1, i],
            device_id=(me, (head + j) % n_head), device_id_type=MESH)

    for j in range(1, n_head):
        def send_chunk(i, carry):
            psend[j - 1, i] = partial(((head + j) % n_head) * chunks + i)
            share(j, i).start()
            return carry

        lax.fori_loop(0, chunks, send_chunk, 0)

    def own_chunk(i, carry):
        cols = pl.ds(pl.multiple_of(i * rows, 128), rows)
        grad_ref[:, cols] = partial(head * chunks + i)
        return carry

    lax.fori_loop(0, chunks, own_chunk, 0)

    def finish(i, carry):
        cols = pl.ds(pl.multiple_of(i * rows, 128), rows)
        total = grad_ref[:, cols].astype(jnp.float32)
        for j in range(1, n_head):
            share(j, i).wait_recv()
            total = total + precv[j - 1, i].astype(jnp.float32)
        grad_ref[:, cols] = total.astype(jnp.bfloat16)
        return carry

    lax.fori_loop(0, chunks, finish, 0)

    def drain(s, carry):
        for p in range(parts):
            for w in range(ways):
                @pl.when(s < m - 1)
                def _():
                    ring(p, w, s).wait_send()

                across(p, w, s, core).wait_send()
        return carry

    lax.fori_loop(0, m, drain, 0)
    for j in range(1, n_head):
        for u in units:
            relay(u, j).wait_send()

        def drain_share(i, carry):
            share(j, i).wait_send()
            return carry

        lax.fori_loop(0, chunks, drain_share, 0)


def pair_kernel(
    n_dp, group, capacity,
    src_hbm, doc_hbm, cos_hbm, sin_hbm, x_hbm, old_hbm, fresh_hbm, k_hbm, v_hbm, g_hbm,
    out_ref, grad_ref,
    src_ref, doc_ref, cos_ref, sin_ref, x_ref, own_ref, g_ref, wkv, wqa, wqb, okv, oqa, oqb, parcel, arrived_0, arrived_1, arrived_2, arrived_3, accq, acckv,
    dq_ref, dkv_ref, eq_ref, ekv_ref, psend, precv,
    in_sem, rs, rr, cs, cr, hs, hr, ys, yr, ts, tr, ds, dr, ps, pr,
):
    me, head = lax.axis_index("dp"), lax.axis_index("head")
    rows, hd = k_hbm.shape
    length = x_ref.shape[0]
    lanes, ways = 2, 2
    m = n_dp // lanes
    half = n_dp // 2
    core, chip = me % lanes, me // lanes
    side, level = chip % 2, chip // 2
    pos = (1 - side) * level + side * (m - 1 - level)
    piece = rows // ways
    kv_parts = [(0, first, piece // 2) for first in range(0, piece, piece // 2)]
    qa_parts = [(1, first, piece // 2) for first in range(0, piece, piece // 2)]
    qb_parts = [(2, first, piece // 1) for first in range(0, piece, piece // 1)]
    parts = kv_parts + qa_parts + qb_parts
    kv_range = range(len(kv_parts))
    qa_range = range(len(kv_parts), len(kv_parts) + len(qa_parts))
    qb_range = range(len(kv_parts) + len(qa_parts), len(parts))
    unit = rows // parcel.shape[0]
    lead = 3
    count = m - m // 4
    signs = (1, -1)
    arrived = (arrived_0, arrived_1, arrived_2, arrived_3)
    bufs = (wkv, wqa, wqb)
    others = (okv, oqa, oqb)
    first_heads = wqa.shape[2] // hd
    width_a = wqa.shape[2]

    def index_of(p, lane):
        p = jnp.where(p < 0, p + m, p)
        p = jnp.where(p >= m, p - m, p)
        return jnp.where(p < m // 2, 2 * p, 2 * (m - 1 - p) + 1) * lanes + lane

    right, left = index_of(pos + 1, core), index_of(pos - 1, core)
    targets = (right, left)
    partner = index_of(pos, 1 - core)
    across_y = (me, 1 - head)

    barrier = pltpu.get_barrier_semaphore()
    peers = [(right, head), (left, head), (partner, head), across_y]
    for peer in peers:
        pl.semaphore_signal(barrier, inc=1, device_id=peer, device_id_type=MESH)

    loads = [
        pltpu.make_async_copy(k_hbm, wkv.at[me, :, pl.ds(0, hd)], in_sem.at[0]),
        pltpu.make_async_copy(v_hbm, wkv.at[me, :, pl.ds(hd, hd)], in_sem.at[1]),
    ]
    loads += [
        pltpu.make_async_copy(old_hbm.at[:, pl.ds(c * hd, hd)], own_ref.at[c], in_sem.at[2 + c])
        for c in range(group - 1)
    ]
    loads += [
        pltpu.make_async_copy(fresh_hbm, own_ref.at[group - 1], in_sem.at[group + 1]),
        pltpu.make_async_copy(src_hbm, src_ref, in_sem.at[group + 7]),
        pltpu.make_async_copy(x_hbm, x_ref, in_sem.at[group + 2]),
        pltpu.make_async_copy(g_hbm, g_ref, in_sem.at[group + 3]),
        pltpu.make_async_copy(doc_hbm, doc_ref, in_sem.at[group + 4]),
        pltpu.make_async_copy(cos_hbm, cos_ref, in_sem.at[group + 5]),
        pltpu.make_async_copy(sin_hbm, sin_ref, in_sem.at[group + 6]),
    ]
    for load in loads:
        load.start()

    def remote(src, dst, send, recv, device):
        return pltpu.make_async_remote_copy(
            src, dst, send, recv, device_id=device, device_id_type=MESH)

    def part_of(p, w, owner):
        b, first, size = parts[p]
        return bufs[b].at[owner, pl.ds(w * piece + first, size)]

    def ring(p, w, s, owner):
        ref = part_of(p, w, owner)
        return remote(ref, ref, rs.at[parts[p][0]], rr.at[p, s], (targets[w], head))

    def ring_in(p, s):
        b, _, size = parts[p]
        ref = bufs[b].at[me, pl.ds(0, ways * size)]
        return remote(ref, ref, rs.at[b], rr.at[p, s], (left, head))

    def across(p, w, s, owner):
        ref = part_of(p, w, owner)
        return remote(ref, ref, cs.at[parts[p][0]], cr.at[parts[p][0], s], (partner, head))

    def across_in(b, s):
        ref = bufs[b].at[me]
        return remote(ref, ref, cs.at[b], cr.at[b, s], (partner, head))

    def forward(p, w, owner):
        b, first, size = parts[p]
        dst = others[b].at[owner - (1 - head) * half, pl.ds(w * piece + first, size)]
        return remote(part_of(p, w, owner), dst, ys.at[b], yr.at[b], across_y)

    def owner_at(w, s, lane):
        return index_of(pos - (1 - 2 * w) * s, lane)

    def share(b, w, s):
        ref = others[b].at[owner_at(w, s, core) - head * half, pl.ds(pl.multiple_of(w * piece, piece), piece)]
        return remote(ref, ref, ts.at[b], tr.at[b], (partner, head))

    def all_of(b, count, send, recv):
        ref = bufs[b].at[pl.ds(0, count), pl.ds(0, piece)]
        return remote(ref, ref, send.at[b], recv.at[b], across_y)

    def for_here(w, s):
        return (index_of(pos - signs[w] * s, 0) >= half) == (head == 1)

    def relay(u):
        return remote(parcel.at[u], arrived[u], hs.at[0], hr.at[u], across_y)

    units = [w * 2 + late for late in range(2) for w in range(ways)]

    for load in loads[:2]:
        load.wait()
    pl.semaphore_wait(barrier, len(peers))
    for p in kv_range:
        for w in range(ways):
            ring(p, w, 0, me).start()
    for p in kv_range:
        for w in range(ways):
            across(p, w, 0, me).start()
    for load in loads[2:3 + group]:
        load.wait()
    shift = [(2 - src_ref[0, k] // group) % 2 for k in range(group)]
    taken = [src_ref[0, k] % group for k in range(group)]
    slot = [
        sum([(shift[l] == 1).astype(jnp.int32) for l in range(k)], jnp.int32(0)) * shift[k]
        for k in range(group)
    ]
    picks = [
        sum([jnp.where((shift[k] == 1) & (slot[k] == c), taken[k], 0) for k in range(group)], jnp.int32(0))
        for c in range(capacity)
    ]
    for u in units:
        for c in range(capacity):
            parcel[u, c] = own_ref[picks[c], u * unit:(u + 1) * unit]
        relay(u).start()

    def by_arrival(to):
        begin = (2 * to + 3) * (m // 4)
        places = [(w, lax.rem(signs[w] * (pos - begin - i) + 3 * m, m)) for w in range(ways) for i in range(m // 2)]
        later = [
            sum([jnp.where(t > s - (v > w), 1, 0) for v, t in places], jnp.int32(0)) for w, s in places
        ]
        order = []
        for r in range(m):
            order.append((
                sum([jnp.where(late == r, w, 0) for late, (w, _) in zip(later, places)], jnp.int32(0)),
                sum([jnp.where(late == r, s, 0) for late, (_, s) in zip(later, places)], jnp.int32(0)),
            ))
        limits = [jnp.int32(-1)] * ways
        for late, (w, s) in zip(later, places):
            limits[w] = jnp.maximum(limits[w], jnp.where(late >= m // 4, s, -1))
        return order, limits

    (order_out, limit_out), (order_in, _) = by_arrival(1 - head), by_arrival(head)
    far_out, far_in, near_in = order_out[:m // 4], order_in[:m // 4], order_in[m // 4:]

    def forwarded(w, s):
        return jnp.logical_not(for_here(w, s)) & (s <= limit_out[w])

    def hand_on(some, w, owner, wanted):
        @pl.when(wanted)
        def _():
            for p in some:
                forward(p, w, owner).start()

    for w in range(ways):
        hand_on(kv_range, w, me, forwarded(w, 0))
    for load in loads[3 + group:]:
        load.wait()

    accs = (acckv, accq.at[:, pl.ds(0, width_a)], accq.at[:, pl.ds(width_a, group * hd - width_a)])

    def add_lanes(b, s, some):
        total = accs[b][...]
        for lane in some:
            for w in range(ways):
                owner = index_of(pos - signs[w] * s, lane)
                xs = x_ref[:, pl.ds(pl.multiple_of(owner * rows + w * piece, 128), piece)]
                total = total + dot(xs, bufs[b][owner, pl.ds(w * piece, piece), :], 1, 0)
        accs[b][...] = total

    def add(b, s):
        across_in(b, s).wait_recv()
        add_lanes(b, s, range(lanes))

    def begin(some, w):
        for p in some:
            ring(p, w, 0, me).start()
        for p in some:
            across(p, w, 0, me).start()
        hand_on(some, w, me, forwarded(w, 0))

    def pass_on(some, s):
        owners = [index_of(pos - signs[w] * s, core) for w in range(ways)]
        wanted = [forwarded(w, s) for w in range(ways)]
        for p in some:
            ring_in(p, s - 1).wait_recv()

            @pl.when(s < m - 1)
            def _():
                for w in range(ways):
                    ring(p, w, s, owners[w]).start()

            for w in range(ways):
                across(p, w, s, owners[w]).start()
                hand_on([p], w, owners[w], wanted[w])

    accq[...] = jnp.zeros_like(accq)
    acckv[...] = jnp.zeros_like(acckv)
    add(0, 0)

    def assemble(u):
        relay(u).wait_recv()
        block = slice(u * unit, (u + 1) * unit)
        for k in range(group):
            b, at = (1, k) if k < first_heads else (2, k - first_heads)
            bufs[b][me, block, at * hd:(at + 1) * hd] = jnp.where(
                shift[k] == 0, own_ref[taken[k], block], arrived[u][slot[k]])
        begin([qa_range[u % 2]], u // 2)

    pass_on(kv_range, 1)
    assemble(units[0])
    assemble(units[1])
    pass_on(kv_range, 2)
    assemble(units[2])
    assemble(units[3])
    for w in range(ways):
        begin(qb_range, w)
    pass_on(kv_range, 3)

    def step(s, carry):
        add(0, s)

        @pl.when(s > 0)
        def _():
            add(1, s - 1)

        @pl.when(s > 1)
        def _():
            add(2, s - 2)

        @pl.when(s + lead < m)
        def _():
            pass_on(kv_range, s + lead)

        @pl.when(s > 1)
        def _():
            pass_on(qb_range, s - 1)

        pass_on(qa_range, s)
        return carry

    lax.fori_loop(1, m, step, 0)
    add(2, m - 2)
    add_lanes(1, m - 1, [core])
    scale = 1.0 / math.sqrt(hd)
    cosine, sine = cos_ref[...], sin_ref[...]

    def rotate(f):
        return f * cosine + pltpu.roll(f, hd // 2, 1) * sine

    def rotate_back(f):
        return f * cosine - pltpu.roll(f, hd // 2, 1) * sine

    def swap_q(first, size):
        cols = pl.ds(first, size)
        return remote(dq_ref.at[:, cols], eq_ref.at[:, cols], ds.at[0], dr.at[0], across_y)

    swap_kv = remote(dkv_ref, ekv_ref, ds.at[1], dr.at[1], across_y)

    def swap_part(first):
        cols = pl.ds(first, hd)
        return remote(dkv_ref.at[:, cols], ekv_ref.at[:, cols], ds.at[1], dr.at[1], across_y)

    swap_all_q = remote(dq_ref, eq_ref, ds.at[0], dr.at[0], across_y)

    docs = jnp.broadcast_to(doc_ref[...].astype(jnp.float32), (length, length))
    at_key = lax.broadcasted_iota(jnp.int32, (length, length), 1)
    at_query = lax.broadcasted_iota(jnp.int32, (length, length), 0)
    allowed = (at_key <= at_query) & (docs == docs.T)
    key = rotate(acckv[:, :hd]).astype(jnp.bfloat16)
    value = acckv[:, hd:].astype(jnp.bfloat16)

    def prepare(heads):
        given = jnp.concatenate([g_ref[:, k * hd:(k + 1) * hd] for k in heads], axis=0)
        return given, dot(given, value, 1, 1)

    def attend(heads, given, prob_grad, before=None):
        cols = [slice(k * hd, (k + 1) * hd) for k in heads]
        block = [slice(i * length, (i + 1) * length) for i in range(len(heads))]
        query = jnp.concatenate([rotate(accq[:, c]).astype(jnp.bfloat16) for c in cols], axis=0)
        mask = jnp.concatenate([allowed] * len(heads), axis=0)
        scores = jnp.where(mask, dot(query, key, 1, 1) * scale, neg_large)
        weights = jnp.exp(scores - jnp.max(scores, axis=-1, keepdims=True))
        probs = weights / jnp.sum(weights, axis=-1, keepdims=True)
        probs_b = probs.astype(jnp.bfloat16)
        dvalue = dot(probs_b, given, 0, 0)
        if before is not None:
            dkv_ref[:, hd:] = (before + dvalue).astype(jnp.bfloat16)
            swap_part(hd).start()
        centre = jnp.sum(probs * prob_grad, axis=-1, keepdims=True)
        dscore = (probs * (prob_grad - centre) * scale).astype(jnp.bfloat16)
        dquery = dot(dscore, key, 1, 0)
        for c, r in zip(cols, block):
            dq_ref[:, c] = rotate_back(dquery[r]).astype(jnp.bfloat16)
        swap_q(heads[0] * hd, len(heads) * hd).start()
        attended = dot(probs_b, value, 1, 0).astype(jnp.bfloat16)
        for c, r in zip(cols, block):
            out_ref[:, c] = attended[r]
        return dot(dscore, query, 0, 0), dvalue

    early, late = prepare(range(first_heads)), prepare(range(first_heads, group))
    across_in(1, m - 1).wait_recv()
    add_lanes(1, m - 1, [1 - core])
    dkey, dvalue = attend(range(first_heads), *early)
    pass_on(qb_range, m - 1)
    add_lanes(2, m - 1, [core])
    across_in(2, m - 1).wait_recv()
    add_lanes(2, m - 1, [1 - core])
    late_dkey, _ = attend(range(first_heads, group), *late, before=dvalue)
    dkey = dkey + late_dkey
    dkv_ref[:, :hd] = rotate_back(dkey).astype(jnp.bfloat16)
    swap_part(0).start()

    def partial(dq, dkv, weights, place, w):
        block = pl.ds(pl.multiple_of(w * piece, piece), piece)
        wk, wa, wb = weights
        return (dot(dq[:, :width_a], wa[place, block, :], 1, 1)
                + dot(dq[:, width_a:], wb[place, block, :], 1, 1)
                + dot(dkv[...], wk[place, block, :], 1, 1)).astype(jnp.bfloat16)

    def send_share(r, lane):
        return remote(psend.at[r, lane], precv.at[r, lane], ps.at[0], pr.at[r, lane], across_y)

    for r, (w, s) in enumerate(far_out):
        for lane in range(lanes):
            psend[r, lane] = partial(dq_ref, dkv_ref, bufs, owner_at(w, s, lane), w)
            send_share(r, lane).start()

    for b in range(3):
        all_of(b, count, ys, yr).wait_recv()
    for w, s in near_in:
        for b in range(3):
            share(b, w, s).start()

    def columns(place, w):
        return pl.ds(pl.multiple_of(place * rows + w * piece, piece), piece)

    def own_part(i, carry):
        for place in (2 * i, 2 * i + 1):
            for w in range(ways):
                grad_ref[:, columns(place, w)] = partial(dq_ref, dkv_ref, bufs, head * half + place, w)
        return carry

    lax.fori_loop(0, half // 2, own_part, 0)
    swap_all_q.wait_recv()
    swap_kv.wait_recv()
    for b in range(3):
        all_of(b, count, ts, tr).wait_recv()

    def plus(place, w, value):
        cols = columns(place, w)
        grad_ref[:, cols] = (grad_ref[:, cols].astype(jnp.float32) + value.astype(jnp.float32)).astype(jnp.bfloat16)

    for w, s in near_in:
        for lane in range(lanes):
            place = owner_at(w, s, lane) - head * half
            plus(place, w, partial(eq_ref, ekv_ref, others, place, w))
    for r, (w, s) in enumerate(far_in):
        for lane in range(lanes):
            send_share(r, lane).wait_recv()
            plus(owner_at(w, s, lane) - head * half, w, precv[r, lane])

    for b in range(3):
        for number, sent in ((ways * (m - 1), rs), (ways * m, cs), (count, ys), (count, ts)):
            all_of(b, number, sent, sent).wait_send()
    remote(parcel, parcel, hs.at[0], hr.at[0], across_y).wait_send()
    swap_all_q.wait_send()
    swap_kv.wait_send()
    remote(psend, psend, ps.at[0], ps.at[0], across_y).wait_send()


def put_out(attended_ref, grad_ref, out_hbm, grad_hbm, sem):
    copies = [
        pltpu.make_async_copy(attended_ref, out_hbm, sem.at[0]),
        pltpu.make_async_copy(grad_ref, grad_hbm, sem.at[1]),
    ]
    for copy in copies:
        copy.start()
    for copy in copies:
        copy.wait()


def pair_call(n_dp, x, old, fresh, wk, wv, g, head_source, doc_ids):
    length, width = x.shape
    rows, hd = wk.shape
    group = g.shape[1] // hd
    m, half, ways, units, parts = n_dp // 2, n_dp // 2, 2, 4, 5
    late = 2 * hd
    early = group * hd - late
    capacity = (group + 1) // 2
    cosine, sine = rotary_tables(length, hd)
    bf, f32 = jnp.bfloat16, jnp.float32
    vm = pl.BlockSpec(memory_space=pltpu.VMEM)
    anyspace = pl.BlockSpec(memory_space=pl.ANY)
    dma = pltpu.SemaphoreType.DMA
    unit = rows // units
    far = (m // 4, 2)
    attended, grad = pl.pallas_call(
        functools.partial(pair_kernel, n_dp, group, capacity),
        out_shape=(
            pltpu.VMEM((length, group * hd), bf),
            pltpu.VMEM((length, width // 2), bf),
        ),
        in_specs=[anyspace] * 10,
        out_specs=(vm, vm),
        scratch_shapes=[
            pltpu.SMEM((1, head_source.shape[0]), jnp.int32),
            pltpu.VMEM((1, length), jnp.int32),
            pltpu.VMEM((length, hd), f32),
            pltpu.VMEM((length, hd), f32),
            pltpu.VMEM((length, width), bf),
            pltpu.VMEM((group, rows, hd), bf),
            pltpu.VMEM((length, group * hd), bf),
            pltpu.VMEM((n_dp, rows, 2 * hd), bf),
            pltpu.VMEM((n_dp, rows, early), bf),
            pltpu.VMEM((n_dp, rows, late), bf),
            pltpu.VMEM((half, rows, 2 * hd), bf),
            pltpu.VMEM((half, rows, early), bf),
            pltpu.VMEM((half, rows, late), bf),
            pltpu.VMEM((units, capacity, unit, hd), bf),
            pltpu.VMEM((capacity, unit, hd), bf),
            pltpu.VMEM((capacity, unit, hd), bf),
            pltpu.VMEM((capacity, unit, hd), bf),
            pltpu.VMEM((capacity, unit, hd), bf),
            pltpu.VMEM((length, group * hd), f32),
            pltpu.VMEM((length, 2 * hd), f32),
            pltpu.VMEM((length, group * hd), bf),
            pltpu.VMEM((length, 2 * hd), bf),
            pltpu.VMEM((length, group * hd), bf),
            pltpu.VMEM((length, 2 * hd), bf),
            pltpu.VMEM(far + (length, rows // ways), bf),
            pltpu.VMEM(far + (length, rows // ways), bf),
            dma((group + 8,)),
            dma((3,)),
            dma((parts, m)),
            dma((3,)),
            dma((3, m)),
            dma((1,)),
            dma((units,)),
            dma((3,)),
            dma((3,)),
            dma((3,)),
            dma((3,)),
            dma((2,)),
            dma((2,)),
            dma((1,)),
            dma(far),
        ],
        compiler_params=pltpu.CompilerParams(
            collective_id=0, has_side_effects=True, vmem_limit_bytes=48*1024*1024),
    )(*(pltpu.with_memory_space_constraint(jnp.asarray(a), pltpu.HBM) for a in (
        head_source.reshape(1, -1), doc_ids.reshape(1, -1), cosine, sine, x, old, fresh, wk, wv, g)))
    return pl.pallas_call(
        put_out,
        out_shape=(pltpu.HBM(attended.shape, bf), pltpu.HBM(grad.shape, bf)),
        in_specs=[vm, vm],
        out_specs=(anyspace, anyspace),
        scratch_shapes=[dma((2,))],
        compiler_params=pltpu.CompilerParams(vmem_limit_bytes=1024 * 1024),
    )(pltpu.with_memory_space_constraint(attended, pltpu.VMEM), pltpu.with_memory_space_constraint(grad, pltpu.VMEM))


def solution(mesh):
    n_dp, n_head = mesh.shape["dp"], mesh.shape["head"]

    def local(x, old, fresh, wk, wv, g, head_source, doc_ids):
        length, width = x.shape
        rows, hd = wk.shape
        group = g.shape[1] // hd
        ways = 2 if rows % 256 == 0 else 1
        m = n_dp // 2
        if n_head == 2 and group > 2 and rows % 512 == 0 and m % 8 == 0:
            return pair_call(n_dp, x, old, fresh, wk, wv, g, head_source, doc_ids)
        capacity = (group + n_head - 1) // n_head
        chunks = n_dp // n_head
        cosine, sine = rotary_tables(length, hd)
        bf, f32 = jnp.bfloat16, jnp.float32
        vm = pl.BlockSpec(memory_space=pltpu.VMEM)
        anyspace = pl.BlockSpec(memory_space=pl.ANY)
        dma = pltpu.SemaphoreType.DMA
        return pl.pallas_call(
            functools.partial(kernel, n_dp, n_head, group, ways),
            out_shape=(
                jax.ShapeDtypeStruct((length, group * hd), bf),
                jax.ShapeDtypeStruct((length, width // n_head), bf),
            ),
            in_specs=[pl.BlockSpec(memory_space=pltpu.SMEM)] + [anyspace] * 9,
            out_specs=(vm, vm),
            scratch_shapes=[
                pltpu.VMEM((1, length), jnp.int32),
                pltpu.VMEM((length, hd), f32),
                pltpu.VMEM((length, hd), f32),
                pltpu.VMEM((length, width), bf),
                pltpu.VMEM((rows, group * hd), bf),
                pltpu.VMEM((length, group * hd), bf),
                pltpu.VMEM((n_dp, rows, group * hd), bf),
                pltpu.VMEM((n_dp, rows, 2 * hd), bf),
                pltpu.VMEM((2 * ways, n_head - 1, capacity, rows // (2 * ways), hd), bf),
                pltpu.VMEM((2 * ways, n_head - 1, capacity, rows // (2 * ways), hd), bf),
                pltpu.VMEM((length, group * hd), f32),
                pltpu.VMEM((length, 2 * hd), f32),
                pltpu.VMEM((length, group * hd), bf),
                pltpu.VMEM((length, 2 * hd), bf),
                pltpu.VMEM((n_head - 1, chunks, length, rows), bf),
                pltpu.VMEM((n_head - 1, chunks, length, rows), bf),
                dma((9,)),
                dma((3 * ways, m)),
                dma((3 * ways, m)),
                dma((3 * ways, m)),
                dma((3 * ways, m)),
                dma((2 * ways, n_head - 1)),
                dma((2 * ways, n_head - 1)),
                dma((n_head - 1, chunks)),
                dma((n_head - 1, chunks)),
            ],
            compiler_params=pltpu.CompilerParams(
                collective_id=0, has_side_effects=True, vmem_limit_bytes=67043328),
        )(head_source, doc_ids.reshape(1, -1), cosine, sine, x, old, fresh, wk, wv, g)

    in_specs = (
        P("dp", None), P("dp", "head"), P("dp", "head"), P("dp", "head"),
        P("dp", "head"), P("dp", "head"), P(), P("dp"),
    )
    return jax.shard_map(
        local, mesh=mesh, in_specs=in_specs,
        out_specs=(P("dp", "head"), P("dp", "head")), check_vma=False)
```
